128 devices in a mesh: seq: 16 (over x_hi, y, core), chan: 8 (over z, x_lo).
Axes of the slice: x: 4 (x_hi: 2, x_lo: 2; x = x_hi * 2 + x_lo), y: 4, z: 4, core: 2. Of those that a mesh axis runs over, the one named last changes fastest.
Arguments:
- projected: bfloat16 [2048, 3, 4096], P('seq', None, 'chan'), may hold values from -6 to 6
- short_filter: float32 [3, 3, 4096], P(None, None, 'chan'), may hold values from -3 to 3
- long_filter: float32 [2048, 4096], P('seq', 'chan'), may hold values from -1.1 to 1.1
- w_out: bfloat16 [4096, 4096], P('chan', 'seq'), may hold values from -0.09375 to 0.09375
- d_out: bfloat16 [2048, 4096], P('seq', 'chan'), may hold values from -0.75 to 0.75
Outputs:
- output: bfloat16 [2048, 4096], P('seq', 'chan')
- d_projected: bfloat16 [2048, 3, 4096], P('seq', None, 'chan')
- d_wout: float32 [4096, 4096], P('chan', 'seq')
- d_filter: float32 [2048, 4096], P('seq', 'chan')
The draws below stay inside these ranges and needn't reach their ends.
All inputs are finite; a program needn't handle non-finite values.
Results may differ from the reference program's by a relative error of at most 0.0049.
Values may be sent and summed in bfloat16 or wider, within the bound.
No kernel may reach another device: no remote copies, remote signals or barrier semaphores. Data moves between devices by JAX's collectives and lax.ppermute only.
A program may use at most 64 MiB of HBM per device.

```python
import math
import jax
import jax.numpy as jnp

D = 4096
SEQUENCE_TOKENS = 2048


def draw_long_filter(key, part):
    random_sources = jax.random.split(key, 6)
    random_jitter = jnp.clip(jax.random.normal(random_sources[0], (SEQUENCE_TOKENS, D), jnp.float32), -4.0, 4.0)
    slow_share = 0.5
    coins = jax.random.uniform(random_sources[1], (D,), jnp.float32)
    slow_rate = jnp.exp(jax.random.uniform(random_sources[2], (D,), jnp.float32, math.log(0.3 / SEQUENCE_TOKENS), math.log(2.0 / SEQUENCE_TOKENS)))
    fast_rate = jnp.exp(jax.random.uniform(random_sources[3], (D,), jnp.float32, math.log(2.0 / SEQUENCE_TOKENS), math.log(1.0 / 30.0)))
    falloff_speed = jnp.where(coins < slow_share, slow_rate, fast_rate)
    delay_offsets = jnp.arange(SEQUENCE_TOKENS, dtype=jnp.float32)[:, None]
    spike_position = jax.random.randint(random_sources[4], (3,), 1, SEQUENCE_TOKENS).astype(jnp.float32)
    spike_retain = jax.random.uniform(random_sources[5], (3,), jnp.float32, 0.5, 0.8)
    spike_events = jnp.ones((SEQUENCE_TOKENS, 1), jnp.float32)
    for element_count in range(3):
        spike_events = spike_events * jnp.where(delay_offsets >= spike_position[element_count], spike_retain[element_count], 1.0)
    scale_factor = jnp.sqrt((1.0 - jnp.exp(-2.0 * falloff_speed)) / (1.0 - jnp.exp(-2.0 * falloff_speed * SEQUENCE_TOKENS)))
    return random_jitter * jnp.exp(-falloff_speed[None, :] * delay_offsets) * scale_factor[None, :] * spike_events


def spiked(drawn, own_key, source, target, blocks, factor):
    owner, partner = [(jnp.arange(drawn.shape[axis_at]) // (drawn.shape[axis_at] // blocks)).reshape([-1 if axis == axis_at else 1 for axis in range(drawn.ndim)]) for axis_at in (source, target)]
    chosen = jax.random.permutation(own_key, blocks)[partner]
    strong = (owner == chosen) | (owner == (partner + blocks // 2) % blocks)
    return jnp.where(strong, factor * drawn, drawn)


def steps_of(stream_key, extent, cuts, smallest, high):
    gain = 1.0
    for axis_at, parts in cuts:
        heights = jax.random.uniform(jax.random.fold_in(jax.random.fold_in(stream_key, 6), axis_at), (parts,), jnp.float32, smallest / len(cuts), high / len(cuts))
        gain = gain * jnp.repeat(jnp.exp(heights), extent[axis_at] // parts).reshape((-1,) + (1,) * (len(extent) - 1 - axis_at))
    return gain


def scatter_about(stream_key, shape, deviation, bound, shards=(), kind=jnp.bfloat16):
    loudness = steps_of(stream_key, shape, shards, -0.22, 0.18) if shards else 1.0
    values = jax.random.normal(stream_key, shape, jnp.float32) * deviation * loudness
    return jnp.minimum(jnp.maximum(values, -bound), bound).astype(kind)


def heavy_noise(key, shape, width, limit, cuts, heavy, kind=jnp.bfloat16):
    drawn = width * jax.random.normal(key, shape, jnp.float32)
    if cuts:
        drawn = drawn * steps_of(key, shape, cuts, -0.22, 0.18)
    return jnp.clip(spiked(drawn, jax.random.fold_in(key, 3), *heavy), -limit, limit).astype(kind)


def setup_inputs(seed: int = 0) -> dict:
    streams_of = jax.random.split(jax.random.key(seed), 6)
    return {
        "projected": scatter_about(streams_of[0], (SEQUENCE_TOKENS, 3, D), 1.0, 6.0, ((0, 16), (2, 8))),
        "short_filter": scatter_about(streams_of[1], (3, 3, D), 0.6, 3.0, ((2, 8),), jnp.float32),
        "long_filter": draw_long_filter(jax.random.fold_in(streams_of[5], 71), 0),
        "w_out": scatter_about(streams_of[3], (D, D), D ** -0.5, 0.09375, ((0, 8), (1, 16))),
        "d_out": heavy_noise(streams_of[4], (SEQUENCE_TOKENS, D), 0.125, 0.75, ((0, 16), (1, 8)), (0, 1, 16, 2.0)),
    }


def filter_apply(kernel_rows, signal_rows, flipped):
    full_len = 2 * kernel_rows.shape[0]
    kernel_spec = jnp.fft.rfft(kernel_rows, n=full_len, axis=0)
    if flipped:
        kernel_spec = jnp.conj(kernel_spec)
    signal_spec = jnp.fft.rfft(signal_rows, n=full_len, axis=0)
    return jnp.fft.irfft(kernel_spec * signal_spec, n=full_len, axis=0)[: kernel_rows.shape[0]]


def reference(projected, short_filter, long_filter, w_out, d_out):
    values = projected.astype(jnp.float32)
    length = values.shape[0]
    zeros_rim = jnp.zeros((2,) + values.shape[1:], values.dtype)
    extended = jnp.concatenate([zeros_rim, values], axis=0)
    mixed = short_filter[0] * values + short_filter[1] * extended[1:length + 1] + short_filter[2] * extended[0:length]
    queries = mixed[:, 0]
    key_rows = mixed[:, 1]
    val_rows = mixed[:, 2]
    carried = key_rows * val_rows
    conv_out = filter_apply(long_filter, carried, False)
    gated = (queries * conv_out).astype(jnp.bfloat16)
    output = jnp.dot(gated, w_out, preferred_element_type=jnp.float32).astype(jnp.bfloat16)
    d_gated = jnp.dot(d_out, w_out.T, preferred_element_type=jnp.float32)
    d_wout = jnp.dot(gated.T, d_out, preferred_element_type=jnp.float32)
    d_conv = d_gated * queries
    d_query = d_gated * conv_out
    d_carried = filter_apply(long_filter, d_conv, True)
    d_filter = filter_apply(carried, d_conv, True)
    d_mixed = jnp.stack([d_query, d_carried * val_rows, d_carried * key_rows], axis=1)
    tail_rim = jnp.zeros((2,) + d_mixed.shape[1:], d_mixed.dtype)
    padded = jnp.concatenate([d_mixed, tail_rim], axis=0)
    d_projected = (short_filter[0] * d_mixed + short_filter[1] * padded[1:length + 1] + short_filter[2] * padded[2:length + 2]).astype(jnp.bfloat16)
    return (output, d_projected, d_wout, d_filter)
```

```python
import numpy as np

import jax
import jax.numpy as jnp
from jax import lax
from jax.sharding import PartitionSpec as P

BF16 = jnp.bfloat16
F32 = jnp.float32

SEQ = 16
CHAN = 8
TOKENS = 2048
ROWS = 128
COLS = 512
LANE = 32
NEAR = 4
FAR = SEQ // NEAR
HALF = 33


def device(seq_at, chan_at):
    return seq_at * CHAN + chan_at


def swap_pairs():
    pairs = []
    for seq_at in range(SEQ):
        for chan_at in range(CHAN):
            a, i = divmod(seq_at, NEAR)
            b, p = divmod(chan_at, CHAN // FAR)
            pairs.append(
                (device(seq_at, chan_at), device(b * NEAR + i, a * (CHAN // FAR) + p))
            )
    return pairs


def swapped(array):
    return lax.ppermute(array, ("seq", "chan"), swap_pairs())


def near_pairs(step):
    return [(i, i ^ step) for i in range(SEQ)]


def exchange(array, axis):
    return lax.all_to_all(array, axis, 0, 0, tiled=True)


def tables():
    n1 = np.arange(32)
    n2 = np.arange(64)
    k1 = np.arange(HALF)
    k2 = np.arange(64)
    time = 64 * n1[None, None, :] + n2[:, None, None]
    outer = 2.0 * np.pi / 4096.0 * ((time * k1[None, :, None]) % 4096)
    inner = 2.0 * np.pi / 64.0 * ((k2[:, None] * n2[None, :]) % 64)
    weight = np.where((k1 == 0) | (k1 == 32), 1.0, 2.0)[None, :, None] / 4096.0
    return outer, inner, weight


def product(form, table, data):
    return jnp.einsum(form, table, data, precision=lax.Precision.HIGHEST)


def spectrum(signal):
    outer, inner, _ = tables()
    blocks = signal.reshape(32, 64, -1)
    mid_re = product("jkn,njl->kjl", jnp.asarray(np.cos(outer), F32), blocks)
    mid_im = product("jkn,njl->kjl", jnp.asarray(-np.sin(outer), F32), blocks)
    cos = jnp.asarray(np.cos(inner), F32)
    sin = jnp.asarray(np.sin(inner), F32)
    out_re = product("qj,kjl->kql", cos, mid_re) + product("qj,kjl->kql", sin, mid_im)
    out_im = product("qj,kjl->kql", cos, mid_im) - product("qj,kjl->kql", sin, mid_re)
    return out_re, out_im


def samples(spec_re, spec_im):
    outer, inner, weight = tables()
    cos = jnp.asarray(np.cos(inner), F32)
    sin = jnp.asarray(np.sin(inner), F32)
    mid_re = product("qj,kql->kjl", cos, spec_re) - product("qj,kql->kjl", sin, spec_im)
    mid_im = product("qj,kql->kjl", cos, spec_im) + product("qj,kql->kjl", sin, spec_re)
    back_re = product("jkn,kjl->njl", jnp.asarray(np.cos(outer) * weight, F32), mid_re)
    back_im = product("jkn,kjl->njl", jnp.asarray(np.sin(outer) * weight, F32), mid_im)
    return (back_re - back_im).reshape(TOKENS, -1)


def shifted(array, by):
    if by > 0:
        return jnp.concatenate([jnp.zeros_like(array[:by]), array[:-by]], axis=0)
    return jnp.concatenate([array[-by:], jnp.zeros_like(array[:-by])], axis=0)


def shards(projected, short_filter, long_filter, w_out, d_out):
    seq_at = lax.axis_index("seq")
    near_at = seq_at % NEAR

    moved = swapped(d_out)

    streams = jnp.concatenate([projected, long_filter.astype(BF16)[:, None, :]], axis=1)
    packed = streams.reshape(ROWS, 4, SEQ, LANE).transpose(2, 0, 1, 3).reshape(SEQ, ROWS, 4 * LANE)
    signals = exchange(packed, "seq").reshape(TOKENS, 4 * LANE).astype(F32)

    cots = exchange(jnp.broadcast_to(moved[None], (CHAN, ROWS, COLS)), "chan")
    cots = cots.reshape(FAR, 2, ROWS, COLS).transpose(0, 2, 1, 3).reshape(FAR * ROWS, 2 * COLS)

    weights = jnp.zeros((NEAR,) + w_out.shape, BF16)
    for step in range(NEAR):
        piece = w_out if step == 0 else lax.ppermute(w_out, "seq", near_pairs(step))
        weights = lax.dynamic_update_slice(weights, piece[None], (near_at ^ step, 0, 0))
    weights = weights.transpose(1, 0, 2).reshape(COLS, NEAR * w_out.shape[1])

    own = lax.dynamic_slice_in_dim(short_filter, seq_at * LANE, LANE, axis=2).reshape(3, 3 * LANE)
    plain = jnp.zeros((3, LANE), F32).at[0].set(1.0)
    taps = jnp.concatenate([own, plain], axis=1)

    mixed = taps[0] * signals + taps[1] * shifted(signals, 1) + taps[2] * shifted(signals, 2)
    queries = mixed[:, :LANE]
    key_rows = mixed[:, LANE : 2 * LANE]
    val_rows = mixed[:, 2 * LANE : 3 * LANE]
    carried = key_rows * val_rows
    both_re, both_im = spectrum(jnp.concatenate([carried, mixed[:, 3 * LANE :]], axis=1))
    carry_re, filt_re = both_re[..., :LANE], both_re[..., LANE:]
    carry_im, filt_im = both_im[..., :LANE], both_im[..., LANE:]
    conv_out = samples(
        filt_re * carry_re - filt_im * carry_im, filt_re * carry_im + filt_im * carry_re
    )
    gated = (queries * conv_out).astype(BF16)

    part = lax.dot_general(
        weights, cots, (((1,), (1,)), ((), ())), preferred_element_type=F32
    ).astype(BF16)
    gated_send = gated.T.reshape(LANE, FAR, NEAR, ROWS).transpose(2, 0, 1, 3)
    gated_send = jnp.broadcast_to(
        gated_send.reshape(1, NEAR, LANE, FAR * ROWS), (FAR, NEAR, LANE, FAR * ROWS)
    ).reshape(SEQ, LANE, FAR * ROWS)
    sent = jnp.concatenate([gated_send, part.reshape(SEQ, LANE, FAR * ROWS)], axis=1)
    got = exchange(sent, "seq")
    gated_cols = got[:, :LANE].reshape(COLS, FAR * ROWS)
    d_gated = jnp.sum(
        got[:, LANE:].astype(F32).reshape(FAR, NEAR, LANE, FAR, ROWS), axis=0
    )
    d_gated = d_gated.transpose(2, 0, 3, 1).reshape(TOKENS, LANE)

    partial_out = lax.dot_general(
        gated_cols, weights, (((0,), (0,)), ((), ())), preferred_element_type=F32
    ).astype(BF16)
    partial_out = partial_out.reshape(FAR, ROWS, 2, COLS).transpose(0, 2, 1, 3)
    shares = exchange(partial_out.reshape(CHAN, ROWS, COLS), "chan")
    output = swapped(jnp.sum(shares.astype(F32), axis=0).astype(BF16))

    grad = jnp.dot(gated_cols, cots, preferred_element_type=F32)
    grad = grad.reshape(COLS, NEAR, -1).transpose(1, 0, 2)
    d_wout = lax.dynamic_index_in_dim(grad, near_at, 0, keepdims=False)
    for step in range(1, NEAR):
        piece = lax.dynamic_index_in_dim(grad, near_at ^ step, 0, keepdims=False).astype(BF16)
        d_wout = d_wout + lax.ppermute(piece, "seq", near_pairs(step)).astype(F32)

    d_conv = d_gated * queries
    d_query = d_gated * conv_out
    grad_re, grad_im = spectrum(d_conv)
    back = samples(
        jnp.concatenate(
            [filt_re * grad_re + filt_im * grad_im, carry_re * grad_re + carry_im * grad_im], axis=2
        ),
        jnp.concatenate(
            [filt_re * grad_im - filt_im * grad_re, carry_re * grad_im - carry_im * grad_re], axis=2
        ),
    )
    d_carried = back[:, :LANE]
    d_mixed = jnp.concatenate(
        [d_query, d_carried * val_rows, d_carried * key_rows, back[:, LANE:]], axis=1
    )
    d_signals = taps[0] * d_mixed + taps[1] * shifted(d_mixed, -1) + taps[2] * shifted(d_mixed, -2)
    returned = exchange(d_signals.astype(BF16).reshape(SEQ, ROWS, 4 * LANE), "seq")
    returned = returned.reshape(SEQ, ROWS, 4, LANE).transpose(1, 2, 0, 3).reshape(ROWS, 4, COLS)
    return (output, returned[:, :3], d_wout, returned[:, 3].astype(F32))


def solution(mesh):
    in_specs = (
        P("seq", None, "chan"),
        P(None, None, "chan"),
        P("seq", "chan"),
        P("chan", "seq"),
        P("seq", "chan"),
    )
    out_specs = (P("seq", "chan"), P("seq", None, "chan"), P("chan", "seq"), P("seq", "chan"))
    return jax.shard_map(shards, mesh=mesh, in_specs=in_specs, out_specs=out_specs, check_vma=False)
```

```python
import numpy as np
import ml_dtypes

import jax
import jax.numpy as jnp
from jax import lax
from jax.experimental import pallas as pl
from jax.experimental.pallas import tpu as pltpu
from jax.sharding import PartitionSpec as P

BF16 = jnp.bfloat16
F32 = jnp.float32

SEQ = 16
CHAN = 8
TOKENS = 2048
ROWS = 128
COLS = 512
LANE = 32
NEAR = 4
FAR = SEQ // NEAR
HALF = 33
MID = 72
BACK = 80
VMEM_LIMIT = 48 * 1024 * 1024


def device(seq_at, chan_at):
    return seq_at * CHAN + chan_at


def swap_pairs():
    pairs = []
    for seq_at in range(SEQ):
        for chan_at in range(CHAN):
            a, i = divmod(seq_at, NEAR)
            b, p = divmod(chan_at, CHAN // FAR)
            pairs.append(
                (device(seq_at, chan_at), device(b * NEAR + i, a * (CHAN // FAR) + p))
            )
    return pairs


def swapped(array):
    return lax.ppermute(array, ("seq", "chan"), swap_pairs())


def near_pairs(step):
    return [(i, i ^ step) for i in range(SEQ)]


def exchange(array, axis):
    return lax.all_to_all(array, axis, 0, 0, tiled=True)


def thrice(table):
    high = table.astype(ml_dtypes.bfloat16)
    low = (table - high.astype(np.float64)).astype(ml_dtypes.bfloat16)
    return np.concatenate([high, high, low], axis=-1)


def tables():
    n1 = np.arange(32)
    n2 = np.arange(64)
    k1 = np.arange(HALF)
    k2 = np.arange(64)
    time = 64 * n1[None, None, :] + n2[:, None, None]
    outer = 2.0 * np.pi / 4096.0 * ((time * k1[None, :, None]) % 4096)
    inner = 2.0 * np.pi / 64.0 * ((k2[:, None] * n2[None, :]) % 64)
    weight = np.where((k1 == 0) | (k1 == 32), 1.0, 2.0)[None, :, None] / 4096.0
    first = np.zeros((64, MID, 32))
    first[:, :HALF] = np.cos(outer)
    first[:, HALF : 2 * HALF] = -np.sin(outer)
    last = np.zeros((64, 32, BACK))
    last[:, :, 0 : 2 * HALF : 2] = (np.cos(outer) * weight).transpose(0, 2, 1)
    last[:, :, 1 : 2 * HALF : 2] = (-np.sin(outer) * weight).transpose(0, 2, 1)
    cos, sin = np.cos(inner), np.sin(inner)
    ahead = np.block([[cos, sin], [-sin, cos]])
    return thrice(first), thrice(ahead), thrice(ahead.T), thrice(last)


def pieces(array):
    high = array.astype(BF16)
    low = (array - high.astype(F32)).astype(BF16)
    return jnp.concatenate([high, low, high], axis=0)


def matmul(left, right):
    return jnp.dot(left, right, preferred_element_type=F32)


def every(count, width, step):
    def body(block, carry):
        for at in range(width):
            step(block * width + at)
        return carry

    lax.fori_loop(0, count // width, body, 0)


def lanes_of(rows):
    return lax.broadcasted_iota(jnp.int32, (rows, 4 * LANE), 1)


def ahead_rows(mid_ref, k1):
    return jnp.concatenate(
        [mid_ref[pl.ds(k1, 64, stride=MID), :], mid_ref[pl.ds(HALF + k1, 64, stride=MID), :]],
        axis=0,
    )


def forward_kernel(
    signal_ref, taps_ref, first_ref, ahead_ref, behind_ref, last_ref,
    gated_ref, kept_ref, spec_ref,
    wide_ref, mid_ref, back_ref, column_ref,
):
    wide_ref[0:8, :] = jnp.zeros((8, 4 * LANE), F32)
    wide_ref[8:, :] = signal_ref[...].astype(F32)
    back_ref[2 * HALF * 64 :, :] = jnp.zeros(((BACK - 2 * HALF) * 64, 4 * LANE), F32)
    lane = lanes_of(32)
    tap0, tap1, tap2 = (jnp.broadcast_to(taps_ref[j : j + 1, :], (32, 4 * LANE)) for j in range(3))

    def outer(n2):
        now = wide_ref[pl.ds(n2 + 8, 32, stride=64), :]
        before = wide_ref[pl.ds(n2 + 7, 32, stride=64), :]
        earlier = wide_ref[pl.ds(n2 + 6, 32, stride=64), :]
        mixed = tap0 * now + tap1 * before + tap2 * earlier
        kept_ref[pl.ds(n2, 32, stride=64), :] = mixed
        carried = mixed * pltpu.roll(mixed, LANE, 1)
        data = jnp.where((lane >= 2 * LANE) & (lane < 3 * LANE), carried, mixed)
        mid_ref[pl.ds(pl.multiple_of(n2 * MID, 8), MID), :] = matmul(first_ref[n2], pieces(data))

    every(64, 4, outer)

    def inner(k1):
        spec = matmul(ahead_ref[...], pieces(ahead_rows(mid_ref, k1)))
        spec_ref[k1] = spec
        other = pltpu.roll(spec, 3 * LANE, 1)
        re, im, other_re, other_im = spec[:64], spec[64:], other[:64], other[64:]
        both = jnp.concatenate(
            [re * other_re - im * other_im, re * other_im + im * other_re], axis=0
        )
        back_ref[pl.ds(pl.multiple_of(k1 * 128, 128), 128), :] = matmul(
            behind_ref[...], pieces(both)
        )

    every(HALF, 3, inner)

    def final(n2):
        conv = matmul(last_ref[n2], pieces(back_ref[pl.ds(n2, BACK, stride=64), :]))
        mixed = kept_ref[pl.ds(n2, 32, stride=64), :]
        column_ref[pl.ds(n2, 32, stride=64), :] = mixed * pltpu.roll(conv, 2 * LANE, 1)
        kept_ref[pl.ds(n2, 32, stride=64), :] = jnp.where(
            lane < 3 * LANE, mixed, pltpu.roll(conv, LANE, 1)
        )

    every(64, 4, final)

    for block in range(SEQ):
        a, i = divmod(block, NEAR)
        turned = column_ref[block * ROWS : (block + 1) * ROWS, :].T
        gated_ref[i, :, a * ROWS : (a + 1) * ROWS] = turned[:LANE].astype(BF16)


def backward_kernel(
    share_ref, kept_ref, spec_ref, taps_ref, first_ref, ahead_ref, behind_ref, last_ref,
    out_ref,
    grad_ref, mid_ref, back_ref, column_ref,
):
    back_ref[2 * HALF * 64 :, :] = jnp.zeros(((BACK - 2 * HALF) * 64, 4 * LANE), F32)
    column_ref[TOKENS:, :] = jnp.zeros((8, 4 * LANE), F32)
    for i in range(NEAR):
        total = share_ref[i].astype(F32)
        for far in range(1, FAR):
            total = total + share_ref[far * NEAR + i].astype(F32)
        for a in range(FAR):
            block = a * NEAR + i
            part = total[:, a * ROWS : (a + 1) * ROWS]
            grad_ref[block * ROWS : (block + 1) * ROWS, :] = jnp.concatenate([part] * 4, axis=0).T
    lane = lanes_of(32)

    def outer(n2):
        kept = kept_ref[pl.ds(n2, 32, stride=64), :]
        query = jnp.where(lane < 3 * LANE, pltpu.roll(kept, 2 * LANE, 1), pltpu.roll(kept, 3 * LANE, 1))
        data = grad_ref[pl.ds(n2, 32, stride=64), :] * query
        mid_ref[pl.ds(pl.multiple_of(n2 * MID, 8), MID), :] = matmul(first_ref[n2], pieces(data))

    every(64, 4, outer)

    wide = lanes_of(128)

    def inner(k1):
        grad = matmul(ahead_ref[...], pieces(ahead_rows(mid_ref, k1)))
        spec = spec_ref[k1]
        other = jnp.where(wide < 3 * LANE, pltpu.roll(spec, 3 * LANE, 1), pltpu.roll(spec, LANE, 1))
        re, im, other_re, other_im = grad[:64], grad[64:], other[:64], other[64:]
        both = jnp.concatenate(
            [other_re * re + other_im * im, other_re * im - other_im * re], axis=0
        )
        back_ref[pl.ds(pl.multiple_of(k1 * 128, 128), 128), :] = matmul(
            behind_ref[...], pieces(both)
        )

    every(HALF, 3, inner)

    def final(n2):
        found = matmul(last_ref[n2], pieces(back_ref[pl.ds(n2, BACK, stride=64), :]))
        kept = kept_ref[pl.ds(n2, 32, stride=64), :]
        grad = grad_ref[pl.ds(n2, 32, stride=64), :]
        up, down = pltpu.roll(kept, LANE, 1), pltpu.roll(kept, 3 * LANE, 1)
        mixed = jnp.where(
            lane < LANE,
            grad * up,
            jnp.where(
                lane < 2 * LANE,
                pltpu.roll(found, 3 * LANE, 1) * down,
                jnp.where(lane < 3 * LANE, found * up, found),
            ),
        )
        column_ref[pl.ds(n2, 32, stride=64), :] = mixed

    every(64, 4, final)

    tap0, tap1, tap2 = (
        jnp.broadcast_to(taps_ref[j : j + 1, :], (ROWS, 4 * LANE)) for j in range(3)
    )
    for block in range(SEQ):
        low = block * ROWS
        out_ref[block] = (
            tap0 * column_ref[low : low + ROWS, :]
            + tap1 * column_ref[low + 1 : low + 1 + ROWS, :]
            + tap2 * column_ref[low + 2 : low + 2 + ROWS, :]
        ).astype(BF16)


def whole(shape):
    return pl.BlockSpec(shape, lambda _: (0,) * len(shape))


def convolve(signals, taps, consts, interpret=False):
    shapes = (
        jax.ShapeDtypeStruct((NEAR, LANE, FAR * ROWS), BF16),
        jax.ShapeDtypeStruct((TOKENS, 4 * LANE), F32),
        jax.ShapeDtypeStruct((HALF, 128, 4 * LANE), F32),
    )
    return pl.pallas_call(
        forward_kernel,
        out_shape=shapes,
        scratch_shapes=[
            pltpu.VMEM((TOKENS + 8, 4 * LANE), F32),
            pltpu.VMEM((64 * MID, 4 * LANE), F32),
            pltpu.VMEM((64 * BACK, 4 * LANE), F32),
            pltpu.VMEM((TOKENS, 4 * LANE), F32),
        ],
        compiler_params=pltpu.CompilerParams(vmem_limit_bytes=VMEM_LIMIT),
        interpret=interpret,
        name="convolve",
    )(signals, taps, *consts)


def correlate(shares, kept, spec, taps, consts, interpret=False):
    inputs = (shares, kept, spec, taps) + tuple(consts)
    specs = [whole(x.shape) for x in inputs]
    specs[0] = pl.BlockSpec((SEQ, LANE, FAR * ROWS), lambda _: (0, 1, 0))
    return pl.pallas_call(
        backward_kernel,
        out_shape=jax.ShapeDtypeStruct((SEQ, ROWS, 4 * LANE), BF16),
        grid=(1,),
        in_specs=specs,
        out_specs=whole((SEQ, ROWS, 4 * LANE)),
        scratch_shapes=[
            pltpu.VMEM((TOKENS, 4 * LANE), F32),
            pltpu.VMEM((64 * MID, 4 * LANE), F32),
            pltpu.VMEM((64 * BACK, 4 * LANE), F32),
            pltpu.VMEM((TOKENS + 8, 4 * LANE), F32),
        ],
        compiler_params=pltpu.CompilerParams(vmem_limit_bytes=VMEM_LIMIT),
        interpret=interpret,
        name="correlate",
    )(*inputs)


def shards(projected, short_filter, long_filter, w_out, d_out):
    seq_at = lax.axis_index("seq")
    near_at = seq_at % NEAR
    consts = [jnp.asarray(table) for table in tables()]

    moved = swapped(d_out)

    streams = jnp.concatenate([projected, long_filter.astype(BF16)[:, None, :]], axis=1)
    packed = streams.reshape(ROWS, 4, SEQ, LANE).transpose(2, 0, 1, 3).reshape(SEQ, ROWS, 4 * LANE)
    signals = exchange(packed, "seq").reshape(TOKENS, 4 * LANE)

    cots = exchange(jnp.broadcast_to(moved[None], (CHAN, ROWS, COLS)), "chan")
    cots = cots.reshape(FAR, 2, ROWS, COLS).transpose(0, 2, 1, 3).reshape(FAR * ROWS, 2 * COLS)

    weights = jnp.zeros((NEAR,) + w_out.shape, BF16)
    for step in range(NEAR):
        piece = w_out if step == 0 else lax.ppermute(w_out, "seq", near_pairs(step))
        weights = lax.dynamic_update_slice(weights, piece[None], (near_at ^ step, 0, 0))
    weights = weights.transpose(1, 0, 2).reshape(COLS, NEAR * w_out.shape[1])

    own = lax.dynamic_slice_in_dim(short_filter, seq_at * LANE, LANE, axis=2).reshape(3, 3 * LANE)
    plain = jnp.zeros((3, LANE), F32).at[0].set(1.0)
    taps = jnp.concatenate([own, plain], axis=1)

    gated_send, kept, spec = convolve(signals, taps, consts)

    part = lax.dot_general(
        weights, cots, (((1,), (1,)), ((), ())), preferred_element_type=F32
    ).astype(BF16)
    gated_send = jnp.broadcast_to(
        gated_send[None], (FAR, NEAR, LANE, FAR * ROWS)
    ).reshape(SEQ, LANE, FAR * ROWS)
    sent = jnp.concatenate([gated_send, part.reshape(SEQ, LANE, FAR * ROWS)], axis=1)
    got = exchange(sent, "seq")
    gated_cols = got[:, :LANE].reshape(COLS, FAR * ROWS)

    partial_out = lax.dot_general(
        gated_cols, weights, (((0,), (0,)), ((), ())), preferred_element_type=F32
    ).astype(BF16)
    partial_out = partial_out.reshape(FAR, ROWS, 2, COLS).transpose(0, 2, 1, 3)
    shares = exchange(partial_out.reshape(CHAN, ROWS, COLS), "chan")
    output = swapped(jnp.sum(shares.astype(F32), axis=0).astype(BF16))

    grad = jnp.dot(gated_cols, cots, preferred_element_type=F32)
    grad = grad.reshape(COLS, NEAR, -1).transpose(1, 0, 2)
    d_wout = lax.dynamic_index_in_dim(grad, near_at, 0, keepdims=False)
    for step in range(1, NEAR):
        piece = lax.dynamic_index_in_dim(grad, near_at ^ step, 0, keepdims=False).astype(BF16)
        d_wout = d_wout + lax.ppermute(piece, "seq", near_pairs(step)).astype(F32)

    d_signals = correlate(got, kept, spec, taps, consts)
    returned = exchange(d_signals, "seq")
    returned = returned.reshape(SEQ, ROWS, 4, LANE).transpose(1, 2, 0, 3).reshape(ROWS, 4, COLS)
    return (output, returned[:, :3], d_wout, returned[:, 3].astype(F32))


def solution(mesh):
    in_specs = (
        P("seq", None, "chan"),
        P(None, None, "chan"),
        P("seq", "chan"),
        P("chan", "seq"),
        P("seq", "chan"),
    )
    out_specs = (P("seq", "chan"), P("seq", None, "chan"), P("chan", "seq"), P("seq", "chan"))
    return jax.shard_map(shards, mesh=mesh, in_specs=in_specs, out_specs=out_specs, check_vma=False)
```

```python
import numpy as np
import ml_dtypes

import jax
import jax.numpy as jnp
from jax import lax
from jax.experimental import pallas as pl
from jax.experimental.pallas import tpu as pltpu
from jax.sharding import PartitionSpec as P

BF16 = jnp.bfloat16
F32 = jnp.float32

SEQ = 16
CHAN = 8
TOKENS = 2048
ROWS = 128
COLS = 512
LANE = 32
NEAR = 4
FAR = SEQ // NEAR
HALF = 33
MID = 72
BACK = 80
VMEM_LIMIT = 48 * 1024 * 1024
WIDE = 16
GROUP = 11


def device(seq_at, chan_at):
    return seq_at * CHAN + chan_at


def swap_pairs():
    pairs = []
    for seq_at in range(SEQ):
        for chan_at in range(CHAN):
            a, i = divmod(seq_at, NEAR)
            b, p = divmod(chan_at, CHAN // FAR)
            pairs.append(
                (device(seq_at, chan_at), device(b * NEAR + i, a * (CHAN // FAR) + p))
            )
    return pairs


def swapped(array):
    return lax.ppermute(array, ("seq", "chan"), swap_pairs())


def near_pairs(step):
    return [(i, i ^ step) for i in range(SEQ)]


def exchange(array, axis):
    return lax.all_to_all(array, axis, 0, 0, tiled=True)


def thrice(table):
    high = table.astype(ml_dtypes.bfloat16)
    low = (table - high.astype(np.float64)).astype(ml_dtypes.bfloat16)
    return np.concatenate([high, high, low], axis=-1)


def tables():
    n1 = np.arange(32)
    n2 = np.arange(64)
    k1 = np.arange(HALF)
    k2 = np.arange(64)
    time = 64 * n1[None, None, :] + n2[:, None, None]
    outer = 2.0 * np.pi / 4096.0 * ((time * k1[None, :, None]) % 4096)
    inner = 2.0 * np.pi / 64.0 * ((k2[:, None] * n2[None, :]) % 64)
    weight = np.where((k1 == 0) | (k1 == 32), 1.0, 2.0)[None, :, None] / 4096.0
    first = np.zeros((64, MID, 32))
    first[:, :HALF] = np.cos(outer)
    first[:, HALF : 2 * HALF] = -np.sin(outer)
    last = np.zeros((64, 32, BACK))
    last[:, :, 0 : 2 * HALF : 2] = (np.cos(outer) * weight).transpose(0, 2, 1)
    last[:, :, 1 : 2 * HALF : 2] = (-np.sin(outer) * weight).transpose(0, 2, 1)
    cos, sin = np.cos(inner), np.sin(inner)
    ahead = np.block([[cos, sin], [-sin, cos]])
    return thrice(first), thrice(ahead), thrice(ahead.T), thrice(last)


def pieces(array):
    high = array.astype(BF16)
    low = (array - high.astype(F32)).astype(BF16)
    return jnp.concatenate([high, low, high], axis=0)


def matmul(left, right):
    return jnp.dot(left, right, preferred_element_type=F32)


def every(count, width, step):
    def body(block, carry):
        for at in range(width):
            step(block * width + at)
        return carry

    lax.fori_loop(0, count // width, body, 0)


def lanes_of(rows):
    return lax.broadcasted_iota(jnp.int32, (rows, 4 * LANE), 1)


def ahead_rows(mid_ref, first):
    return jnp.concatenate(
        [
            jnp.concatenate(
                [
                    mid_ref[pl.ds(first + at, 64, stride=MID), :],
                    mid_ref[pl.ds(HALF + first + at, 64, stride=MID), :],
                ],
                axis=0,
            )
            for at in range(GROUP)
        ],
        axis=1,
    )


def behind_rows(back_ref, first, behind_ref, products):
    found = matmul(behind_ref[...], pieces(jnp.concatenate(products, axis=1)))
    for at in range(GROUP):
        back_ref[pl.ds(pl.multiple_of((first + at) * 128, 128), 128), :] = found[
            :, at * 128 : (at + 1) * 128
        ]


def forward_kernel(
    signal_ref, taps_ref, first_ref, ahead_ref, behind_ref, last_ref,
    gated_ref, kept_ref, spec_ref,
    wide_ref, mid_ref, back_ref, column_ref,
):
    wide_ref[0:8, :] = jnp.zeros((8, 4 * LANE), F32)
    wide_ref[8:, :] = signal_ref[...].astype(F32)
    back_ref[2 * HALF * 64 :, :] = jnp.zeros(((BACK - 2 * HALF) * 64, 4 * LANE), F32)
    lane = lanes_of(32)
    tap0, tap1, tap2 = (jnp.broadcast_to(taps_ref[j : j + 1, :], (32, 4 * LANE)) for j in range(3))

    def outer(n2):
        now = wide_ref[pl.ds(n2 + 8, 32, stride=64), :]
        before = wide_ref[pl.ds(n2 + 7, 32, stride=64), :]
        earlier = wide_ref[pl.ds(n2 + 6, 32, stride=64), :]
        mixed = tap0 * now + tap1 * before + tap2 * earlier
        kept_ref[pl.ds(n2, 32, stride=64), :] = mixed
        carried = mixed * pltpu.roll(mixed, LANE, 1)
        data = jnp.where((lane >= 2 * LANE) & (lane < 3 * LANE), carried, mixed)
        mid_ref[pl.ds(pl.multiple_of(n2 * MID, 8), MID), :] = matmul(first_ref[n2], pieces(data))

    every(64, WIDE, outer)

    def inner(group):
        spec = matmul(ahead_ref[...], pieces(ahead_rows(mid_ref, group * GROUP)))
        products = []
        for at in range(GROUP):
            one = spec[:, at * 128 : (at + 1) * 128]
            spec_ref[group * GROUP + at] = one
            other = pltpu.roll(one, 3 * LANE, 1)
            re, im, other_re, other_im = one[:64], one[64:], other[:64], other[64:]
            products.append(
                jnp.concatenate(
                    [re * other_re - im * other_im, re * other_im + im * other_re], axis=0
                )
            )
        behind_rows(back_ref, group * GROUP, behind_ref, products)

    every(HALF // GROUP, 1, inner)

    def final(n2):
        conv = matmul(last_ref[n2], pieces(back_ref[pl.ds(n2, BACK, stride=64), :]))
        mixed = kept_ref[pl.ds(n2, 32, stride=64), :]
        column_ref[pl.ds(n2, 32, stride=64), :] = mixed * pltpu.roll(conv, 2 * LANE, 1)
        kept_ref[pl.ds(n2, 32, stride=64), :] = jnp.where(
            lane < 3 * LANE, mixed, pltpu.roll(conv, LANE, 1)
        )

    every(64, WIDE, final)

    for block in range(SEQ):
        a, i = divmod(block, NEAR)
        turned = column_ref[block * ROWS : (block + 1) * ROWS, :].T
        gated_ref[i, :, a * ROWS : (a + 1) * ROWS] = turned[:LANE].astype(BF16)


def backward_kernel(
    share_ref, kept_ref, spec_ref, taps_ref, first_ref, ahead_ref, behind_ref, last_ref,
    out_ref,
    grad_ref, mid_ref, back_ref, column_ref,
):
    back_ref[2 * HALF * 64 :, :] = jnp.zeros(((BACK - 2 * HALF) * 64, 4 * LANE), F32)
    column_ref[TOKENS:, :] = jnp.zeros((8, 4 * LANE), F32)
    for i in range(NEAR):
        total = share_ref[i].astype(F32)
        for far in range(1, FAR):
            total = total + share_ref[far * NEAR + i].astype(F32)
        for a in range(FAR):
            block = a * NEAR + i
            part = total[:, a * ROWS : (a + 1) * ROWS]
            grad_ref[block * ROWS : (block + 1) * ROWS, :] = jnp.concatenate([part] * 4, axis=0).T
    lane = lanes_of(32)

    def outer(n2):
        kept = kept_ref[pl.ds(n2, 32, stride=64), :]
        query = jnp.where(lane < 3 * LANE, pltpu.roll(kept, 2 * LANE, 1), pltpu.roll(kept, 3 * LANE, 1))
        data = grad_ref[pl.ds(n2, 32, stride=64), :] * query
        mid_ref[pl.ds(pl.multiple_of(n2 * MID, 8), MID), :] = matmul(first_ref[n2], pieces(data))

    every(64, WIDE, outer)

    wide = lanes_of(128)

    def inner(group):
        grad = matmul(ahead_ref[...], pieces(ahead_rows(mid_ref, group * GROUP)))
        products = []
        for at in range(GROUP):
            one = grad[:, at * 128 : (at + 1) * 128]
            spec = spec_ref[group * GROUP + at]
            other = jnp.where(
                wide < 3 * LANE, pltpu.roll(spec, 3 * LANE, 1), pltpu.roll(spec, LANE, 1)
            )
            re, im, other_re, other_im = one[:64], one[64:], other[:64], other[64:]
            products.append(
                jnp.concatenate(
                    [other_re * re + other_im * im, other_re * im - other_im * re], axis=0
                )
            )
        behind_rows(back_ref, group * GROUP, behind_ref, products)

    every(HALF // GROUP, 1, inner)

    def final(n2):
        found = matmul(last_ref[n2], pieces(back_ref[pl.ds(n2, BACK, stride=64), :]))
        kept = kept_ref[pl.ds(n2, 32, stride=64), :]
        grad = grad_ref[pl.ds(n2, 32, stride=64), :]
        up, down = pltpu.roll(kept, LANE, 1), pltpu.roll(kept, 3 * LANE, 1)
        mixed = jnp.where(
            lane < LANE,
            grad * up,
            jnp.where(
                lane < 2 * LANE,
                pltpu.roll(found, 3 * LANE, 1) * down,
                jnp.where(lane < 3 * LANE, found * up, found),
            ),
        )
        column_ref[pl.ds(n2, 32, stride=64), :] = mixed

    every(64, WIDE, final)

    tap0, tap1, tap2 = (
        jnp.broadcast_to(taps_ref[j : j + 1, :], (ROWS, 4 * LANE)) for j in range(3)
    )
    for block in range(SEQ):
        low = block * ROWS
        out_ref[block] = (
            tap0 * column_ref[low : low + ROWS, :]
            + tap1 * column_ref[low + 1 : low + 1 + ROWS, :]
            + tap2 * column_ref[low + 2 : low + 2 + ROWS, :]
        ).astype(BF16)


LONG = pl.CostEstimate(flops=8_000_000_000, transcendentals=0, bytes_accessed=6_000_000)


def whole(shape):
    return pl.BlockSpec(shape, lambda _: (0,) * len(shape))


def convolve(signals, taps, consts, interpret=False):
    shapes = (
        jax.ShapeDtypeStruct((NEAR, LANE, FAR * ROWS), BF16),
        jax.ShapeDtypeStruct((TOKENS, 4 * LANE), F32),
        jax.ShapeDtypeStruct((HALF, 128, 4 * LANE), F32),
    )
    return pl.pallas_call(
        forward_kernel,
        out_shape=shapes,
        scratch_shapes=[
            pltpu.VMEM((TOKENS + 8, 4 * LANE), F32),
            pltpu.VMEM((64 * MID, 4 * LANE), F32),
            pltpu.VMEM((64 * BACK, 4 * LANE), F32),
            pltpu.VMEM((TOKENS, 4 * LANE), F32),
        ],
        compiler_params=pltpu.CompilerParams(vmem_limit_bytes=VMEM_LIMIT),
        cost_estimate=LONG,
        interpret=interpret,
        name="convolve",
    )(signals, taps, *consts)


def correlate(shares, kept, spec, taps, consts, interpret=False):
    inputs = (shares, kept, spec, taps) + tuple(consts)
    specs = [whole(x.shape) for x in inputs]
    specs[0] = pl.BlockSpec((SEQ, LANE, FAR * ROWS), lambda _: (0, 1, 0))
    return pl.pallas_call(
        backward_kernel,
        out_shape=jax.ShapeDtypeStruct((SEQ, ROWS, 4 * LANE), BF16),
        grid=(1,),
        in_specs=specs,
        out_specs=whole((SEQ, ROWS, 4 * LANE)),
        scratch_shapes=[
            pltpu.VMEM((TOKENS, 4 * LANE), F32),
            pltpu.VMEM((64 * MID, 4 * LANE), F32),
            pltpu.VMEM((64 * BACK, 4 * LANE), F32),
            pltpu.VMEM((TOKENS + 8, 4 * LANE), F32),
        ],
        compiler_params=pltpu.CompilerParams(vmem_limit_bytes=VMEM_LIMIT),
        cost_estimate=LONG,
        interpret=interpret,
        name="correlate",
    )(*inputs)


def pack_kernel(streams_ref, filter_ref, out_ref):
    lane = lanes_of(ROWS)
    for column in range(COLS // 128):
        at = slice(column * 128, (column + 1) * 128)
        blocks = [streams_ref[j, :, at].astype(F32) for j in range(3)] + [filter_ref[:, at]]
        for part in range(4):
            placed = [pltpu.roll(b, ((j - part) % 4) * LANE, 1) if j != part else b
                      for j, b in enumerate(blocks)]
            joined = placed[3]
            for j in range(2, -1, -1):
                joined = jnp.where(lane < (j + 1) * LANE, placed[j], joined)
            out_ref[column * 4 + part] = joined.astype(BF16)


def unpack_kernel(got_ref, streams_ref, filter_ref):
    lane = lanes_of(ROWS)
    for column in range(COLS // 128):
        at = slice(column * 128, (column + 1) * 128)
        blocks = [got_ref[column * 4 + part].astype(F32) for part in range(4)]
        for j in range(4):
            placed = [pltpu.roll(b, ((part - j) % 4) * LANE, 1) if j != part else b
                      for part, b in enumerate(blocks)]
            joined = placed[3]
            for part in range(2, -1, -1):
                joined = jnp.where(lane < (part + 1) * LANE, placed[part], joined)
            if j < 3:
                streams_ref[j, :, at] = joined.astype(BF16)
            else:
                filter_ref[:, at] = joined


def cot_columns(cots_ref, block):
    low = pl.multiple_of((block % 2) * 256, 256)
    return jnp.concatenate(
        [cots_ref[2 * a + block // 2, :, pl.ds(low, 256)] for a in range(FAR)], axis=0
    )


def contract(left, right, left_dim, right_dim):
    return lax.dot_general(
        left, right, (((left_dim,), (right_dim,)), ((), ())), preferred_element_type=F32
    )


def send_kernel(near_ref, gated_ref, cots_ref, *refs):
    weight_refs, sent_ref = refs[:NEAR], refs[NEAR]
    total = None
    for step in range(NEAR):
        term = contract(weight_refs[step][...], cot_columns(cots_ref, near_ref[0] ^ step), 1, 1)
        total = term if total is None else total + term
    total = total.astype(BF16)
    for s in range(SEQ):
        sent_ref[s, :LANE, :] = gated_ref[s % NEAR]
        sent_ref[s, LANE:, :] = total[s * LANE : (s + 1) * LANE]


def product_kernel(near_ref, got_ref, cots_ref, *refs):
    weight_refs, out_ref, grad_refs = refs[:NEAR], refs[NEAR], refs[NEAR + 1 :]
    gated = got_ref[...].reshape(COLS, FAR * ROWS)
    for step in range(NEAR):
        block = near_ref[0] ^ step
        low = pl.multiple_of((block % 2) * 256, 256)
        part = contract(gated, weight_refs[step][...], 0, 0).astype(BF16)
        for a in range(FAR):
            out_ref[2 * a + block // 2, :, pl.ds(low, 256)] = part[a * ROWS : (a + 1) * ROWS]
        grad = contract(gated, cot_columns(cots_ref, block), 1, 0)
        grad_refs[step][...] = grad.astype(grad_refs[step].dtype)


def call(kernel, name, out_shape, interpret, *inputs, specs=None):
    many = isinstance(out_shape, tuple)
    outs = out_shape if many else (out_shape,)
    in_specs = [whole(x.shape) for x in inputs]
    for at, spec in (specs or {}).items():
        in_specs[at] = spec
    out_specs = tuple(whole(x.shape) for x in outs)
    return pl.pallas_call(
        kernel,
        out_shape=out_shape,
        grid=(1,),
        in_specs=in_specs,
        out_specs=out_specs if many else out_specs[0],
        compiler_params=pltpu.CompilerParams(vmem_limit_bytes=VMEM_LIMIT),
        cost_estimate=pl.CostEstimate(flops=1_000_000_000, transcendentals=0, bytes_accessed=2_000_000),
        interpret=interpret,
        name=name,
    )(*inputs)


SCALAR = pl.BlockSpec(memory_space=pltpu.SMEM)


def pack(streams, long_filter, interpret=False):
    shape = jax.ShapeDtypeStruct((SEQ, ROWS, 4 * LANE), BF16)
    return call(pack_kernel, "pack", shape, interpret, streams, long_filter)


def unpack(got, interpret=False):
    shapes = (
        jax.ShapeDtypeStruct((3, ROWS, COLS), BF16),
        jax.ShapeDtypeStruct((ROWS, COLS), F32),
    )
    return call(unpack_kernel, "unpack", shapes, interpret, got)


def to_send(near, gated, cots, weights, interpret=False):
    shape = jax.ShapeDtypeStruct((SEQ, 2 * LANE, FAR * ROWS), BF16)
    return call(send_kernel, "send", shape, interpret, near, gated, cots, *weights, specs={0: SCALAR})


def products(near, got, cots, weights, interpret=False):
    width = weights[0].shape[1]
    shapes = (jax.ShapeDtypeStruct((CHAN, ROWS, COLS), BF16),) + tuple(
        jax.ShapeDtypeStruct((COLS, width), BF16 if step else F32) for step in range(NEAR)
    )
    half = pl.BlockSpec((SEQ, LANE, FAR * ROWS), lambda _: (0, 0, 0))
    return call(
        product_kernel, "products", shapes, interpret, near, got, cots, *weights,
        specs={0: SCALAR, 1: half},
    )


def shards(projected, short_filter, long_filter, w_out, d_out):
    seq_at = lax.axis_index("seq")
    near = (seq_at % NEAR).astype(jnp.int32).reshape(1)
    consts = [jnp.asarray(table) for table in tables()]

    moved = swapped(d_out)
    signals = exchange(pack(projected.transpose(1, 0, 2), long_filter), "seq")
    cots = exchange(jnp.broadcast_to(moved[None], (CHAN, ROWS, COLS)), "chan")
    weights = [w_out] + [lax.ppermute(w_out, "seq", near_pairs(step)) for step in range(1, NEAR)]

    own = lax.dynamic_slice_in_dim(short_filter, seq_at * LANE, LANE, axis=2).reshape(3, 3 * LANE)
    plain = jnp.zeros((3, LANE), F32).at[0].set(1.0)
    taps = jnp.concatenate([own, plain], axis=1)

    gated, kept, spec = convolve(signals.reshape(TOKENS, 4 * LANE), taps, consts)
    got = exchange(to_send(near, gated, cots, weights), "seq")

    partial_out, d_wout, *others = products(near, got, cots, weights)
    shares = exchange(partial_out, "chan")
    output = swapped(jnp.sum(shares.astype(F32), axis=0).astype(BF16))
    for step, piece in enumerate(others, 1):
        d_wout = d_wout + lax.ppermute(piece, "seq", near_pairs(step)).astype(F32)

    returned = exchange(correlate(got, kept, spec, taps, consts), "seq")
    d_projected, d_filter = unpack(returned)
    return (output, d_projected.transpose(1, 0, 2), d_wout, d_filter)


def solution(mesh):
    in_specs = (
        P("seq", None, "chan"),
        P(None, None, "chan"),
        P("seq", "chan"),
        P("chan", "seq"),
        P("seq", "chan"),
    )
    out_specs = (P("seq", "chan"), P("seq", None, "chan"), P("chan", "seq"), P("seq", "chan"))
    return jax.shard_map(shards, mesh=mesh, in_specs=in_specs, out_specs=out_specs, check_vma=False)
```

```python
import numpy as np
import ml_dtypes

import jax
import jax.numpy as jnp
from jax import lax
from jax.experimental import pallas as pl
from jax.experimental.pallas import tpu as pltpu
from jax.sharding import PartitionSpec as P

BF16 = jnp.bfloat16
F32 = jnp.float32

SEQ = 16
CHAN = 8
TOKENS = 2048
ROWS = 128
COLS = 512
LANE = 32
NEAR = 4
FAR = SEQ // NEAR
HALF = 33
MID = 72
BACK = 80
VMEM_LIMIT = 48 * 1024 * 1024
WIDE = 16
GROUP = 11


def device(seq_at, chan_at):
    return seq_at * CHAN + chan_at


def swap_pairs():
    pairs = []
    for seq_at in range(SEQ):
        for chan_at in range(CHAN):
            a, i = divmod(seq_at, NEAR)
            b, p = divmod(chan_at, CHAN // FAR)
            pairs.append(
                (device(seq_at, chan_at), device(b * NEAR + i, a * (CHAN // FAR) + p))
            )
    return pairs


def swapped(array):
    return lax.ppermute(array, ("seq", "chan"), swap_pairs())


def near_pairs(step):
    return [(i, i ^ step) for i in range(SEQ)]


def chan_pairs(step):
    return [(i, i ^ step) for i in range(CHAN)]


def exchange(array, axis):
    return lax.all_to_all(array, axis, 0, 0, tiled=True)


def thrice(table):
    high = table.astype(ml_dtypes.bfloat16)
    low = (table - high.astype(np.float64)).astype(ml_dtypes.bfloat16)
    return np.concatenate([high, high, low], axis=-1)


def tables():
    n1 = np.arange(32)
    n2 = np.arange(64)
    k1 = np.arange(HALF)
    k2 = np.arange(64)
    time = 64 * n1[None, None, :] + n2[:, None, None]
    outer = 2.0 * np.pi / 4096.0 * ((time * k1[None, :, None]) % 4096)
    inner = 2.0 * np.pi / 64.0 * ((k2[:, None] * n2[None, :]) % 64)
    weight = np.where((k1 == 0) | (k1 == 32), 1.0, 2.0)[None, :, None] / 4096.0
    first = np.zeros((64, MID, 32))
    first[:, :HALF] = np.cos(outer)
    first[:, HALF : 2 * HALF] = -np.sin(outer)
    last = np.zeros((64, 32, BACK))
    last[:, :, 0 : 2 * HALF : 2] = (np.cos(outer) * weight).transpose(0, 2, 1)
    last[:, :, 1 : 2 * HALF : 2] = (-np.sin(outer) * weight).transpose(0, 2, 1)
    cos, sin = np.cos(inner), np.sin(inner)
    ahead = np.block([[cos, sin], [-sin, cos]])
    return thrice(first), thrice(ahead), thrice(ahead.T), thrice(last)


def pieces(array):
    high = array.astype(BF16)
    low = (array - high.astype(F32)).astype(BF16)
    return jnp.concatenate([high, low, high], axis=0)


def matmul(left, right):
    return jnp.dot(left, right, preferred_element_type=F32)


def every(count, width, step):
    def body(block, carry):
        for at in range(width):
            step(block * width + at)
        return carry

    lax.fori_loop(0, count // width, body, 0)


def lanes_of(rows):
    return lax.broadcasted_iota(jnp.int32, (rows, 4 * LANE), 1)


def ahead_rows(mid_ref, first):
    return jnp.concatenate(
        [
            jnp.concatenate(
                [
                    mid_ref[pl.ds(first + at, 64, stride=MID), :],
                    mid_ref[pl.ds(HALF + first + at, 64, stride=MID), :],
                ],
                axis=0,
            )
            for at in range(GROUP)
        ],
        axis=1,
    )


def behind_rows(back_ref, first, behind_ref, products):
    found = matmul(behind_ref[...], pieces(jnp.concatenate(products, axis=1)))
    for at in range(GROUP):
        back_ref[pl.ds(pl.multiple_of((first + at) * 128, 128), 128), :] = found[
            :, at * 128 : (at + 1) * 128
        ]


def started(source, target, sem):
    copy = pltpu.make_async_copy(source, target, sem)
    copy.start()
    return copy


def forward_kernel(
    signal_ref, taps_ref, first_hbm, ahead_hbm, behind_hbm, last_hbm,
    gated_ref, kept_hbm, spec_hbm,
    wide_ref, mid_ref, back_ref, column_ref,
    first_ref, ahead_ref, behind_ref, last_ref, kept_ref, spec_ref, sems,
):
    first_copy = started(first_hbm, first_ref, sems.at[0])
    ahead_copy = started(ahead_hbm, ahead_ref, sems.at[1])
    behind_copy = started(behind_hbm, behind_ref, sems.at[2])
    last_copy = started(last_hbm, last_ref, sems.at[3])
    wide_ref[0:8, :] = jnp.zeros((8, 4 * LANE), F32)
    wide_ref[8:, :] = signal_ref[...].astype(F32)
    back_ref[2 * HALF * 64 :, :] = jnp.zeros(((BACK - 2 * HALF) * 64, 4 * LANE), F32)
    lane = lanes_of(32)
    tap0, tap1, tap2 = (jnp.broadcast_to(taps_ref[j : j + 1, :], (32, 4 * LANE)) for j in range(3))

    def outer(n2):
        now = wide_ref[pl.ds(n2 + 8, 32, stride=64), :]
        before = wide_ref[pl.ds(n2 + 7, 32, stride=64), :]
        earlier = wide_ref[pl.ds(n2 + 6, 32, stride=64), :]
        mixed = tap0 * now + tap1 * before + tap2 * earlier
        kept_ref[pl.ds(n2, 32, stride=64), :] = mixed
        carried = mixed * pltpu.roll(mixed, LANE, 1)
        data = jnp.where((lane >= 2 * LANE) & (lane < 3 * LANE), carried, mixed)
        mid_ref[pl.ds(pl.multiple_of(n2 * MID, 8), MID), :] = matmul(first_ref[n2], pieces(data))

    first_copy.wait()
    every(64, WIDE, outer)

    def inner(group):
        spec = matmul(ahead_ref[...], pieces(ahead_rows(mid_ref, group * GROUP)))
        products = []
        for at in range(GROUP):
            one = spec[:, at * 128 : (at + 1) * 128]
            spec_ref[group * GROUP + at] = one
            other = pltpu.roll(one, 3 * LANE, 1)
            re, im, other_re, other_im = one[:64], one[64:], other[:64], other[64:]
            products.append(
                jnp.concatenate(
                    [re * other_re - im * other_im, re * other_im + im * other_re], axis=0
                )
            )
        behind_rows(back_ref, group * GROUP, behind_ref, products)

    ahead_copy.wait()
    behind_copy.wait()
    every(HALF // GROUP, 1, inner)
    spec_copy = started(spec_ref, spec_hbm, sems.at[4])

    def final(n2):
        conv = matmul(last_ref[n2], pieces(back_ref[pl.ds(n2, BACK, stride=64), :]))
        mixed = kept_ref[pl.ds(n2, 32, stride=64), :]
        column_ref[pl.ds(n2, 32, stride=64), :] = mixed * pltpu.roll(conv, 2 * LANE, 1)
        kept_ref[pl.ds(n2, 32, stride=64), :] = jnp.where(
            lane < 3 * LANE, mixed, pltpu.roll(conv, LANE, 1)
        )

    last_copy.wait()
    every(64, WIDE, final)
    kept_copy = started(kept_ref, kept_hbm, sems.at[5])

    for block in range(SEQ):
        a, i = divmod(block, NEAR)
        turned = column_ref[block * ROWS : (block + 1) * ROWS, :].T
        gated_ref[i, :, a * ROWS : (a + 1) * ROWS] = turned[:LANE].astype(BF16)
    spec_copy.wait()
    kept_copy.wait()


def backward_kernel(
    share_ref, kept_hbm, spec_hbm, taps_ref, first_hbm, ahead_hbm, behind_hbm, last_hbm,
    out_ref,
    grad_ref, mid_ref, back_ref, column_ref,
    first_ref, ahead_ref, behind_ref, last_ref, kept_ref, spec_ref, sems,
):
    first_copy = started(first_hbm, first_ref, sems.at[0])
    kept_copy = started(kept_hbm, kept_ref, sems.at[5])
    ahead_copy = started(ahead_hbm, ahead_ref, sems.at[1])
    behind_copy = started(behind_hbm, behind_ref, sems.at[2])
    spec_copy = started(spec_hbm, spec_ref, sems.at[4])
    last_copy = started(last_hbm, last_ref, sems.at[3])
    back_ref[2 * HALF * 64 :, :] = jnp.zeros(((BACK - 2 * HALF) * 64, 4 * LANE), F32)
    column_ref[TOKENS:, :] = jnp.zeros((8, 4 * LANE), F32)
    for i in range(NEAR):
        total = share_ref[i].astype(F32)
        for far in range(1, FAR):
            total = total + share_ref[far * NEAR + i].astype(F32)
        for a in range(FAR):
            block = a * NEAR + i
            part = total[:, a * ROWS : (a + 1) * ROWS]
            grad_ref[block * ROWS : (block + 1) * ROWS, :] = jnp.concatenate([part] * 4, axis=0).T
    lane = lanes_of(32)

    def outer(n2):
        kept = kept_ref[pl.ds(n2, 32, stride=64), :]
        query = jnp.where(lane < 3 * LANE, pltpu.roll(kept, 2 * LANE, 1), pltpu.roll(kept, 3 * LANE, 1))
        data = grad_ref[pl.ds(n2, 32, stride=64), :] * query
        mid_ref[pl.ds(pl.multiple_of(n2 * MID, 8), MID), :] = matmul(first_ref[n2], pieces(data))

    first_copy.wait()
    kept_copy.wait()
    every(64, WIDE, outer)

    wide = lanes_of(128)

    def inner(group):
        grad = matmul(ahead_ref[...], pieces(ahead_rows(mid_ref, group * GROUP)))
        products = []
        for at in range(GROUP):
            one = grad[:, at * 128 : (at + 1) * 128]
            spec = spec_ref[group * GROUP + at]
            other = jnp.where(
                wide < 3 * LANE, pltpu.roll(spec, 3 * LANE, 1), pltpu.roll(spec, LANE, 1)
            )
            re, im, other_re, other_im = one[:64], one[64:], other[:64], other[64:]
            products.append(
                jnp.concatenate(
                    [other_re * re + other_im * im, other_re * im - other_im * re], axis=0
                )
            )
        behind_rows(back_ref, group * GROUP, behind_ref, products)

    ahead_copy.wait()
    behind_copy.wait()
    spec_copy.wait()
    every(HALF // GROUP, 1, inner)

    def final(n2):
        found = matmul(last_ref[n2], pieces(back_ref[pl.ds(n2, BACK, stride=64), :]))
        kept = kept_ref[pl.ds(n2, 32, stride=64), :]
        grad = grad_ref[pl.ds(n2, 32, stride=64), :]
        up, down = pltpu.roll(kept, LANE, 1), pltpu.roll(kept, 3 * LANE, 1)
        mixed = jnp.where(
            lane < LANE,
            grad * up,
            jnp.where(
                lane < 2 * LANE,
                pltpu.roll(found, 3 * LANE, 1) * down,
                jnp.where(lane < 3 * LANE, found * up, found),
            ),
        )
        column_ref[pl.ds(n2, 32, stride=64), :] = mixed

    last_copy.wait()
    every(64, WIDE, final)

    tap0, tap1, tap2 = (
        jnp.broadcast_to(taps_ref[j : j + 1, :], (ROWS, 4 * LANE)) for j in range(3)
    )
    for block in range(SEQ):
        low = block * ROWS
        out_ref[block] = (
            tap0 * column_ref[low : low + ROWS, :]
            + tap1 * column_ref[low + 1 : low + 1 + ROWS, :]
            + tap2 * column_ref[low + 2 : low + 2 + ROWS, :]
        ).astype(BF16)


LONG = pl.CostEstimate(flops=8_000_000_000, transcendentals=0, bytes_accessed=6_000_000)


def whole(shape):
    return pl.BlockSpec(shape, lambda _: (0,) * len(shape))


HELD = (
    pltpu.VMEM((64, MID, 96), BF16),
    pltpu.VMEM((128, 384), BF16),
    pltpu.VMEM((128, 384), BF16),
    pltpu.VMEM((64, 32, 3 * BACK), BF16),
    pltpu.VMEM((TOKENS, 4 * LANE), F32),
    pltpu.VMEM((HALF, 128, 4 * LANE), F32),
    pltpu.SemaphoreType.DMA((6,)),
)
FAR_OFF = pl.BlockSpec(memory_space=pltpu.HBM)


def resident(array):
    return pltpu.with_memory_space_constraint(array, pltpu.HBM)


def convolve(signals, taps, consts, interpret=False):
    return pl.pallas_call(
        forward_kernel,
        out_shape=(
            jax.ShapeDtypeStruct((NEAR, LANE, FAR * ROWS), BF16),
            pltpu.HBM((TOKENS, 4 * LANE), F32),
            pltpu.HBM((HALF, 128, 4 * LANE), F32),
        ),
        grid=(1,),
        in_specs=[whole(signals.shape), whole(taps.shape)] + [FAR_OFF] * 4,
        out_specs=(whole((NEAR, LANE, FAR * ROWS)), FAR_OFF, FAR_OFF),
        scratch_shapes=[
            pltpu.VMEM((TOKENS + 8, 4 * LANE), F32),
            pltpu.VMEM((64 * MID, 4 * LANE), F32),
            pltpu.VMEM((64 * BACK, 4 * LANE), F32),
            pltpu.VMEM((TOKENS, 4 * LANE), F32),
            *HELD,
        ],
        compiler_params=pltpu.CompilerParams(vmem_limit_bytes=VMEM_LIMIT),
        cost_estimate=LONG,
        interpret=interpret,
        name="convolve",
    )(signals, taps, *(resident(x) for x in consts))


def correlate(shares, kept, spec, taps, consts, interpret=False):
    half = pl.BlockSpec((SEQ, LANE, FAR * ROWS), lambda _: (0, 1, 0))
    return pl.pallas_call(
        backward_kernel,
        out_shape=jax.ShapeDtypeStruct((SEQ, ROWS, 4 * LANE), BF16),
        grid=(1,),
        in_specs=[half, FAR_OFF, FAR_OFF, whole(taps.shape)] + [FAR_OFF] * 4,
        out_specs=whole((SEQ, ROWS, 4 * LANE)),
        scratch_shapes=[
            pltpu.VMEM((TOKENS, 4 * LANE), F32),
            pltpu.VMEM((64 * MID, 4 * LANE), F32),
            pltpu.VMEM((64 * BACK, 4 * LANE), F32),
            pltpu.VMEM((TOKENS + 8, 4 * LANE), F32),
            *HELD,
        ],
        compiler_params=pltpu.CompilerParams(vmem_limit_bytes=VMEM_LIMIT),
        cost_estimate=LONG,
        interpret=interpret,
        name="correlate",
    )(shares, resident(kept), resident(spec), taps, *(resident(x) for x in consts))


def pack_kernel(streams_ref, filter_ref, out_ref):
    lane = lanes_of(ROWS)
    for column in range(COLS // 128):
        at = slice(column * 128, (column + 1) * 128)
        blocks = [streams_ref[j, :, at].astype(F32) for j in range(3)] + [filter_ref[:, at]]
        for part in range(4):
            placed = [pltpu.roll(b, ((j - part) % 4) * LANE, 1) if j != part else b
                      for j, b in enumerate(blocks)]
            joined = placed[3]
            for j in range(2, -1, -1):
                joined = jnp.where(lane < (j + 1) * LANE, placed[j], joined)
            out_ref[column * 4 + part] = joined.astype(BF16)


def unpack_kernel(got_ref, streams_ref, filter_ref):
    lane = lanes_of(ROWS)
    for column in range(COLS // 128):
        at = slice(column * 128, (column + 1) * 128)
        blocks = [got_ref[column * 4 + part].astype(F32) for part in range(4)]
        for j in range(4):
            placed = [pltpu.roll(b, ((part - j) % 4) * LANE, 1) if j != part else b
                      for part, b in enumerate(blocks)]
            joined = placed[3]
            for part in range(2, -1, -1):
                joined = jnp.where(lane < (part + 1) * LANE, placed[part], joined)
            if j < 3:
                streams_ref[j, :, at] = joined.astype(BF16)
            else:
                filter_ref[:, at] = joined


def contract(left, right, left_dim, right_dim):
    return lax.dot_general(
        left, right, (((left_dim,), (right_dim,)), ((), ())), preferred_element_type=F32
    )


def fetch(place_ref, refs, weights, cots, sems):
    copies = []
    for step in range(NEAR):
        low = pl.multiple_of((place_ref[0] ^ step) * 256, 256)
        copies.append(started(refs[step], weights.at[:, pl.ds(low, 256)], sems.at[step]))
    for far in range(FAR):
        row = pl.multiple_of((place_ref[1] ^ far) * ROWS, ROWS)
        for side in range(2):
            low = pl.multiple_of((place_ref[2] ^ side) * COLS, COLS)
            copies.append(
                started(
                    refs[NEAR + far].at[side],
                    cots.at[pl.ds(row, ROWS), pl.ds(low, COLS)],
                    sems.at[NEAR + 2 * far + side],
                )
            )
    return copies


def send_kernel(place_ref, gated_ref, *refs):
    sent_ref, weights, cots, sems = refs[NEAR + FAR :]
    copies = fetch(place_ref, refs, weights, cots, sems)
    for s in range(SEQ):
        sent_ref[s, :LANE, :] = gated_ref[s % NEAR]
    for copy in copies:
        copy.wait()
    total = contract(weights[...], cots[...], 1, 1).astype(BF16)
    for s in range(SEQ):
        sent_ref[s, LANE:, :] = total[s * LANE : (s + 1) * LANE]


def product_kernel(place_ref, got_ref, *refs):
    out_ref, *grad_refs = refs[NEAR + FAR : NEAR + FAR + 1 + NEAR]
    weights, cots, sems = refs[NEAR + FAR + 1 + NEAR :]
    copies = fetch(place_ref, refs, weights, cots, sems)
    turned = got_ref[...].reshape(COLS, FAR * ROWS).T
    for copy in copies:
        copy.wait()
    for side in range(2):
        part = contract(turned, weights[:, side * COLS : (side + 1) * COLS], 1, 0).astype(BF16)
        for a in range(FAR):
            out_ref[2 * a + side] = part[a * ROWS : (a + 1) * ROWS]
    gated = got_ref[...].reshape(COLS, FAR * ROWS)
    for step in range(NEAR):
        low = pl.multiple_of((place_ref[0] ^ step) * 256, 256)
        grad = contract(gated, cots[:, pl.ds(low, 256)], 1, 0)
        grad_refs[step][...] = grad.astype(grad_refs[step].dtype)


def call(kernel, name, out_shape, interpret, *inputs, specs=None, scratch=()):
    many = isinstance(out_shape, tuple)
    outs = out_shape if many else (out_shape,)
    in_specs = [whole(x.shape) for x in inputs]
    for at, spec in (specs or {}).items():
        in_specs[at] = spec
    out_specs = tuple(whole(x.shape) for x in outs)
    return pl.pallas_call(
        kernel,
        out_shape=out_shape,
        grid=(1,),
        in_specs=in_specs,
        out_specs=out_specs if many else out_specs[0],
        scratch_shapes=list(scratch),
        compiler_params=pltpu.CompilerParams(vmem_limit_bytes=VMEM_LIMIT),
        cost_estimate=pl.CostEstimate(flops=1_000_000_000, transcendentals=0, bytes_accessed=2_000_000),
        interpret=interpret,
        name=name,
    )(*inputs)


SCALAR = pl.BlockSpec(memory_space=pltpu.SMEM)


def pack(streams, long_filter, interpret=False):
    shape = jax.ShapeDtypeStruct((SEQ, ROWS, 4 * LANE), BF16)
    return call(
        pack_kernel, "pack", shape, interpret, resident(streams), resident(long_filter)
    )


def unpack(got, interpret=False):
    shapes = (
        jax.ShapeDtypeStruct((3, ROWS, COLS), BF16),
        jax.ShapeDtypeStruct((ROWS, COLS), F32),
    )
    return call(unpack_kernel, "unpack", shapes, interpret, got)


def far_off(low, high):
    return {at: FAR_OFF for at in range(low, high)}


GATHERED = (
    pltpu.VMEM((COLS, 2 * COLS), BF16),
    pltpu.VMEM((FAR * ROWS, 2 * COLS), BF16),
    pltpu.SemaphoreType.DMA((NEAR + 2 * FAR,)),
)


def to_send(place, gated, weights, cots, interpret=False):
    shape = jax.ShapeDtypeStruct((SEQ, 2 * LANE, FAR * ROWS), BF16)
    return call(
        send_kernel, "send", shape, interpret, place, gated, *weights, *cots,
        specs={0: SCALAR, **far_off(2, 2 + NEAR + FAR)}, scratch=GATHERED,
    )


def products(place, got, weights, cots, interpret=False):
    width = weights[0].shape[1]
    shapes = (pltpu.HBM((CHAN, ROWS, COLS), BF16),) + tuple(
        pltpu.HBM((COLS, width), BF16 if step else F32) for step in range(NEAR)
    )
    half = pl.BlockSpec((SEQ, LANE, FAR * ROWS), lambda _: (0, 0, 0))
    return call(
        product_kernel, "products", shapes, interpret, place, got, *weights, *cots,
        specs={0: SCALAR, 1: half, **far_off(2, 2 + NEAR + FAR)}, scratch=GATHERED,
    )


def shards(projected, short_filter, long_filter, w_out, d_out):
    seq_at = lax.axis_index("seq")
    chan_at = lax.axis_index("chan")
    place = jnp.stack([seq_at % NEAR, chan_at // 2, chan_at % 2]).astype(jnp.int32)
    consts = [jnp.asarray(table) for table in tables()]

    moved = swapped(d_out)
    signals = exchange(pack(projected.transpose(1, 0, 2), long_filter), "seq")
    pair = jnp.stack([moved, lax.ppermute(moved, "chan", chan_pairs(1))])
    cots = [pair] + [lax.ppermute(pair, "chan", chan_pairs(2 * far)) for far in range(1, FAR)]
    weights = [w_out] + [lax.ppermute(w_out, "seq", near_pairs(step)) for step in range(1, NEAR)]

    own = lax.dynamic_slice_in_dim(short_filter, seq_at * LANE, LANE, axis=2).reshape(3, 3 * LANE)
    plain = jnp.zeros((3, LANE), F32).at[0].set(1.0)
    taps = jnp.concatenate([own, plain], axis=1)

    gated, kept, spec = convolve(signals.reshape(TOKENS, 4 * LANE), taps, consts)
    got = exchange(to_send(place, gated, weights, cots), "seq")

    partial_out, d_wout, *others = products(place, got, weights, cots)
    shares = exchange(partial_out, "chan")
    output = swapped(jnp.sum(shares.astype(F32), axis=0).astype(BF16))
    for step, piece in enumerate(others, 1):
        d_wout = d_wout + lax.ppermute(piece, "seq", near_pairs(step)).astype(F32)

    returned = exchange(correlate(got, kept, spec, taps, consts), "seq")
    d_projected, d_filter = unpack(returned)
    return (output, d_projected.transpose(1, 0, 2), d_wout, d_filter)


def solution(mesh):
    in_specs = (
        P("seq", None, "chan"),
        P(None, None, "chan"),
        P("seq", "chan"),
        P("chan", "seq"),
        P("seq", "chan"),
    )
    out_specs = (P("seq", "chan"), P("seq", None, "chan"), P("chan", "seq"), P("seq", "chan"))
    return jax.shard_map(shards, mesh=mesh, in_specs=in_specs, out_specs=out_specs, check_vma=False)
```

```python
import numpy as np
import ml_dtypes

import jax
import jax.numpy as jnp
from jax import lax
from jax.experimental import pallas as pl
from jax.experimental.pallas import tpu as pltpu
from jax.sharding import PartitionSpec as P

BF16 = jnp.bfloat16
F32 = jnp.float32

SEQ = 16
CHAN = 8
TOKENS = 2048
ROWS = 128
COLS = 512
LANE = 32
NEAR = 4
FAR = SEQ // NEAR
HALF = 33
MID = 72
BACK = 80
VMEM_LIMIT = 48 * 1024 * 1024
WIDE = 16
GROUP = 11


def device(seq_at, chan_at):
    return seq_at * CHAN + chan_at


def swap_pairs():
    pairs = []
    for seq_at in range(SEQ):
        for chan_at in range(CHAN):
            a, i = divmod(seq_at, NEAR)
            b, p = divmod(chan_at, CHAN // FAR)
            pairs.append(
                (device(seq_at, chan_at), device(b * NEAR + i, a * (CHAN // FAR) + p))
            )
    return pairs


def swapped(array):
    return lax.ppermute(array, ("seq", "chan"), swap_pairs())


def near_pairs(step):
    return [(i, i ^ step) for i in range(SEQ)]


def chan_pairs(step):
    return [(i, i ^ step) for i in range(CHAN)]


def exchange(array, axis):
    return lax.all_to_all(array, axis, 0, 0, tiled=True)


def thrice(table):
    high = table.astype(ml_dtypes.bfloat16)
    low = (table - high.astype(np.float64)).astype(ml_dtypes.bfloat16)
    return np.concatenate([high, high, low], axis=-1)


def tables():
    n1 = np.arange(32)
    n2 = np.arange(64)
    k1 = np.arange(HALF)
    k2 = np.arange(64)
    time = 64 * n1[None, None, :] + n2[:, None, None]
    outer = 2.0 * np.pi / 4096.0 * ((time * k1[None, :, None]) % 4096)
    inner = 2.0 * np.pi / 64.0 * ((k2[:, None] * n2[None, :]) % 64)
    weight = np.where((k1 == 0) | (k1 == 32), 1.0, 2.0)[None, :, None] / 4096.0
    first = np.zeros((64, MID, 32))
    first[:, :HALF] = np.cos(outer)
    first[:, HALF : 2 * HALF] = -np.sin(outer)
    last = np.zeros((64, 32, BACK))
    last[:, :, 0 : 2 * HALF : 2] = (np.cos(outer) * weight).transpose(0, 2, 1)
    last[:, :, 1 : 2 * HALF : 2] = (-np.sin(outer) * weight).transpose(0, 2, 1)
    cos, sin = np.cos(inner), np.sin(inner)
    ahead = np.block([[cos, sin], [-sin, cos]])
    return thrice(first), thrice(ahead), thrice(ahead.T), thrice(last)


def pieces(array):
    high = array.astype(BF16)
    low = (array - high.astype(F32)).astype(BF16)
    return jnp.concatenate([high, low, high], axis=0)


def matmul(left, right):
    return jnp.dot(left, right, preferred_element_type=F32)


def every(count, width, step):
    def body(block, carry):
        for at in range(width):
            step(block * width + at)
        return carry

    lax.fori_loop(0, count // width, body, 0)


def lanes_of(rows):
    return lax.broadcasted_iota(jnp.int32, (rows, 4 * LANE), 1)


def ahead_rows(mid_ref, first):
    return jnp.concatenate(
        [
            jnp.concatenate(
                [
                    mid_ref[pl.ds(first + at, 64, stride=MID), :],
                    mid_ref[pl.ds(HALF + first + at, 64, stride=MID), :],
                ],
                axis=0,
            )
            for at in range(GROUP)
        ],
        axis=1,
    )


def behind_rows(back_ref, first, behind_ref, products):
    found = matmul(behind_ref[...], pieces(jnp.concatenate(products, axis=1)))
    for at in range(GROUP):
        back_ref[pl.ds(pl.multiple_of((first + at) * 128, 128), 128), :] = found[
            :, at * 128 : (at + 1) * 128
        ]


def started(source, target, sem):
    copy = pltpu.make_async_copy(source, target, sem)
    copy.start()
    return copy


def forward_kernel(
    signal_ref, taps_ref, first_hbm, ahead_hbm, behind_hbm, last_hbm,
    gated_ref, kept_hbm, spec_hbm,
    wide_ref, mid_ref, back_ref, column_ref,
    first_ref, ahead_ref, behind_ref, last_ref, kept_ref, spec_ref, sems,
):
    first_copy = started(first_hbm, first_ref, sems.at[0])
    ahead_copy = started(ahead_hbm, ahead_ref, sems.at[1])
    behind_copy = started(behind_hbm, behind_ref, sems.at[2])
    last_copy = started(last_hbm, last_ref, sems.at[3])
    wide_ref[0:8, :] = jnp.zeros((8, 4 * LANE), F32)
    wide_ref[8:, :] = signal_ref[...].astype(F32)
    back_ref[2 * HALF * 64 :, :] = jnp.zeros(((BACK - 2 * HALF) * 64, 4 * LANE), F32)
    lane = lanes_of(32)
    tap0, tap1, tap2 = (jnp.broadcast_to(taps_ref[j : j + 1, :], (32, 4 * LANE)) for j in range(3))

    def outer(n2):
        now = wide_ref[pl.ds(n2 + 8, 32, stride=64), :]
        before = wide_ref[pl.ds(n2 + 7, 32, stride=64), :]
        earlier = wide_ref[pl.ds(n2 + 6, 32, stride=64), :]
        mixed = tap0 * now + tap1 * before + tap2 * earlier
        kept_ref[pl.ds(n2, 32, stride=64), :] = mixed
        carried = mixed * pltpu.roll(mixed, LANE, 1)
        data = jnp.where((lane >= 2 * LANE) & (lane < 3 * LANE), carried, mixed)
        mid_ref[pl.ds(pl.multiple_of(n2 * MID, 8), MID), :] = matmul(first_ref[n2], pieces(data))

    first_copy.wait()
    every(64, WIDE, outer)

    def inner(group):
        spec = matmul(ahead_ref[...], pieces(ahead_rows(mid_ref, group * GROUP)))
        products = []
        for at in range(GROUP):
            one = spec[:, at * 128 : (at + 1) * 128]
            spec_ref[group * GROUP + at] = one
            other = pltpu.roll(one, 3 * LANE, 1)
            re, im, other_re, other_im = one[:64], one[64:], other[:64], other[64:]
            products.append(
                jnp.concatenate(
                    [re * other_re - im * other_im, re * other_im + im * other_re], axis=0
                )
            )
        behind_rows(back_ref, group * GROUP, behind_ref, products)

    ahead_copy.wait()
    behind_copy.wait()
    every(HALF // GROUP, 1, inner)
    spec_copy = started(spec_ref, spec_hbm, sems.at[4])

    def final(n2):
        conv = matmul(last_ref[n2], pieces(back_ref[pl.ds(n2, BACK, stride=64), :]))
        mixed = kept_ref[pl.ds(n2, 32, stride=64), :]
        column_ref[pl.ds(n2, 32, stride=64), :] = mixed * pltpu.roll(conv, 2 * LANE, 1)
        kept_ref[pl.ds(n2, 32, stride=64), :] = jnp.where(
            lane < 3 * LANE, mixed, pltpu.roll(conv, LANE, 1)
        )

    last_copy.wait()
    every(64, WIDE, final)
    kept_copy = started(kept_ref, kept_hbm, sems.at[5])

    for block in range(SEQ):
        a, i = divmod(block, NEAR)
        turned = column_ref[block * ROWS : (block + 1) * ROWS, :].T
        turned = turned[:LANE].astype(BF16)
        for far in range(FAR):
            gated_ref[far * NEAR + i, :, a * ROWS : (a + 1) * ROWS] = turned
    spec_copy.wait()
    kept_copy.wait()


def backward_kernel(
    share_ref, kept_hbm, spec_hbm, taps_ref, first_hbm, ahead_hbm, behind_hbm, last_hbm,
    out_ref,
    grad_ref, mid_ref, back_ref, column_ref,
    first_ref, ahead_ref, behind_ref, last_ref, kept_ref, spec_ref, sems,
):
    first_copy = started(first_hbm, first_ref, sems.at[0])
    kept_copy = started(kept_hbm, kept_ref, sems.at[5])
    ahead_copy = started(ahead_hbm, ahead_ref, sems.at[1])
    behind_copy = started(behind_hbm, behind_ref, sems.at[2])
    spec_copy = started(spec_hbm, spec_ref, sems.at[4])
    last_copy = started(last_hbm, last_ref, sems.at[3])
    back_ref[2 * HALF * 64 :, :] = jnp.zeros(((BACK - 2 * HALF) * 64, 4 * LANE), F32)
    column_ref[TOKENS:, :] = jnp.zeros((8, 4 * LANE), F32)
    for i in range(NEAR):
        total = share_ref[i].astype(F32)
        for far in range(1, FAR):
            total = total + share_ref[far * NEAR + i].astype(F32)
        for a in range(FAR):
            block = a * NEAR + i
            part = total[:, a * ROWS : (a + 1) * ROWS]
            grad_ref[block * ROWS : (block + 1) * ROWS, :] = jnp.concatenate([part] * 4, axis=0).T
    lane = lanes_of(32)

    def outer(n2):
        kept = kept_ref[pl.ds(n2, 32, stride=64), :]
        query = jnp.where(lane < 3 * LANE, pltpu.roll(kept, 2 * LANE, 1), pltpu.roll(kept, 3 * LANE, 1))
        data = grad_ref[pl.ds(n2, 32, stride=64), :] * query
        mid_ref[pl.ds(pl.multiple_of(n2 * MID, 8), MID), :] = matmul(first_ref[n2], pieces(data))

    first_copy.wait()
    kept_copy.wait()
    every(64, WIDE, outer)

    wide = lanes_of(128)

    def inner(group):
        grad = matmul(ahead_ref[...], pieces(ahead_rows(mid_ref, group * GROUP)))
        products = []
        for at in range(GROUP):
            one = grad[:, at * 128 : (at + 1) * 128]
            spec = spec_ref[group * GROUP + at]
            other = jnp.where(
                wide < 3 * LANE, pltpu.roll(spec, 3 * LANE, 1), pltpu.roll(spec, LANE, 1)
            )
            re, im, other_re, other_im = one[:64], one[64:], other[:64], other[64:]
            products.append(
                jnp.concatenate(
                    [other_re * re + other_im * im, other_re * im - other_im * re], axis=0
                )
            )
        behind_rows(back_ref, group * GROUP, behind_ref, products)

    ahead_copy.wait()
    behind_copy.wait()
    spec_copy.wait()
    every(HALF // GROUP, 1, inner)

    def final(n2):
        found = matmul(last_ref[n2], pieces(back_ref[pl.ds(n2, BACK, stride=64), :]))
        kept = kept_ref[pl.ds(n2, 32, stride=64), :]
        grad = grad_ref[pl.ds(n2, 32, stride=64), :]
        up, down = pltpu.roll(kept, LANE, 1), pltpu.roll(kept, 3 * LANE, 1)
        mixed = jnp.where(
            lane < LANE,
            grad * up,
            jnp.where(
                lane < 2 * LANE,
                pltpu.roll(found, 3 * LANE, 1) * down,
                jnp.where(lane < 3 * LANE, found * up, found),
            ),
        )
        column_ref[pl.ds(n2, 32, stride=64), :] = mixed

    last_copy.wait()
    every(64, WIDE, final)

    tap0, tap1, tap2 = (
        jnp.broadcast_to(taps_ref[j : j + 1, :], (ROWS, 4 * LANE)) for j in range(3)
    )
    for block in range(SEQ):
        low = block * ROWS
        out_ref[block] = (
            tap0 * column_ref[low : low + ROWS, :]
            + tap1 * column_ref[low + 1 : low + 1 + ROWS, :]
            + tap2 * column_ref[low + 2 : low + 2 + ROWS, :]
        ).astype(BF16)


LONG = pl.CostEstimate(flops=8_000_000_000, transcendentals=0, bytes_accessed=6_000_000)


def whole(shape):
    return pl.BlockSpec(shape, lambda _: (0,) * len(shape))


HELD = (
    pltpu.VMEM((64, MID, 96), BF16),
    pltpu.VMEM((128, 384), BF16),
    pltpu.VMEM((128, 384), BF16),
    pltpu.VMEM((64, 32, 3 * BACK), BF16),
    pltpu.VMEM((TOKENS, 4 * LANE), F32),
    pltpu.VMEM((HALF, 128, 4 * LANE), F32),
    pltpu.SemaphoreType.DMA((6,)),
)
FAR_OFF = pl.BlockSpec(memory_space=pltpu.HBM)


def resident(array):
    return pltpu.with_memory_space_constraint(array, pltpu.HBM)


def convolve(signals, taps, consts, interpret=False):
    return pl.pallas_call(
        forward_kernel,
        out_shape=(
            jax.ShapeDtypeStruct((SEQ, LANE, FAR * ROWS), BF16),
            pltpu.HBM((TOKENS, 4 * LANE), F32),
            pltpu.HBM((HALF, 128, 4 * LANE), F32),
        ),
        grid=(1,),
        in_specs=[whole(signals.shape), whole(taps.shape)] + [FAR_OFF] * 4,
        out_specs=(whole((SEQ, LANE, FAR * ROWS)), FAR_OFF, FAR_OFF),
        scratch_shapes=[
            pltpu.VMEM((TOKENS + 8, 4 * LANE), F32),
            pltpu.VMEM((64 * MID, 4 * LANE), F32),
            pltpu.VMEM((64 * BACK, 4 * LANE), F32),
            pltpu.VMEM((TOKENS, 4 * LANE), F32),
            *HELD,
        ],
        compiler_params=pltpu.CompilerParams(vmem_limit_bytes=VMEM_LIMIT),
        cost_estimate=LONG,
        interpret=interpret,
        name="convolve",
    )(signals, taps, *(resident(x) for x in consts))


def correlate(shares, kept, spec, taps, consts, interpret=False):
    return pl.pallas_call(
        backward_kernel,
        out_shape=jax.ShapeDtypeStruct((SEQ, ROWS, 4 * LANE), BF16),
        grid=(1,),
        in_specs=[whole(shares.shape), FAR_OFF, FAR_OFF, whole(taps.shape)] + [FAR_OFF] * 4,
        out_specs=whole((SEQ, ROWS, 4 * LANE)),
        scratch_shapes=[
            pltpu.VMEM((TOKENS, 4 * LANE), F32),
            pltpu.VMEM((64 * MID, 4 * LANE), F32),
            pltpu.VMEM((64 * BACK, 4 * LANE), F32),
            pltpu.VMEM((TOKENS + 8, 4 * LANE), F32),
            *HELD,
        ],
        compiler_params=pltpu.CompilerParams(vmem_limit_bytes=VMEM_LIMIT),
        cost_estimate=LONG,
        interpret=interpret,
        name="correlate",
    )(shares, resident(kept), resident(spec), taps, *(resident(x) for x in consts))


def pack_kernel(streams_ref, filter_ref, out_ref):
    lane = lanes_of(ROWS)
    for column in range(COLS // 128):
        at = slice(column * 128, (column + 1) * 128)
        blocks = [streams_ref[j, :, at].astype(F32) for j in range(3)] + [filter_ref[:, at]]
        for part in range(4):
            placed = [pltpu.roll(b, ((j - part) % 4) * LANE, 1) if j != part else b
                      for j, b in enumerate(blocks)]
            joined = placed[3]
            for j in range(2, -1, -1):
                joined = jnp.where(lane < (j + 1) * LANE, placed[j], joined)
            out_ref[column * 4 + part] = joined.astype(BF16)


def unpack_kernel(got_ref, streams_ref, filter_ref):
    lane = lanes_of(ROWS)
    for column in range(COLS // 128):
        at = slice(column * 128, (column + 1) * 128)
        blocks = [got_ref[column * 4 + part].astype(F32) for part in range(4)]
        for j in range(4):
            placed = [pltpu.roll(b, ((part - j) % 4) * LANE, 1) if j != part else b
                      for part, b in enumerate(blocks)]
            joined = placed[3]
            for part in range(2, -1, -1):
                joined = jnp.where(lane < (part + 1) * LANE, placed[part], joined)
            if j < 3:
                streams_ref[j, :, at] = joined.astype(BF16)
            else:
                filter_ref[:, at] = joined


def contract(left, right, left_dim, right_dim):
    return lax.dot_general(
        left, right, (((left_dim,), (right_dim,)), ((), ())), preferred_element_type=F32
    )


def fetch(place_ref, refs, weights, cots, sems):
    copies = []
    for step in range(NEAR):
        low = pl.multiple_of((place_ref[0] ^ step) * 256, 256)
        copies.append(started(refs[step], weights.at[:, pl.ds(low, 256)], sems.at[step]))
    for block in range(CHAN):
        far, side = divmod(block, 2)
        copies.append(
            started(
                refs[NEAR].at[block],
                cots.at[far * ROWS : (far + 1) * ROWS, side * COLS : (side + 1) * COLS],
                sems.at[NEAR + block],
            )
        )
    return copies


def send_kernel(place_ref, *refs):
    sent_ref, weights, cots, sems = refs[NEAR + 1 :]
    for copy in fetch(place_ref, refs, weights, cots, sems):
        copy.wait()
    total = contract(weights[...], cots[...], 1, 1).astype(BF16)
    sent_ref[...] = total.reshape(SEQ, LANE, FAR * ROWS)


def product_kernel(place_ref, got_ref, *refs):
    out_ref, *grad_refs = refs[NEAR + 1 : NEAR + 2 + NEAR]
    weights, cots, sems = refs[NEAR + 2 + NEAR :]
    copies = fetch(place_ref, refs, weights, cots, sems)
    gated = got_ref[...].reshape(COLS, FAR * ROWS)
    turned = gated.T
    for copy in copies:
        copy.wait()
    for side in range(2):
        part = contract(turned, weights[:, side * COLS : (side + 1) * COLS], 1, 0).astype(BF16)
        for a in range(FAR):
            out_ref[2 * a + side] = part[a * ROWS : (a + 1) * ROWS]
    for step in range(NEAR):
        low = pl.multiple_of((place_ref[0] ^ step) * 256, 256)
        grad = contract(gated, cots[:, pl.ds(low, 256)], 1, 0)
        grad_refs[step][...] = grad.astype(grad_refs[step].dtype)


def call(kernel, name, out_shape, interpret, *inputs, specs=None, scratch=()):
    many = isinstance(out_shape, tuple)
    outs = out_shape if many else (out_shape,)
    in_specs = [whole(x.shape) for x in inputs]
    for at, spec in (specs or {}).items():
        in_specs[at] = spec
    out_specs = tuple(whole(x.shape) for x in outs)
    return pl.pallas_call(
        kernel,
        out_shape=out_shape,
        grid=(1,),
        in_specs=in_specs,
        out_specs=out_specs if many else out_specs[0],
        scratch_shapes=list(scratch),
        compiler_params=pltpu.CompilerParams(vmem_limit_bytes=VMEM_LIMIT),
        cost_estimate=pl.CostEstimate(flops=1_000_000_000, transcendentals=0, bytes_accessed=2_000_000),
        interpret=interpret,
        name=name,
    )(*inputs)


SCALAR = pl.BlockSpec(memory_space=pltpu.SMEM)


def pack(streams, long_filter, interpret=False):
    shape = jax.ShapeDtypeStruct((SEQ, ROWS, 4 * LANE), BF16)
    return call(
        pack_kernel, "pack", shape, interpret, resident(streams), resident(long_filter)
    )


def unpack(got, interpret=False):
    shapes = (
        jax.ShapeDtypeStruct((3, ROWS, COLS), BF16),
        jax.ShapeDtypeStruct((ROWS, COLS), F32),
    )
    return call(unpack_kernel, "unpack", shapes, interpret, got)


def far_off(low, high):
    return {at: FAR_OFF for at in range(low, high)}


GATHERED = (
    pltpu.VMEM((COLS, 2 * COLS), BF16),
    pltpu.VMEM((FAR * ROWS, 2 * COLS), BF16),
    pltpu.SemaphoreType.DMA((NEAR + 2 * FAR,)),
)


def to_send(place, weights, cots, interpret=False):
    shape = jax.ShapeDtypeStruct((SEQ, LANE, FAR * ROWS), BF16)
    return call(
        send_kernel, "send", shape, interpret, place, *weights, cots,
        specs={0: SCALAR, **far_off(1, 2 + NEAR)}, scratch=GATHERED,
    )


def products(place, got, weights, cots, interpret=False):
    width = weights[0].shape[1]
    shapes = (pltpu.HBM((CHAN, ROWS, COLS), BF16),) + tuple(
        pltpu.HBM((COLS, width), BF16 if step else F32) for step in range(NEAR)
    )
    return call(
        product_kernel, "products", shapes, interpret, place, got, *weights, cots,
        specs={0: SCALAR, **far_off(2, 3 + NEAR)}, scratch=GATHERED,
    )


def shards(projected, short_filter, long_filter, w_out, d_out):
    seq_at = lax.axis_index("seq")
    chan_at = lax.axis_index("chan")
    place = jnp.stack([seq_at % NEAR, chan_at // 2, chan_at % 2]).astype(jnp.int32)
    consts = [jnp.asarray(table) for table in tables()]

    packed = pack(projected.transpose(1, 0, 2), long_filter)
    moved, packed = lax.optimization_barrier((swapped(d_out), packed))
    signals = exchange(packed, "seq")
    cots = lax.all_gather(moved, "chan", axis=0)
    weights = [w_out] + [lax.ppermute(w_out, "seq", near_pairs(step)) for step in range(1, NEAR)]

    own = lax.dynamic_slice_in_dim(short_filter, seq_at * LANE, LANE, axis=2).reshape(3, 3 * LANE)
    plain = jnp.zeros((3, LANE), F32).at[0].set(1.0)
    taps = jnp.concatenate([own, plain], axis=1)

    gated, kept, spec = convolve(signals.reshape(TOKENS, 4 * LANE), taps, consts)
    got = exchange(gated, "seq")
    d_gated = exchange(to_send(place, weights, cots), "seq")

    partial_out, d_wout, *others = products(place, got, weights, cots)
    partial_out, d_gated = lax.optimization_barrier((partial_out, d_gated))
    shares = exchange(partial_out, "chan")
    output = swapped(jnp.sum(shares.astype(F32), axis=0).astype(BF16))
    for step, piece in enumerate(others, 1):
        d_wout = d_wout + lax.ppermute(piece, "seq", near_pairs(step)).astype(F32)

    returned = exchange(correlate(d_gated, kept, spec, taps, consts), "seq")
    d_projected, d_filter = unpack(returned)
    return (output, d_projected.transpose(1, 0, 2), d_wout, d_filter)


def solution(mesh):
    in_specs = (
        P("seq", None, "chan"),
        P(None, None, "chan"),
        P("seq", "chan"),
        P("chan", "seq"),
        P("seq", "chan"),
    )
    out_specs = (P("seq", "chan"), P("seq", None, "chan"), P("chan", "seq"), P("seq", "chan"))
    return jax.shard_map(shards, mesh=mesh, in_specs=in_specs, out_specs=out_specs, check_vma=False)
```

```python
import numpy as np
import ml_dtypes

import jax
import jax.numpy as jnp
from jax import lax
from jax.experimental import pallas as pl
from jax.experimental.pallas import tpu as pltpu
from jax.sharding import PartitionSpec as P

BF16 = jnp.bfloat16
F32 = jnp.float32

SEQ = 16
CHAN = 8
TOKENS = 2048
ROWS = 128
COLS = 512
LANE = 32
NEAR = 4
FAR = SEQ // NEAR
HALF = 33
MID = 72
BACK = 80
VMEM_LIMIT = 48 * 1024 * 1024
WIDE = 16
GROUP = 11


def device(seq_at, chan_at):
    return seq_at * CHAN + chan_at


def swap_pairs():
    pairs = []
    for seq_at in range(SEQ):
        for chan_at in range(CHAN):
            a, i = divmod(seq_at, NEAR)
            b, p = divmod(chan_at, CHAN // FAR)
            pairs.append(
                (device(seq_at, chan_at), device(b * NEAR + i, a * (CHAN // FAR) + p))
            )
    return pairs


def swapped(array):
    return lax.ppermute(array, ("seq", "chan"), swap_pairs())


def near_pairs(step):
    return [(i, i ^ step) for i in range(SEQ)]


def chan_pairs(step):
    return [(i, i ^ step) for i in range(CHAN)]


def exchange(array, axis):
    return lax.all_to_all(array, axis, 0, 0, tiled=True)


def thrice(table):
    high = table.astype(ml_dtypes.bfloat16)
    low = (table - high.astype(np.float64)).astype(ml_dtypes.bfloat16)
    return np.concatenate([high, high, low], axis=-1)


def tables():
    n1 = np.arange(32)
    n2 = np.arange(64)
    k1 = np.arange(HALF)
    k2 = np.arange(64)
    time = 64 * n1[None, None, :] + n2[:, None, None]
    outer = 2.0 * np.pi / 4096.0 * ((time * k1[None, :, None]) % 4096)
    inner = 2.0 * np.pi / 64.0 * ((k2[:, None] * n2[None, :]) % 64)
    weight = np.where((k1 == 0) | (k1 == 32), 1.0, 2.0)[None, :, None] / 4096.0
    first = np.zeros((64, MID, 32))
    first[:, :HALF] = np.cos(outer)
    first[:, HALF : 2 * HALF] = -np.sin(outer)
    last = np.zeros((64, 32, BACK))
    last[:, :, 0 : 2 * HALF : 2] = (np.cos(outer) * weight).transpose(0, 2, 1)
    last[:, :, 1 : 2 * HALF : 2] = (-np.sin(outer) * weight).transpose(0, 2, 1)
    cos, sin = np.cos(inner), np.sin(inner)
    ahead = np.block([[cos, sin], [-sin, cos]])
    return thrice(first), thrice(ahead), thrice(ahead.T), thrice(last)


def pieces(array):
    high = array.astype(BF16)
    low = (array - high.astype(F32)).astype(BF16)
    return jnp.concatenate([high, low, high], axis=0)


def matmul(left, right):
    return jnp.dot(left, right, preferred_element_type=F32)


def every(count, width, step):
    def body(block, carry):
        for at in range(width):
            step(block * width + at)
        return carry

    lax.fori_loop(0, count // width, body, 0)


def lanes_of(rows):
    return lax.broadcasted_iota(jnp.int32, (rows, 4 * LANE), 1)


def ahead_rows(mid_ref, first):
    return jnp.concatenate(
        [
            jnp.concatenate(
                [
                    mid_ref[pl.ds(first + at, 64, stride=MID), :],
                    mid_ref[pl.ds(HALF + first + at, 64, stride=MID), :],
                ],
                axis=0,
            )
            for at in range(GROUP)
        ],
        axis=1,
    )


def behind_rows(back_ref, first, behind_ref, products):
    found = matmul(behind_ref[...], pieces(jnp.concatenate(products, axis=1)))
    for at in range(GROUP):
        back_ref[pl.ds(pl.multiple_of((first + at) * 128, 128), 128), :] = found[
            :, at * 128 : (at + 1) * 128
        ]


def started(source, target, sem):
    copy = pltpu.make_async_copy(source, target, sem)
    copy.start()
    return copy


def forward_kernel(
    signal_ref, taps_ref, first_hbm, ahead_hbm, behind_hbm, last_hbm,
    gated_ref, kept_hbm, spec_hbm,
    wide_ref, mid_ref, back_ref, column_ref,
    first_ref, ahead_ref, behind_ref, last_ref, kept_ref, spec_ref, sems,
):
    first_copy = started(first_hbm, first_ref, sems.at[0])
    ahead_copy = started(ahead_hbm, ahead_ref, sems.at[1])
    behind_copy = started(behind_hbm, behind_ref, sems.at[2])
    last_copy = started(last_hbm, last_ref, sems.at[3])
    wide_ref[0:8, :] = jnp.zeros((8, 4 * LANE), F32)
    wide_ref[8:, :] = signal_ref[...].astype(F32)
    back_ref[2 * HALF * 64 :, :] = jnp.zeros(((BACK - 2 * HALF) * 64, 4 * LANE), F32)
    lane = lanes_of(32)
    tap0, tap1, tap2 = (jnp.broadcast_to(taps_ref[j : j + 1, :], (32, 4 * LANE)) for j in range(3))

    def outer(n2):
        now = wide_ref[pl.ds(n2 + 8, 32, stride=64), :]
        before = wide_ref[pl.ds(n2 + 7, 32, stride=64), :]
        earlier = wide_ref[pl.ds(n2 + 6, 32, stride=64), :]
        mixed = tap0 * now + tap1 * before + tap2 * earlier
        kept_ref[pl.ds(n2, 32, stride=64), :] = mixed
        carried = mixed * pltpu.roll(mixed, LANE, 1)
        data = jnp.where((lane >= 2 * LANE) & (lane < 3 * LANE), carried, mixed)
        mid_ref[pl.ds(pl.multiple_of(n2 * MID, 8), MID), :] = matmul(first_ref[n2], pieces(data))

    first_copy.wait()
    every(64, WIDE, outer)

    def inner(group):
        spec = matmul(ahead_ref[...], pieces(ahead_rows(mid_ref, group * GROUP)))
        products = []
        for at in range(GROUP):
            one = spec[:, at * 128 : (at + 1) * 128]
            spec_ref[group * GROUP + at] = one
            other = pltpu.roll(one, 3 * LANE, 1)
            re, im, other_re, other_im = one[:64], one[64:], other[:64], other[64:]
            products.append(
                jnp.concatenate(
                    [re * other_re - im * other_im, re * other_im + im * other_re], axis=0
                )
            )
        behind_rows(back_ref, group * GROUP, behind_ref, products)

    ahead_copy.wait()
    behind_copy.wait()
    every(HALF // GROUP, 1, inner)
    spec_copy = started(spec_ref, spec_hbm, sems.at[4])

    def final(n2):
        conv = matmul(last_ref[n2], pieces(back_ref[pl.ds(n2, BACK, stride=64), :]))
        mixed = kept_ref[pl.ds(n2, 32, stride=64), :]
        column_ref[pl.ds(n2, 32, stride=64), :] = mixed * pltpu.roll(conv, 2 * LANE, 1)
        kept_ref[pl.ds(n2, 32, stride=64), :] = jnp.where(
            lane < 3 * LANE, mixed, pltpu.roll(conv, LANE, 1)
        )

    last_copy.wait()
    every(64, WIDE, final)
    kept_copy = started(kept_ref, kept_hbm, sems.at[5])

    for block in range(SEQ):
        a, i = divmod(block, NEAR)
        turned = column_ref[block * ROWS : (block + 1) * ROWS, :].T
        gated_ref[i, :, a * ROWS : (a + 1) * ROWS] = turned[:LANE].astype(BF16)
    spec_copy.wait()
    kept_copy.wait()


def backward_kernel(
    share_ref, kept_hbm, spec_hbm, taps_ref, first_hbm, ahead_hbm, behind_hbm, last_hbm,
    out_ref,
    grad_ref, mid_ref, back_ref, column_ref,
    first_ref, ahead_ref, behind_ref, last_ref, kept_ref, spec_ref, sems,
):
    first_copy = started(first_hbm, first_ref, sems.at[0])
    kept_copy = started(kept_hbm, kept_ref, sems.at[5])
    ahead_copy = started(ahead_hbm, ahead_ref, sems.at[1])
    behind_copy = started(behind_hbm, behind_ref, sems.at[2])
    spec_copy = started(spec_hbm, spec_ref, sems.at[4])
    last_copy = started(last_hbm, last_ref, sems.at[3])
    back_ref[2 * HALF * 64 :, :] = jnp.zeros(((BACK - 2 * HALF) * 64, 4 * LANE), F32)
    column_ref[TOKENS:, :] = jnp.zeros((8, 4 * LANE), F32)
    for i in range(NEAR):
        total = share_ref[i].astype(F32)
        for far in range(1, FAR):
            total = total + share_ref[far * NEAR + i].astype(F32)
        for a in range(FAR):
            block = a * NEAR + i
            part = total[:, a * ROWS : (a + 1) * ROWS]
            grad_ref[block * ROWS : (block + 1) * ROWS, :] = jnp.concatenate([part] * 4, axis=0).T
    lane = lanes_of(32)

    def outer(n2):
        kept = kept_ref[pl.ds(n2, 32, stride=64), :]
        query = jnp.where(lane < 3 * LANE, pltpu.roll(kept, 2 * LANE, 1), pltpu.roll(kept, 3 * LANE, 1))
        data = grad_ref[pl.ds(n2, 32, stride=64), :] * query
        mid_ref[pl.ds(pl.multiple_of(n2 * MID, 8), MID), :] = matmul(first_ref[n2], pieces(data))

    first_copy.wait()
    kept_copy.wait()
    every(64, WIDE, outer)

    wide = lanes_of(128)

    def inner(group):
        grad = matmul(ahead_ref[...], pieces(ahead_rows(mid_ref, group * GROUP)))
        products = []
        for at in range(GROUP):
            one = grad[:, at * 128 : (at + 1) * 128]
            spec = spec_ref[group * GROUP + at]
            other = jnp.where(
                wide < 3 * LANE, pltpu.roll(spec, 3 * LANE, 1), pltpu.roll(spec, LANE, 1)
            )
            re, im, other_re, other_im = one[:64], one[64:], other[:64], other[64:]
            products.append(
                jnp.concatenate(
                    [other_re * re + other_im * im, other_re * im - other_im * re], axis=0
                )
            )
        behind_rows(back_ref, group * GROUP, behind_ref, products)

    ahead_copy.wait()
    behind_copy.wait()
    spec_copy.wait()
    every(HALF // GROUP, 1, inner)

    def final(n2):
        found = matmul(last_ref[n2], pieces(back_ref[pl.ds(n2, BACK, stride=64), :]))
        kept = kept_ref[pl.ds(n2, 32, stride=64), :]
        grad = grad_ref[pl.ds(n2, 32, stride=64), :]
        up, down = pltpu.roll(kept, LANE, 1), pltpu.roll(kept, 3 * LANE, 1)
        mixed = jnp.where(
            lane < LANE,
            grad * up,
            jnp.where(
                lane < 2 * LANE,
                pltpu.roll(found, 3 * LANE, 1) * down,
                jnp.where(lane < 3 * LANE, found * up, found),
            ),
        )
        column_ref[pl.ds(n2, 32, stride=64), :] = mixed

    last_copy.wait()
    every(64, WIDE, final)

    tap0, tap1, tap2 = (
        jnp.broadcast_to(taps_ref[j : j + 1, :], (ROWS, 4 * LANE)) for j in range(3)
    )
    for block in range(SEQ):
        low = block * ROWS
        out_ref[block] = (
            tap0 * column_ref[low : low + ROWS, :]
            + tap1 * column_ref[low + 1 : low + 1 + ROWS, :]
            + tap2 * column_ref[low + 2 : low + 2 + ROWS, :]
        ).astype(BF16)


LONG = pl.CostEstimate(flops=8_000_000_000, transcendentals=0, bytes_accessed=6_000_000)


def whole(shape):
    return pl.BlockSpec(shape, lambda _: (0,) * len(shape))


HELD = (
    pltpu.VMEM((64, MID, 96), BF16),
    pltpu.VMEM((128, 384), BF16),
    pltpu.VMEM((128, 384), BF16),
    pltpu.VMEM((64, 32, 3 * BACK), BF16),
    pltpu.VMEM((TOKENS, 4 * LANE), F32),
    pltpu.VMEM((HALF, 128, 4 * LANE), F32),
    pltpu.SemaphoreType.DMA((6,)),
)
FAR_OFF = pl.BlockSpec(memory_space=pltpu.HBM)


def resident(array):
    return pltpu.with_memory_space_constraint(array, pltpu.HBM)


def convolve(signals, taps, consts, interpret=False):
    return pl.pallas_call(
        forward_kernel,
        out_shape=(
            jax.ShapeDtypeStruct((NEAR, LANE, FAR * ROWS), BF16),
            pltpu.HBM((TOKENS, 4 * LANE), F32),
            pltpu.HBM((HALF, 128, 4 * LANE), F32),
        ),
        grid=(1,),
        in_specs=[whole(signals.shape), whole(taps.shape)] + [FAR_OFF] * 4,
        out_specs=(whole((NEAR, LANE, FAR * ROWS)), FAR_OFF, FAR_OFF),
        scratch_shapes=[
            pltpu.VMEM((TOKENS + 8, 4 * LANE), F32),
            pltpu.VMEM((64 * MID, 4 * LANE), F32),
            pltpu.VMEM((64 * BACK, 4 * LANE), F32),
            pltpu.VMEM((TOKENS, 4 * LANE), F32),
            *HELD,
        ],
        compiler_params=pltpu.CompilerParams(vmem_limit_bytes=VMEM_LIMIT),
        cost_estimate=LONG,
        interpret=interpret,
        name="convolve",
    )(signals, taps, *(resident(x) for x in consts))


def correlate(shares, kept, spec, taps, consts, interpret=False):
    half = pl.BlockSpec((SEQ, LANE, FAR * ROWS), lambda _: (0, 1, 0))
    return pl.pallas_call(
        backward_kernel,
        out_shape=jax.ShapeDtypeStruct((SEQ, ROWS, 4 * LANE), BF16),
        grid=(1,),
        in_specs=[half, FAR_OFF, FAR_OFF, whole(taps.shape)] + [FAR_OFF] * 4,
        out_specs=whole((SEQ, ROWS, 4 * LANE)),
        scratch_shapes=[
            pltpu.VMEM((TOKENS, 4 * LANE), F32),
            pltpu.VMEM((64 * MID, 4 * LANE), F32),
            pltpu.VMEM((64 * BACK, 4 * LANE), F32),
            pltpu.VMEM((TOKENS + 8, 4 * LANE), F32),
            *HELD,
        ],
        compiler_params=pltpu.CompilerParams(vmem_limit_bytes=VMEM_LIMIT),
        cost_estimate=LONG,
        interpret=interpret,
        name="correlate",
    )(shares, resident(kept), resident(spec), taps, *(resident(x) for x in consts))


def pack_kernel(streams_ref, filter_ref, out_ref):
    lane = lanes_of(ROWS)
    for column in range(COLS // 128):
        at = slice(column * 128, (column + 1) * 128)
        blocks = [streams_ref[j, :, at].astype(F32) for j in range(3)] + [filter_ref[:, at]]
        for part in range(4):
            placed = [pltpu.roll(b, ((j - part) % 4) * LANE, 1) if j != part else b
                      for j, b in enumerate(blocks)]
            joined = placed[3]
            for j in range(2, -1, -1):
                joined = jnp.where(lane < (j + 1) * LANE, placed[j], joined)
            out_ref[column * 4 + part] = joined.astype(BF16)


def unpack_kernel(got_ref, streams_ref, filter_ref):
    lane = lanes_of(ROWS)
    for column in range(COLS // 128):
        at = slice(column * 128, (column + 1) * 128)
        blocks = [got_ref[column * 4 + part].astype(F32) for part in range(4)]
        for j in range(4):
            placed = [pltpu.roll(b, ((part - j) % 4) * LANE, 1) if j != part else b
                      for part, b in enumerate(blocks)]
            joined = placed[3]
            for part in range(2, -1, -1):
                joined = jnp.where(lane < (part + 1) * LANE, placed[part], joined)
            if j < 3:
                streams_ref[j, :, at] = joined.astype(BF16)
            else:
                filter_ref[:, at] = joined


def contract(left, right, left_dim, right_dim):
    return lax.dot_general(
        left, right, (((left_dim,), (right_dim,)), ((), ())), preferred_element_type=F32
    )


def fetch(place_ref, refs, weights, cots, sems):
    copies = []
    for step in range(NEAR):
        low = pl.multiple_of((place_ref[0] ^ step) * 256, 256)
        copies.append(started(refs[step], weights.at[:, pl.ds(low, 256)], sems.at[step]))
    for far in range(FAR):
        row = pl.multiple_of((place_ref[1] ^ far) * ROWS, ROWS)
        for side in range(2):
            low = pl.multiple_of((place_ref[2] ^ side) * COLS, COLS)
            copies.append(
                started(
                    refs[NEAR + far].at[side],
                    cots.at[pl.ds(row, ROWS), pl.ds(low, COLS)],
                    sems.at[NEAR + 2 * far + side],
                )
            )
    return copies


def send_kernel(place_ref, gated_ref, *refs):
    sent_ref, weights, cots, sems = refs[NEAR + FAR :]
    copies = fetch(place_ref, refs, weights, cots, sems)
    for s in range(SEQ):
        sent_ref[s, :LANE, :] = gated_ref[s % NEAR]
    for copy in copies:
        copy.wait()
    total = contract(weights[...], cots[...], 1, 1).astype(BF16)
    for s in range(SEQ):
        sent_ref[s, LANE:, :] = total[s * LANE : (s + 1) * LANE]


def product_kernel(place_ref, got_ref, *refs):
    out_ref, *grad_refs = refs[NEAR + FAR : NEAR + FAR + 1 + NEAR]
    weights, cots, sems = refs[NEAR + FAR + 1 + NEAR :]
    copies = fetch(place_ref, refs, weights, cots, sems)
    turned = got_ref[...].reshape(COLS, FAR * ROWS).T
    for copy in copies:
        copy.wait()
    for side in range(2):
        part = contract(turned, weights[:, side * COLS : (side + 1) * COLS], 1, 0).astype(BF16)
        for a in range(FAR):
            out_ref[2 * a + side] = part[a * ROWS : (a + 1) * ROWS]
    gated = got_ref[...].reshape(COLS, FAR * ROWS)
    for step in range(NEAR):
        low = pl.multiple_of((place_ref[0] ^ step) * 256, 256)
        grad = contract(gated, cots[:, pl.ds(low, 256)], 1, 0)
        grad_refs[step][...] = grad.astype(grad_refs[step].dtype)


def call(kernel, name, out_shape, interpret, *inputs, specs=None, scratch=()):
    many = isinstance(out_shape, tuple)
    outs = out_shape if many else (out_shape,)
    in_specs = [whole(x.shape) for x in inputs]
    for at, spec in (specs or {}).items():
        in_specs[at] = spec
    out_specs = tuple(whole(x.shape) for x in outs)
    return pl.pallas_call(
        kernel,
        out_shape=out_shape,
        grid=(1,),
        in_specs=in_specs,
        out_specs=out_specs if many else out_specs[0],
        scratch_shapes=list(scratch),
        compiler_params=pltpu.CompilerParams(vmem_limit_bytes=VMEM_LIMIT),
        cost_estimate=pl.CostEstimate(flops=1_000_000_000, transcendentals=0, bytes_accessed=2_000_000),
        interpret=interpret,
        name=name,
    )(*inputs)


SCALAR = pl.BlockSpec(memory_space=pltpu.SMEM)


def pack(streams, long_filter, interpret=False):
    shape = jax.ShapeDtypeStruct((SEQ, ROWS, 4 * LANE), BF16)
    return call(
        pack_kernel, "pack", shape, interpret, resident(streams), resident(long_filter)
    )


def unpack(got, interpret=False):
    shapes = (
        jax.ShapeDtypeStruct((3, ROWS, COLS), BF16),
        jax.ShapeDtypeStruct((ROWS, COLS), F32),
    )
    return call(unpack_kernel, "unpack", shapes, interpret, got)


def far_off(low, high):
    return {at: FAR_OFF for at in range(low, high)}


GATHERED = (
    pltpu.VMEM((COLS, 2 * COLS), BF16),
    pltpu.VMEM((FAR * ROWS, 2 * COLS), BF16),
    pltpu.SemaphoreType.DMA((NEAR + 2 * FAR,)),
)


def to_send(place, gated, weights, cots, interpret=False):
    shape = jax.ShapeDtypeStruct((SEQ, 2 * LANE, FAR * ROWS), BF16)
    return call(
        send_kernel, "send", shape, interpret, place, gated, *weights, *cots,
        specs={0: SCALAR, **far_off(2, 2 + NEAR + FAR)}, scratch=GATHERED,
    )


def products(place, got, weights, cots, interpret=False):
    width = weights[0].shape[1]
    shapes = (pltpu.HBM((CHAN, ROWS, COLS), BF16),) + tuple(
        pltpu.HBM((COLS, width), BF16 if step else F32) for step in range(NEAR)
    )
    half = pl.BlockSpec((SEQ, LANE, FAR * ROWS), lambda _: (0, 0, 0))
    return call(
        product_kernel, "products", shapes, interpret, place, got, *weights, *cots,
        specs={0: SCALAR, 1: half, **far_off(2, 2 + NEAR + FAR)}, scratch=GATHERED,
    )


def shards(projected, short_filter, long_filter, w_out, d_out):
    seq_at = lax.axis_index("seq")
    chan_at = lax.axis_index("chan")
    place = jnp.stack([seq_at % NEAR, chan_at // 2, chan_at % 2]).astype(jnp.int32)
    consts = [jnp.asarray(table) for table in tables()]

    packed = pack(projected.transpose(1, 0, 2), long_filter)
    moved, packed = lax.optimization_barrier((swapped(d_out), packed))
    signals = exchange(packed, "seq")
    pair = jnp.stack([moved, lax.ppermute(moved, "chan", chan_pairs(1))])
    pair, late = lax.optimization_barrier((pair, w_out))
    cots = [pair] + [lax.ppermute(pair, "chan", chan_pairs(2 * far)) for far in range(1, FAR)]
    across = lax.ppermute(late, "seq", near_pairs(2))
    weights = [late, lax.ppermute(late, "seq", near_pairs(1)), across,
               lax.ppermute(across, "seq", near_pairs(1))]

    own = lax.dynamic_slice_in_dim(short_filter, seq_at * LANE, LANE, axis=2).reshape(3, 3 * LANE)
    plain = jnp.zeros((3, LANE), F32).at[0].set(1.0)
    taps = jnp.concatenate([own, plain], axis=1)

    gated, kept, spec = convolve(signals.reshape(TOKENS, 4 * LANE), taps, consts)
    got = exchange(to_send(place, gated, weights, cots), "seq")

    partial_out, d_wout, *others = products(place, got, weights, cots)
    shares = exchange(partial_out, "chan")
    output = swapped(jnp.sum(shares.astype(F32), axis=0).astype(BF16))
    for step, piece in enumerate(others, 1):
        d_wout = d_wout + lax.ppermute(piece, "seq", near_pairs(step)).astype(F32)

    returned = exchange(correlate(got, kept, spec, taps, consts), "seq")
    d_projected, d_filter = unpack(returned)
    return (output, d_projected.transpose(1, 0, 2), d_wout, d_filter)


def solution(mesh):
    in_specs = (
        P("seq", None, "chan"),
        P(None, None, "chan"),
        P("seq", "chan"),
        P("chan", "seq"),
        P("seq", "chan"),
    )
    out_specs = (P("seq", "chan"), P("seq", None, "chan"), P("chan", "seq"), P("seq", "chan"))
    return jax.shard_map(shards, mesh=mesh, in_specs=in_specs, out_specs=out_specs, check_vma=False)
```

```python
import numpy as np
import ml_dtypes

import jax
import jax.numpy as jnp
from jax import lax
from jax.experimental import pallas as pl
from jax.experimental.pallas import tpu as pltpu
from jax.sharding import PartitionSpec as P

BF16 = jnp.bfloat16
F32 = jnp.float32

SEQ = 16
CHAN = 8
TOKENS = 2048
ROWS = 128
COLS = 512
LANE = 32
NEAR = 4
FAR = SEQ // NEAR
HALF = 33
MID = 72
BACK = 80
VMEM_LIMIT = 48 * 1024 * 1024
WIDE = 16
GROUP = 11


def device(seq_at, chan_at):
    return seq_at * CHAN + chan_at


def swap_pairs():
    pairs = []
    for seq_at in range(SEQ):
        for chan_at in range(CHAN):
            a, i = divmod(seq_at, NEAR)
            b, p = divmod(chan_at, CHAN // FAR)
            pairs.append(
                (device(seq_at, chan_at), device(b * NEAR + i, a * (CHAN // FAR) + p))
            )
    return pairs


def swapped(array):
    return lax.ppermute(array, ("seq", "chan"), swap_pairs())


def near_pairs(step):
    return [(i, i ^ step) for i in range(SEQ)]


def chan_pairs(step):
    return [(i, i ^ step) for i in range(CHAN)]


def exchange(array, axis):
    return lax.all_to_all(array, axis, 0, 0, tiled=True)


def thrice(table):
    high = table.astype(ml_dtypes.bfloat16)
    low = (table - high.astype(np.float64)).astype(ml_dtypes.bfloat16)
    return np.concatenate([high, high, low], axis=-1)


def tables():
    n1 = np.arange(32)
    n2 = np.arange(64)
    k1 = np.arange(HALF)
    k2 = np.arange(64)
    time = 64 * n1[None, None, :] + n2[:, None, None]
    outer = 2.0 * np.pi / 4096.0 * ((time * k1[None, :, None]) % 4096)
    inner = 2.0 * np.pi / 64.0 * ((k2[:, None] * n2[None, :]) % 64)
    weight = np.where((k1 == 0) | (k1 == 32), 1.0, 2.0)[None, :, None] / 4096.0
    first = np.zeros((64, MID, 32))
    first[:, :HALF] = np.cos(outer)
    first[:, HALF : 2 * HALF] = -np.sin(outer)
    last = np.zeros((64, 32, BACK))
    last[:, :, 0 : 2 * HALF : 2] = (np.cos(outer) * weight).transpose(0, 2, 1)
    last[:, :, 1 : 2 * HALF : 2] = (-np.sin(outer) * weight).transpose(0, 2, 1)
    cos, sin = np.cos(inner), np.sin(inner)
    ahead = np.block([[cos, sin], [-sin, cos]])
    return thrice(first), thrice(ahead), thrice(ahead.T), thrice(last)


def pieces(array):
    high = array.astype(BF16)
    low = (array - high.astype(F32)).astype(BF16)
    return jnp.concatenate([high, low, high], axis=0)


def matmul(left, right):
    return jnp.dot(left, right, preferred_element_type=F32)


def every(count, width, step):
    def body(block, carry):
        for at in range(width):
            step(block * width + at)
        return carry

    lax.fori_loop(0, count // width, body, 0)


def lanes_of(rows):
    return lax.broadcasted_iota(jnp.int32, (rows, 4 * LANE), 1)


def ahead_rows(mid_ref, first):
    return jnp.concatenate(
        [
            jnp.concatenate(
                [
                    mid_ref[pl.ds(first + at, 64, stride=MID), :],
                    mid_ref[pl.ds(HALF + first + at, 64, stride=MID), :],
                ],
                axis=0,
            )
            for at in range(GROUP)
        ],
        axis=1,
    )


def behind_rows(back_ref, first, behind_ref, products):
    found = matmul(behind_ref[...], pieces(jnp.concatenate(products, axis=1)))
    for at in range(GROUP):
        back_ref[pl.ds(pl.multiple_of((first + at) * 128, 128), 128), :] = found[
            :, at * 128 : (at + 1) * 128
        ]


def started(source, target, sem):
    copy = pltpu.make_async_copy(source, target, sem)
    copy.start()
    return copy


def forward_kernel(
    signal_ref, taps_ref, first_hbm, ahead_hbm, behind_hbm, last_hbm,
    gated_ref, kept_hbm, spec_hbm,
    wide_ref, mid_ref, back_ref, column_ref,
    first_ref, ahead_ref, behind_ref, last_ref, kept_ref, spec_ref, sems,
):
    first_copy = started(first_hbm, first_ref, sems.at[0])
    ahead_copy = started(ahead_hbm, ahead_ref, sems.at[1])
    behind_copy = started(behind_hbm, behind_ref, sems.at[2])
    last_copy = started(last_hbm, last_ref, sems.at[3])
    wide_ref[0:8, :] = jnp.zeros((8, 4 * LANE), F32)
    wide_ref[8:, :] = signal_ref[...].astype(F32)
    back_ref[2 * HALF * 64 :, :] = jnp.zeros(((BACK - 2 * HALF) * 64, 4 * LANE), F32)
    lane = lanes_of(32)
    tap0, tap1, tap2 = (jnp.broadcast_to(taps_ref[j : j + 1, :], (32, 4 * LANE)) for j in range(3))

    def outer(n2):
        now = wide_ref[pl.ds(n2 + 8, 32, stride=64), :]
        before = wide_ref[pl.ds(n2 + 7, 32, stride=64), :]
        earlier = wide_ref[pl.ds(n2 + 6, 32, stride=64), :]
        mixed = tap0 * now + tap1 * before + tap2 * earlier
        kept_ref[pl.ds(n2, 32, stride=64), :] = mixed
        carried = mixed * pltpu.roll(mixed, LANE, 1)
        data = jnp.where((lane >= 2 * LANE) & (lane < 3 * LANE), carried, mixed)
        mid_ref[pl.ds(pl.multiple_of(n2 * MID, 8), MID), :] = matmul(first_ref[n2], pieces(data))

    first_copy.wait()
    every(64, WIDE, outer)

    def inner(group):
        spec = matmul(ahead_ref[...], pieces(ahead_rows(mid_ref, group * GROUP)))
        products = []
        for at in range(GROUP):
            one = spec[:, at * 128 : (at + 1) * 128]
            spec_ref[group * GROUP + at] = one
            other = pltpu.roll(one, 3 * LANE, 1)
            re, im, other_re, other_im = one[:64], one[64:], other[:64], other[64:]
            products.append(
                jnp.concatenate(
                    [re * other_re - im * other_im, re * other_im + im * other_re], axis=0
                )
            )
        behind_rows(back_ref, group * GROUP, behind_ref, products)

    ahead_copy.wait()
    behind_copy.wait()
    every(HALF // GROUP, 1, inner)
    spec_copy = started(spec_ref, spec_hbm, sems.at[4])

    def final(n2):
        conv = matmul(last_ref[n2], pieces(back_ref[pl.ds(n2, BACK, stride=64), :]))
        mixed = kept_ref[pl.ds(n2, 32, stride=64), :]
        column_ref[pl.ds(n2, 32, stride=64), :] = mixed * pltpu.roll(conv, 2 * LANE, 1)
        kept_ref[pl.ds(n2, 32, stride=64), :] = jnp.where(
            lane < 3 * LANE, mixed, pltpu.roll(conv, LANE, 1)
        )

    last_copy.wait()
    every(64, WIDE, final)
    kept_copy = started(kept_ref, kept_hbm, sems.at[5])

    for block in range(SEQ):
        a, i = divmod(block, NEAR)
        turned = column_ref[block * ROWS : (block + 1) * ROWS, :].T
        gated_ref[i, :, a * ROWS : (a + 1) * ROWS] = turned[:LANE].astype(BF16)
    spec_copy.wait()
    kept_copy.wait()


def backward_kernel(
    share_ref, kept_hbm, spec_hbm, taps_ref, first_hbm, ahead_hbm, behind_hbm, last_hbm,
    out_ref,
    grad_ref, mid_ref, back_ref, column_ref,
    first_ref, ahead_ref, behind_ref, last_ref, kept_ref, spec_ref, sems,
):
    first_copy = started(first_hbm, first_ref, sems.at[0])
    kept_copy = started(kept_hbm, kept_ref, sems.at[5])
    ahead_copy = started(ahead_hbm, ahead_ref, sems.at[1])
    behind_copy = started(behind_hbm, behind_ref, sems.at[2])
    spec_copy = started(spec_hbm, spec_ref, sems.at[4])
    last_copy = started(last_hbm, last_ref, sems.at[3])
    back_ref[2 * HALF * 64 :, :] = jnp.zeros(((BACK - 2 * HALF) * 64, 4 * LANE), F32)
    column_ref[TOKENS:, :] = jnp.zeros((8, 4 * LANE), F32)
    for i in range(NEAR):
        total = share_ref[i].astype(F32)
        for far in range(1, FAR):
            total = total + share_ref[far * NEAR + i].astype(F32)
        for a in range(FAR):
            block = a * NEAR + i
            part = total[:, a * ROWS : (a + 1) * ROWS]
            grad_ref[block * ROWS : (block + 1) * ROWS, :] = jnp.concatenate([part] * 4, axis=0).T
    lane = lanes_of(32)

    def outer(n2):
        kept = kept_ref[pl.ds(n2, 32, stride=64), :]
        query = jnp.where(lane < 3 * LANE, pltpu.roll(kept, 2 * LANE, 1), pltpu.roll(kept, 3 * LANE, 1))
        data = grad_ref[pl.ds(n2, 32, stride=64), :] * query
        mid_ref[pl.ds(pl.multiple_of(n2 * MID, 8), MID), :] = matmul(first_ref[n2], pieces(data))

    first_copy.wait()
    kept_copy.wait()
    every(64, WIDE, outer)

    wide = lanes_of(128)

    def inner(group):
        grad = matmul(ahead_ref[...], pieces(ahead_rows(mid_ref, group * GROUP)))
        products = []
        for at in range(GROUP):
            one = grad[:, at * 128 : (at + 1) * 128]
            spec = spec_ref[group * GROUP + at]
            other = jnp.where(
                wide < 3 * LANE, pltpu.roll(spec, 3 * LANE, 1), pltpu.roll(spec, LANE, 1)
            )
            re, im, other_re, other_im = one[:64], one[64:], other[:64], other[64:]
            products.append(
                jnp.concatenate(
                    [other_re * re + other_im * im, other_re * im - other_im * re], axis=0
                )
            )
        behind_rows(back_ref, group * GROUP, behind_ref, products)

    ahead_copy.wait()
    behind_copy.wait()
    spec_copy.wait()
    every(HALF // GROUP, 1, inner)

    def final(n2):
        found = matmul(last_ref[n2], pieces(back_ref[pl.ds(n2, BACK, stride=64), :]))
        kept = kept_ref[pl.ds(n2, 32, stride=64), :]
        grad = grad_ref[pl.ds(n2, 32, stride=64), :]
        up, down = pltpu.roll(kept, LANE, 1), pltpu.roll(kept, 3 * LANE, 1)
        mixed = jnp.where(
            lane < LANE,
            grad * up,
            jnp.where(
                lane < 2 * LANE,
                pltpu.roll(found, 3 * LANE, 1) * down,
                jnp.where(lane < 3 * LANE, found * up, found),
            ),
        )
        column_ref[pl.ds(n2, 32, stride=64), :] = mixed

    last_copy.wait()
    every(64, WIDE, final)

    tap0, tap1, tap2 = (
        jnp.broadcast_to(taps_ref[j : j + 1, :], (ROWS, 4 * LANE)) for j in range(3)
    )
    for block in range(SEQ):
        low = block * ROWS
        out_ref[block] = (
            tap0 * column_ref[low : low + ROWS, :]
            + tap1 * column_ref[low + 1 : low + 1 + ROWS, :]
            + tap2 * column_ref[low + 2 : low + 2 + ROWS, :]
        ).astype(BF16)


LONG = pl.CostEstimate(flops=8_000_000_000, transcendentals=0, bytes_accessed=6_000_000)


def whole(shape):
    return pl.BlockSpec(shape, lambda _: (0,) * len(shape))


HELD = (
    pltpu.VMEM((64, MID, 96), BF16),
    pltpu.VMEM((128, 384), BF16),
    pltpu.VMEM((128, 384), BF16),
    pltpu.VMEM((64, 32, 3 * BACK), BF16),
    pltpu.VMEM((TOKENS, 4 * LANE), F32),
    pltpu.VMEM((HALF, 128, 4 * LANE), F32),
    pltpu.SemaphoreType.DMA((6,)),
)
FAR_OFF = pl.BlockSpec(memory_space=pltpu.HBM)


def resident(array):
    return pltpu.with_memory_space_constraint(array, pltpu.HBM)


def convolve(signals, taps, consts, interpret=False):
    return pl.pallas_call(
        forward_kernel,
        out_shape=(
            jax.ShapeDtypeStruct((NEAR, LANE, FAR * ROWS), BF16),
            pltpu.HBM((TOKENS, 4 * LANE), F32),
            pltpu.HBM((HALF, 128, 4 * LANE), F32),
        ),
        grid=(1,),
        in_specs=[whole(signals.shape), whole(taps.shape)] + [FAR_OFF] * 4,
        out_specs=(whole((NEAR, LANE, FAR * ROWS)), FAR_OFF, FAR_OFF),
        scratch_shapes=[
            pltpu.VMEM((TOKENS + 8, 4 * LANE), F32),
            pltpu.VMEM((64 * MID, 4 * LANE), F32),
            pltpu.VMEM((64 * BACK, 4 * LANE), F32),
            pltpu.VMEM((TOKENS, 4 * LANE), F32),
            *HELD,
        ],
        compiler_params=pltpu.CompilerParams(vmem_limit_bytes=VMEM_LIMIT),
        cost_estimate=LONG,
        interpret=interpret,
        name="convolve",
    )(signals, taps, *(resident(x) for x in consts))


def correlate(shares, kept, spec, taps, consts, interpret=False):
    half = pl.BlockSpec((SEQ, LANE, FAR * ROWS), lambda _: (0, 1, 0))
    return pl.pallas_call(
        backward_kernel,
        out_shape=jax.ShapeDtypeStruct((SEQ, ROWS, 4 * LANE), BF16),
        grid=(1,),
        in_specs=[half, FAR_OFF, FAR_OFF, whole(taps.shape)] + [FAR_OFF] * 4,
        out_specs=whole((SEQ, ROWS, 4 * LANE)),
        scratch_shapes=[
            pltpu.VMEM((TOKENS, 4 * LANE), F32),
            pltpu.VMEM((64 * MID, 4 * LANE), F32),
            pltpu.VMEM((64 * BACK, 4 * LANE), F32),
            pltpu.VMEM((TOKENS + 8, 4 * LANE), F32),
            *HELD,
        ],
        compiler_params=pltpu.CompilerParams(vmem_limit_bytes=VMEM_LIMIT),
        cost_estimate=LONG,
        interpret=interpret,
        name="correlate",
    )(shares, resident(kept), resident(spec), taps, *(resident(x) for x in consts))


def pack_kernel(streams_ref, filter_ref, out_ref):
    lane = lanes_of(ROWS)
    for column in range(COLS // 128):
        at = slice(column * 128, (column + 1) * 128)
        blocks = [streams_ref[j, :, at].astype(F32) for j in range(3)] + [filter_ref[:, at]]
        for part in range(4):
            placed = [pltpu.roll(b, ((j - part) % 4) * LANE, 1) if j != part else b
                      for j, b in enumerate(blocks)]
            joined = placed[3]
            for j in range(2, -1, -1):
                joined = jnp.where(lane < (j + 1) * LANE, placed[j], joined)
            out_ref[column * 4 + part] = joined.astype(BF16)


def unpack_kernel(got_ref, streams_ref, filter_ref):
    lane = lanes_of(ROWS)
    for column in range(COLS // 128):
        at = slice(column * 128, (column + 1) * 128)
        blocks = [got_ref[column * 4 + part].astype(F32) for part in range(4)]
        for j in range(4):
            placed = [pltpu.roll(b, ((part - j) % 4) * LANE, 1) if j != part else b
                      for part, b in enumerate(blocks)]
            joined = placed[3]
            for part in range(2, -1, -1):
                joined = jnp.where(lane < (part + 1) * LANE, placed[part], joined)
            if j < 3:
                streams_ref[j, :, at] = joined.astype(BF16)
            else:
                filter_ref[:, at] = joined


def contract(left, right, left_dim, right_dim):
    return lax.dot_general(
        left, right, (((left_dim,), (right_dim,)), ((), ())), preferred_element_type=F32
    )


def fetch(place_ref, refs, weights, cots, sems):
    copies = []
    for step in range(NEAR):
        low = pl.multiple_of((place_ref[0] ^ step) * 256, 256)
        copies.append(started(refs[step], weights.at[:, pl.ds(low, 256)], sems.at[step]))
    for far in range(FAR):
        row = pl.multiple_of((place_ref[1] ^ far) * ROWS, ROWS)
        for side in range(2):
            low = pl.multiple_of((place_ref[2] ^ side) * COLS, COLS)
            copies.append(
                started(
                    refs[NEAR + far].at[side],
                    cots.at[pl.ds(row, ROWS), pl.ds(low, COLS)],
                    sems.at[NEAR + 2 * far + side],
                )
            )
    return copies


def send_kernel(place_ref, gated_ref, *refs):
    sent_ref, weights, cots, sems = refs[NEAR + FAR :]
    copies = fetch(place_ref, refs, weights, cots, sems)
    for s in range(SEQ):
        sent_ref[s, :LANE, :] = gated_ref[s % NEAR]
    for copy in copies:
        copy.wait()
    total = contract(weights[...], cots[...], 1, 1).astype(BF16)
    for s in range(SEQ):
        sent_ref[s, LANE:, :] = total[s * LANE : (s + 1) * LANE]


def product_kernel(place_ref, got_ref, *refs):
    out_ref, *grad_refs = refs[NEAR + FAR : NEAR + FAR + 1 + NEAR]
    weights, cots, sems = refs[NEAR + FAR + 1 + NEAR :]
    copies = fetch(place_ref, refs, weights, cots, sems)
    turned = got_ref[...].reshape(COLS, FAR * ROWS).T
    for copy in copies:
        copy.wait()
    for side in range(2):
        part = contract(turned, weights[:, side * COLS : (side + 1) * COLS], 1, 0).astype(BF16)
        for a in range(FAR):
            out_ref[2 * a + side] = part[a * ROWS : (a + 1) * ROWS]
    gated = got_ref[...].reshape(COLS, FAR * ROWS)
    for step in range(NEAR):
        low = pl.multiple_of((place_ref[0] ^ step) * 256, 256)
        grad = contract(gated, cots[:, pl.ds(low, 256)], 1, 0)
        grad_refs[step][...] = grad.astype(grad_refs[step].dtype)


def call(kernel, name, out_shape, interpret, *inputs, specs=None, scratch=()):
    many = isinstance(out_shape, tuple)
    outs = out_shape if many else (out_shape,)
    in_specs = [whole(x.shape) for x in inputs]
    for at, spec in (specs or {}).items():
        in_specs[at] = spec
    out_specs = tuple(whole(x.shape) for x in outs)
    return pl.pallas_call(
        kernel,
        out_shape=out_shape,
        grid=(1,),
        in_specs=in_specs,
        out_specs=out_specs if many else out_specs[0],
        scratch_shapes=list(scratch),
        compiler_params=pltpu.CompilerParams(vmem_limit_bytes=VMEM_LIMIT),
        cost_estimate=pl.CostEstimate(flops=1_000_000_000, transcendentals=0, bytes_accessed=2_000_000),
        interpret=interpret,
        name=name,
    )(*inputs)


SCALAR = pl.BlockSpec(memory_space=pltpu.SMEM)


def pack(streams, long_filter, interpret=False):
    shape = jax.ShapeDtypeStruct((SEQ, ROWS, 4 * LANE), BF16)
    return call(
        pack_kernel, "pack", shape, interpret, resident(streams), resident(long_filter)
    )


def unpack(got, interpret=False):
    shapes = (
        jax.ShapeDtypeStruct((3, ROWS, COLS), BF16),
        jax.ShapeDtypeStruct((ROWS, COLS), F32),
    )
    return call(unpack_kernel, "unpack", shapes, interpret, got)


def far_off(low, high):
    return {at: FAR_OFF for at in range(low, high)}


GATHERED = (
    pltpu.VMEM((COLS, 2 * COLS), BF16),
    pltpu.VMEM((FAR * ROWS, 2 * COLS), BF16),
    pltpu.SemaphoreType.DMA((NEAR + 2 * FAR,)),
)


def to_send(place, gated, weights, cots, interpret=False):
    shape = jax.ShapeDtypeStruct((SEQ, 2 * LANE, FAR * ROWS), BF16)
    return call(
        send_kernel, "send", shape, interpret, place, gated, *weights, *cots,
        specs={0: SCALAR, **far_off(2, 2 + NEAR + FAR)}, scratch=GATHERED,
    )


def products(place, got, weights, cots, interpret=False):
    width = weights[0].shape[1]
    shapes = (pltpu.HBM((CHAN, ROWS, COLS), BF16),) + tuple(
        pltpu.HBM((COLS, width), BF16 if step else F32) for step in range(NEAR)
    )
    half = pl.BlockSpec((SEQ, LANE, FAR * ROWS), lambda _: (0, 0, 0))
    return call(
        product_kernel, "products", shapes, interpret, place, got, *weights, *cots,
        specs={0: SCALAR, 1: half, **far_off(2, 2 + NEAR + FAR)}, scratch=GATHERED,
    )


def shards(projected, short_filter, long_filter, w_out, d_out):
    seq_at = lax.axis_index("seq")
    chan_at = lax.axis_index("chan")
    place = jnp.stack([seq_at % NEAR, chan_at // 2, chan_at % 2]).astype(jnp.int32)
    consts = [jnp.asarray(table) for table in tables()]

    packed = pack(projected.transpose(1, 0, 2), long_filter)
    moved = swapped(d_out)
    signals = exchange(packed, "seq")
    pair = jnp.stack([moved, lax.ppermute(moved, "chan", chan_pairs(1))])
    pair, late = lax.optimization_barrier((pair, w_out))
    cots = [pair] + [lax.ppermute(pair, "chan", chan_pairs(2 * far)) for far in range(1, FAR)]
    weights = [late] + [lax.ppermute(late, "seq", near_pairs(step)) for step in range(1, NEAR)]

    own = lax.dynamic_slice_in_dim(short_filter, seq_at * LANE, LANE, axis=2).reshape(3, 3 * LANE)
    plain = jnp.zeros((3, LANE), F32).at[0].set(1.0)
    taps = jnp.concatenate([own, plain], axis=1)

    gated, kept, spec = convolve(signals.reshape(TOKENS, 4 * LANE), taps, consts)
    got = exchange(to_send(place, gated, weights, cots), "seq")

    partial_out, d_wout, *others = products(place, got, weights, cots)
    shares = exchange(partial_out, "chan")
    output = swapped(jnp.sum(shares.astype(F32), axis=0).astype(BF16))
    for step, piece in enumerate(others, 1):
        d_wout = d_wout + lax.ppermute(piece, "seq", near_pairs(step)).astype(F32)

    returned = exchange(correlate(got, kept, spec, taps, consts), "seq")
    d_projected, d_filter = unpack(returned)
    return (output, d_projected.transpose(1, 0, 2), d_wout, d_filter)


def solution(mesh):
    in_specs = (
        P("seq", None, "chan"),
        P(None, None, "chan"),
        P("seq", "chan"),
        P("chan", "seq"),
        P("seq", "chan"),
    )
    out_specs = (P("seq", "chan"), P("seq", None, "chan"), P("chan", "seq"), P("seq", "chan"))
    return jax.shard_map(shards, mesh=mesh, in_specs=in_specs, out_specs=out_specs, check_vma=False)
```

```python
import numpy as np
import ml_dtypes

import jax
import jax.numpy as jnp
from jax import lax
from jax.experimental import pallas as pl
from jax.experimental.pallas import tpu as pltpu
from jax.sharding import PartitionSpec as P

BF16 = jnp.bfloat16
F32 = jnp.float32

SEQ = 16
CHAN = 8
TOKENS = 2048
ROWS = 128
COLS = 512
LANE = 32
NEAR = 4
FAR = SEQ // NEAR
HALF = 33
MID = 72
BACK = 80
VMEM_LIMIT = 48 * 1024 * 1024
WIDE = 16
GROUP = 11


def device(seq_at, chan_at):
    return seq_at * CHAN + chan_at


def swap_pairs():
    pairs = []
    for seq_at in range(SEQ):
        for chan_at in range(CHAN):
            a, i = divmod(seq_at, NEAR)
            b, p = divmod(chan_at, CHAN // FAR)
            pairs.append(
                (device(seq_at, chan_at), device(b * NEAR + i, a * (CHAN // FAR) + p))
            )
    return pairs


def swapped(array):
    return lax.ppermute(array, ("seq", "chan"), swap_pairs())


def near_pairs(step):
    return [(i, i ^ step) for i in range(SEQ)]


def chan_pairs(step):
    return [(i, i ^ step) for i in range(CHAN)]


def exchange(array, axis):
    return lax.all_to_all(array, axis, 0, 0, tiled=True)


def thrice(table):
    high = table.astype(ml_dtypes.bfloat16)
    low = (table - high.astype(np.float64)).astype(ml_dtypes.bfloat16)
    return np.concatenate([high, high, low], axis=-1)


def tables():
    n1 = np.arange(32)
    n2 = np.arange(64)
    k1 = np.arange(HALF)
    k2 = np.arange(64)
    time = 64 * n1[None, None, :] + n2[:, None, None]
    outer = 2.0 * np.pi / 4096.0 * ((time * k1[None, :, None]) % 4096)
    inner = 2.0 * np.pi / 64.0 * ((k2[:, None] * n2[None, :]) % 64)
    weight = np.where((k1 == 0) | (k1 == 32), 1.0, 2.0)[None, :, None] / 4096.0
    first = np.zeros((64, MID, 32))
    first[:, :HALF] = np.cos(outer)
    first[:, HALF : 2 * HALF] = -np.sin(outer)
    last = np.zeros((64, 32, BACK))
    last[:, :, 0 : 2 * HALF : 2] = (np.cos(outer) * weight).transpose(0, 2, 1)
    last[:, :, 1 : 2 * HALF : 2] = (-np.sin(outer) * weight).transpose(0, 2, 1)
    cos, sin = np.cos(inner), np.sin(inner)
    ahead = np.block([[cos, sin], [-sin, cos]])
    return thrice(first), thrice(ahead), thrice(ahead.T), thrice(last)


def pieces(array):
    high = array.astype(BF16)
    low = (array - high.astype(F32)).astype(BF16)
    return jnp.concatenate([high, low, high], axis=0)


def matmul(left, right):
    return jnp.dot(left, right, preferred_element_type=F32)


def every(count, width, step):
    def body(block, carry):
        for at in range(width):
            step(block * width + at)
        return carry

    lax.fori_loop(0, count // width, body, 0)


def column_rows(n2):
    return pl.ds(pl.multiple_of(n2 * 32, 32), 32)


def lanes_of(rows):
    return lax.broadcasted_iota(jnp.int32, (rows, 4 * LANE), 1)


def ahead_rows(mid_ref, first):
    return jnp.concatenate(
        [
            jnp.concatenate(
                [
                    mid_ref[pl.ds(first + at, 64, stride=MID), :],
                    mid_ref[pl.ds(HALF + first + at, 64, stride=MID), :],
                ],
                axis=0,
            )
            for at in range(GROUP)
        ],
        axis=1,
    )


def behind_rows(back_ref, first, behind_ref, products):
    found = matmul(behind_ref[...], pieces(jnp.concatenate(products, axis=1)))
    for at in range(GROUP):
        back_ref[pl.ds(pl.multiple_of((first + at) * 128, 128), 128), :] = found[
            :, at * 128 : (at + 1) * 128
        ]


def started(source, target, sem):
    copy = pltpu.make_async_copy(source, target, sem)
    copy.start()
    return copy


def forward_kernel(
    signal_ref, taps_ref, first_hbm, ahead_hbm, behind_hbm, last_hbm,
    gated_ref, kept_hbm, spec_hbm,
    wide_ref, mid_ref, back_ref, column_ref,
    first_ref, ahead_ref, behind_ref, last_ref, kept_ref, spec_ref, sems,
):
    first_copy = started(first_hbm, first_ref, sems.at[0])
    ahead_copy = started(ahead_hbm, ahead_ref, sems.at[1])
    behind_copy = started(behind_hbm, behind_ref, sems.at[2])
    last_copy = started(last_hbm, last_ref, sems.at[3])
    wide_ref[0:8, :] = jnp.zeros((8, 4 * LANE), F32)
    wide_ref[8:, :] = signal_ref[...].astype(F32)
    back_ref[2 * HALF * 64 :, :] = jnp.zeros(((BACK - 2 * HALF) * 64, 4 * LANE), F32)
    lane = lanes_of(32)
    tap0, tap1, tap2 = (jnp.broadcast_to(taps_ref[j : j + 1, :], (32, 4 * LANE)) for j in range(3))

    def outer(n2):
        now = wide_ref[pl.ds(n2 + 8, 32, stride=64), :]
        before = wide_ref[pl.ds(n2 + 7, 32, stride=64), :]
        earlier = wide_ref[pl.ds(n2 + 6, 32, stride=64), :]
        mixed = tap0 * now + tap1 * before + tap2 * earlier
        kept_ref[column_rows(n2), :] = mixed
        carried = mixed * pltpu.roll(mixed, LANE, 1)
        data = jnp.where((lane >= 2 * LANE) & (lane < 3 * LANE), carried, mixed)
        mid_ref[pl.ds(pl.multiple_of(n2 * MID, 8), MID), :] = matmul(first_ref[n2], pieces(data))

    first_copy.wait()
    every(64, WIDE, outer)

    def inner(group):
        spec = matmul(ahead_ref[...], pieces(ahead_rows(mid_ref, group * GROUP)))
        products = []
        for at in range(GROUP):
            one = spec[:, at * 128 : (at + 1) * 128]
            spec_ref[group * GROUP + at] = one
            other = pltpu.roll(one, 3 * LANE, 1)
            re, im, other_re, other_im = one[:64], one[64:], other[:64], other[64:]
            products.append(
                jnp.concatenate(
                    [re * other_re - im * other_im, re * other_im + im * other_re], axis=0
                )
            )
        behind_rows(back_ref, group * GROUP, behind_ref, products)

    ahead_copy.wait()
    behind_copy.wait()
    every(HALF // GROUP, 1, inner)
    spec_copy = started(spec_ref, spec_hbm, sems.at[4])

    def final(n2):
        conv = matmul(last_ref[n2], pieces(back_ref[pl.ds(n2, BACK, stride=64), :]))
        mixed = kept_ref[column_rows(n2), :]
        column_ref[pl.ds(n2, 32, stride=64), :] = mixed * pltpu.roll(conv, 2 * LANE, 1)
        kept_ref[column_rows(n2), :] = jnp.where(
            lane < 3 * LANE, mixed, pltpu.roll(conv, LANE, 1)
        )

    last_copy.wait()

    def block_of(block, carry):
        for at in range(WIDE):
            final(block * WIDE + at)
        rows = pl.ds(pl.multiple_of(block * WIDE * 32, 32), WIDE * 32)
        started(kept_ref.at[rows], kept_hbm.at[rows], sems.at[5])
        return carry

    lax.fori_loop(0, 64 // WIDE, block_of, 0)
    kept_copy = pltpu.make_async_copy(kept_ref, kept_hbm, sems.at[5])

    for block in range(SEQ):
        a, i = divmod(block, NEAR)
        turned = column_ref[block * ROWS : (block + 1) * ROWS, :].T
        gated_ref[i, :, a * ROWS : (a + 1) * ROWS] = turned[:LANE].astype(BF16)
    spec_copy.wait()
    kept_copy.wait()


def backward_kernel(
    share_ref, kept_hbm, spec_hbm, taps_ref, first_hbm, ahead_hbm, behind_hbm, last_hbm,
    out_ref,
    grad_ref, mid_ref, back_ref, column_ref,
    first_ref, ahead_ref, behind_ref, last_ref, kept_ref, spec_ref, sems,
):
    first_copy = started(first_hbm, first_ref, sems.at[0])
    kept_copy = started(kept_hbm, kept_ref, sems.at[5])
    ahead_copy = started(ahead_hbm, ahead_ref, sems.at[1])
    behind_copy = started(behind_hbm, behind_ref, sems.at[2])
    spec_copy = started(spec_hbm, spec_ref, sems.at[4])
    last_copy = started(last_hbm, last_ref, sems.at[3])
    back_ref[2 * HALF * 64 :, :] = jnp.zeros(((BACK - 2 * HALF) * 64, 4 * LANE), F32)
    column_ref[TOKENS:, :] = jnp.zeros((8, 4 * LANE), F32)
    for i in range(NEAR):
        total = share_ref[i].astype(F32)
        for far in range(1, FAR):
            total = total + share_ref[far * NEAR + i].astype(F32)
        for a in range(FAR):
            block = a * NEAR + i
            part = total[:, a * ROWS : (a + 1) * ROWS]
            grad_ref[block * ROWS : (block + 1) * ROWS, :] = jnp.concatenate([part] * 4, axis=0).T
    lane = lanes_of(32)

    def outer(n2):
        kept = kept_ref[column_rows(n2), :]
        query = jnp.where(lane < 3 * LANE, pltpu.roll(kept, 2 * LANE, 1), pltpu.roll(kept, 3 * LANE, 1))
        data = grad_ref[pl.ds(n2, 32, stride=64), :] * query
        mid_ref[pl.ds(pl.multiple_of(n2 * MID, 8), MID), :] = matmul(first_ref[n2], pieces(data))

    first_copy.wait()
    kept_copy.wait()
    every(64, WIDE, outer)

    wide = lanes_of(128)

    def inner(group):
        grad = matmul(ahead_ref[...], pieces(ahead_rows(mid_ref, group * GROUP)))
        products = []
        for at in range(GROUP):
            one = grad[:, at * 128 : (at + 1) * 128]
            spec = spec_ref[group * GROUP + at]
            other = jnp.where(
                wide < 3 * LANE, pltpu.roll(spec, 3 * LANE, 1), pltpu.roll(spec, LANE, 1)
            )
            re, im, other_re, other_im = one[:64], one[64:], other[:64], other[64:]
            products.append(
                jnp.concatenate(
                    [other_re * re + other_im * im, other_re * im - other_im * re], axis=0
                )
            )
        behind_rows(back_ref, group * GROUP, behind_ref, products)

    ahead_copy.wait()
    behind_copy.wait()
    spec_copy.wait()
    every(HALF // GROUP, 1, inner)

    def final(n2):
        found = matmul(last_ref[n2], pieces(back_ref[pl.ds(n2, BACK, stride=64), :]))
        kept = kept_ref[column_rows(n2), :]
        grad = grad_ref[pl.ds(n2, 32, stride=64), :]
        up, down = pltpu.roll(kept, LANE, 1), pltpu.roll(kept, 3 * LANE, 1)
        mixed = jnp.where(
            lane < LANE,
            grad * up,
            jnp.where(
                lane < 2 * LANE,
                pltpu.roll(found, 3 * LANE, 1) * down,
                jnp.where(lane < 3 * LANE, found * up, found),
            ),
        )
        column_ref[pl.ds(n2, 32, stride=64), :] = mixed

    last_copy.wait()
    every(64, WIDE, final)

    tap0, tap1, tap2 = (
        jnp.broadcast_to(taps_ref[j : j + 1, :], (ROWS, 4 * LANE)) for j in range(3)
    )
    for block in range(SEQ):
        low = block * ROWS
        out_ref[block] = (
            tap0 * column_ref[low : low + ROWS, :]
            + tap1 * column_ref[low + 1 : low + 1 + ROWS, :]
            + tap2 * column_ref[low + 2 : low + 2 + ROWS, :]
        ).astype(BF16)


LONG = pl.CostEstimate(flops=8_000_000_000, transcendentals=0, bytes_accessed=6_000_000)


def whole(shape):
    return pl.BlockSpec(shape, lambda _: (0,) * len(shape))


HELD = (
    pltpu.VMEM((64, MID, 96), BF16),
    pltpu.VMEM((128, 384), BF16),
    pltpu.VMEM((128, 384), BF16),
    pltpu.VMEM((64, 32, 3 * BACK), BF16),
    pltpu.VMEM((TOKENS, 4 * LANE), F32),
    pltpu.VMEM((HALF, 128, 4 * LANE), F32),
    pltpu.SemaphoreType.DMA((6,)),
)
FAR_OFF = pl.BlockSpec(memory_space=pltpu.HBM)


def resident(array):
    return pltpu.with_memory_space_constraint(array, pltpu.HBM)


def convolve(signals, taps, consts, interpret=False):
    return pl.pallas_call(
        forward_kernel,
        out_shape=(
            jax.ShapeDtypeStruct((NEAR, LANE, FAR * ROWS), BF16),
            pltpu.HBM((TOKENS, 4 * LANE), F32),
            pltpu.HBM((HALF, 128, 4 * LANE), F32),
        ),
        grid=(1,),
        in_specs=[whole(signals.shape), whole(taps.shape)] + [FAR_OFF] * 4,
        out_specs=(whole((NEAR, LANE, FAR * ROWS)), FAR_OFF, FAR_OFF),
        scratch_shapes=[
            pltpu.VMEM((TOKENS + 8, 4 * LANE), F32),
            pltpu.VMEM((64 * MID, 4 * LANE), F32),
            pltpu.VMEM((64 * BACK, 4 * LANE), F32),
            pltpu.VMEM((TOKENS, 4 * LANE), F32),
            *HELD,
        ],
        compiler_params=pltpu.CompilerParams(vmem_limit_bytes=VMEM_LIMIT),
        cost_estimate=LONG,
        interpret=interpret,
        name="convolve",
    )(signals, taps, *(resident(x) for x in consts))


def correlate(shares, kept, spec, taps, consts, interpret=False):
    half = pl.BlockSpec((SEQ, LANE, FAR * ROWS), lambda _: (0, 1, 0))
    return pl.pallas_call(
        backward_kernel,
        out_shape=jax.ShapeDtypeStruct((SEQ, ROWS, 4 * LANE), BF16),
        grid=(1,),
        in_specs=[half, FAR_OFF, FAR_OFF, whole(taps.shape)] + [FAR_OFF] * 4,
        out_specs=whole((SEQ, ROWS, 4 * LANE)),
        scratch_shapes=[
            pltpu.VMEM((TOKENS, 4 * LANE), F32),
            pltpu.VMEM((64 * MID, 4 * LANE), F32),
            pltpu.VMEM((64 * BACK, 4 * LANE), F32),
            pltpu.VMEM((TOKENS + 8, 4 * LANE), F32),
            *HELD,
        ],
        compiler_params=pltpu.CompilerParams(vmem_limit_bytes=VMEM_LIMIT),
        cost_estimate=LONG,
        interpret=interpret,
        name="correlate",
    )(shares, resident(kept), resident(spec), taps, *(resident(x) for x in consts))


def pack_kernel(streams_hbm, filter_hbm, out_hbm, streams_ref, filter_ref, out_ref, sems):
    lane = lanes_of(ROWS)
    columns = range(COLS // 128)
    spans = [slice(column * 128, (column + 1) * 128) for column in columns]
    arrivals = [
        (
            started(streams_hbm.at[:, :, span], streams_ref.at[column], sems.at[column]),
            started(filter_hbm.at[:, span], filter_ref.at[column], sems.at[4 + column]),
        )
        for column, span in zip(columns, spans)
    ]
    departures = []
    for column in columns:
        for copy in arrivals[column]:
            copy.wait()
        blocks = [streams_ref[column, j].astype(F32) for j in range(3)] + [filter_ref[column]]
        for part in range(4):
            placed = [pltpu.roll(b, ((j - part) % 4) * LANE, 1) if j != part else b
                      for j, b in enumerate(blocks)]
            joined = placed[3]
            for j in range(2, -1, -1):
                joined = jnp.where(lane < (j + 1) * LANE, placed[j], joined)
            out_ref[column * 4 + part] = joined.astype(BF16)
        part = slice(column * 4, column * 4 + 4)
        departures.append(started(out_ref.at[part], out_hbm.at[part], sems.at[8 + column]))
    for copy in departures:
        copy.wait()


def unpack_kernel(got_ref, streams_ref, filter_ref):
    lane = lanes_of(ROWS)
    for column in range(COLS // 128):
        at = slice(column * 128, (column + 1) * 128)
        blocks = [got_ref[column * 4 + part].astype(F32) for part in range(4)]
        for j in range(4):
            placed = [pltpu.roll(b, ((part - j) % 4) * LANE, 1) if j != part else b
                      for part, b in enumerate(blocks)]
            joined = placed[3]
            for part in range(2, -1, -1):
                joined = jnp.where(lane < (part + 1) * LANE, placed[part], joined)
            if j < 3:
                streams_ref[j, :, at] = joined.astype(BF16)
            else:
                filter_ref[:, at] = joined


def contract(left, right, left_dim, right_dim):
    return lax.dot_general(
        left, right, (((left_dim,), (right_dim,)), ((), ())), preferred_element_type=F32
    )


def fetch_weights(place_ref, refs, weights, sems):
    copies = []
    for step in range(NEAR):
        low = pl.multiple_of((place_ref[0] ^ step) * 256, 256)
        copies.append(started(refs[step], weights.at[:, pl.ds(low, 256)], sems.at[step]))
    return copies


def fetch_cots(place_ref, refs, cots, sems):
    copies = []
    for far in range(FAR):
        row = pl.multiple_of((place_ref[1] ^ far) * ROWS, ROWS)
        for side in range(2):
            low = pl.multiple_of((place_ref[2] ^ side) * COLS, COLS)
            copies.append(
                started(
                    refs[far].at[side],
                    cots.at[pl.ds(row, ROWS), pl.ds(low, COLS)],
                    sems.at[NEAR + 2 * far + side],
                )
            )
    return copies


def send_kernel(place_ref, gated_ref, *refs):
    sent_ref, weights, cots, sems = refs[NEAR + FAR :]
    copies = fetch_weights(place_ref, refs[:NEAR], weights, sems)
    copies += fetch_cots(place_ref, refs[NEAR : NEAR + FAR], cots, sems)
    for s in range(SEQ):
        sent_ref[s, :LANE, :] = gated_ref[s % NEAR]
    for copy in copies:
        copy.wait()
    total = contract(weights[...], cots[...], 1, 1).astype(BF16)
    for s in range(SEQ):
        sent_ref[s, LANE:, :] = total[s * LANE : (s + 1) * LANE]


def output_kernel(place_ref, got_ref, *refs):
    out_ref, weights, sems = refs[NEAR:]
    copies = fetch_weights(place_ref, refs[:NEAR], weights, sems)
    turned = got_ref[...].reshape(COLS, FAR * ROWS).T
    for copy in copies:
        copy.wait()
    for side in range(2):
        part = contract(turned, weights[:, side * COLS : (side + 1) * COLS], 1, 0).astype(BF16)
        for a in range(FAR):
            out_ref[2 * a + side] = part[a * ROWS : (a + 1) * ROWS]


def weight_kernel(place_ref, got_ref, *refs):
    grad_refs, (cots, sems) = refs[FAR : FAR + NEAR], refs[FAR + NEAR :]
    copies = fetch_cots(place_ref, refs[:FAR], cots, sems)
    gated = got_ref[...].reshape(COLS, FAR * ROWS)
    for copy in copies:
        copy.wait()
    for step in range(NEAR):
        low = pl.multiple_of((place_ref[0] ^ step) * 256, 256)
        grad = contract(gated, cots[:, pl.ds(low, 256)], 1, 0)
        grad_refs[step][...] = grad.astype(grad_refs[step].dtype)


def call(kernel, name, out_shape, interpret, *inputs, specs=None, scratch=()):
    many = isinstance(out_shape, tuple)
    outs = out_shape if many else (out_shape,)
    in_specs = [whole(x.shape) for x in inputs]
    for at, spec in (specs or {}).items():
        in_specs[at] = spec
    out_specs = tuple(whole(x.shape) for x in outs)
    return pl.pallas_call(
        kernel,
        out_shape=out_shape,
        grid=(1,),
        in_specs=in_specs,
        out_specs=out_specs if many else out_specs[0],
        scratch_shapes=list(scratch),
        compiler_params=pltpu.CompilerParams(vmem_limit_bytes=VMEM_LIMIT),
        cost_estimate=pl.CostEstimate(flops=1_000_000_000, transcendentals=0, bytes_accessed=2_000_000),
        interpret=interpret,
        name=name,
    )(*inputs)


SCALAR = pl.BlockSpec(memory_space=pltpu.SMEM)


def pack(streams, long_filter, interpret=False):
    return pl.pallas_call(
        pack_kernel,
        out_shape=pltpu.HBM((SEQ, ROWS, 4 * LANE), BF16),
        in_specs=[FAR_OFF, FAR_OFF],
        out_specs=FAR_OFF,
        scratch_shapes=[
            pltpu.VMEM((4, 3, ROWS, 128), BF16),
            pltpu.VMEM((4, ROWS, 128), F32),
            pltpu.VMEM((SEQ, ROWS, 4 * LANE), BF16),
            pltpu.SemaphoreType.DMA((12,)),
        ],
        compiler_params=pltpu.CompilerParams(vmem_limit_bytes=VMEM_LIMIT),
        interpret=interpret,
        name="pack",
    )(resident(streams), resident(long_filter))


def unpack(got, interpret=False):
    shapes = (
        jax.ShapeDtypeStruct((3, ROWS, COLS), BF16),
        jax.ShapeDtypeStruct((ROWS, COLS), F32),
    )
    return call(unpack_kernel, "unpack", shapes, interpret, got)


def far_off(low, high):
    return {at: FAR_OFF for at in range(low, high)}


GATHERED = (
    pltpu.VMEM((COLS, 2 * COLS), BF16),
    pltpu.VMEM((FAR * ROWS, 2 * COLS), BF16),
    pltpu.SemaphoreType.DMA((NEAR + 2 * FAR,)),
)


def to_send(place, gated, weights, cots, interpret=False):
    shape = jax.ShapeDtypeStruct((SEQ, 2 * LANE, FAR * ROWS), BF16)
    return call(
        send_kernel, "send", shape, interpret, place, gated, *weights, *cots,
        specs={0: SCALAR, **far_off(2, 2 + NEAR + FAR)}, scratch=GATHERED,
    )


GATED = pl.BlockSpec((SEQ, LANE, FAR * ROWS), lambda _: (0, 0, 0))


def output_shares(place, got, weights, interpret=False):
    return call(
        output_kernel, "outputs", pltpu.HBM((CHAN, ROWS, COLS), BF16), interpret,
        place, got, *weights, specs={0: SCALAR, 1: GATED, **far_off(2, 2 + NEAR)},
        scratch=(GATHERED[0], GATHERED[2]),
    )


def weight_shares(place, got, cots, width, interpret=False):
    shapes = tuple(pltpu.HBM((COLS, width), BF16 if step else F32) for step in range(NEAR))
    return call(
        weight_kernel, "weights", shapes, interpret, place, got, *cots,
        specs={0: SCALAR, 1: GATED, **far_off(2, 2 + FAR)}, scratch=GATHERED[1:],
    )


def shards(projected, short_filter, long_filter, w_out, d_out):
    seq_at = lax.axis_index("seq")
    chan_at = lax.axis_index("chan")
    place = jnp.stack([seq_at % NEAR, chan_at // 2, chan_at % 2]).astype(jnp.int32)
    consts = [jnp.asarray(table) for table in tables()]

    moved = swapped(d_out)
    signals = exchange(pack(projected.transpose(1, 0, 2), long_filter), "seq")
    pair = jnp.stack([moved, lax.ppermute(moved, "chan", chan_pairs(1))])
    cots = [pair] + [lax.ppermute(pair, "chan", chan_pairs(2 * far)) for far in range(1, FAR)]
    weights = [w_out] + [lax.ppermute(w_out, "seq", near_pairs(step)) for step in range(1, NEAR)]

    own = lax.dynamic_slice_in_dim(short_filter, seq_at * LANE, LANE, axis=2).reshape(3, 3 * LANE)
    plain = jnp.zeros((3, LANE), F32).at[0].set(1.0)
    taps = jnp.concatenate([own, plain], axis=1)

    gated, kept, spec = convolve(signals.reshape(TOKENS, 4 * LANE), taps, consts)
    got = exchange(to_send(place, gated, weights, cots), "seq")

    shares = exchange(output_shares(place, got, weights), "chan")
    d_wout, *others = weight_shares(place, got, cots, w_out.shape[1])
    output = swapped(jnp.sum(shares.astype(F32), axis=0).astype(BF16))
    for step, piece in enumerate(others, 1):
        d_wout = d_wout + lax.ppermute(piece, "seq", near_pairs(step)).astype(F32)

    returned = exchange(correlate(got, kept, spec, taps, consts), "seq")
    d_projected, d_filter = unpack(returned)
    return (output, d_projected.transpose(1, 0, 2), d_wout, d_filter)


def solution(mesh):
    in_specs = (
        P("seq", None, "chan"),
        P(None, None, "chan"),
        P("seq", "chan"),
        P("chan", "seq"),
        P("seq", "chan"),
    )
    out_specs = (P("seq", "chan"), P("seq", None, "chan"), P("chan", "seq"), P("seq", "chan"))
    return jax.shard_map(shards, mesh=mesh, in_specs=in_specs, out_specs=out_specs, check_vma=False)
```

```python
import numpy as np
import ml_dtypes

import jax
import jax.numpy as jnp
from jax import lax
from jax.experimental import pallas as pl
from jax.experimental.pallas import tpu as pltpu
from jax.sharding import PartitionSpec as P

BF16 = jnp.bfloat16
F32 = jnp.float32

SEQ = 16
CHAN = 8
TOKENS = 2048
ROWS = 128
COLS = 512
LANE = 32
NEAR = 4
FAR = SEQ // NEAR
HALF = 33
MID = 72
BACK = 80
VMEM_LIMIT = 48 * 1024 * 1024
WIDE = 16
GROUP = 33


def device(seq_at, chan_at):
    return seq_at * CHAN + chan_at


def swap_pairs():
    pairs = []
    for seq_at in range(SEQ):
        for chan_at in range(CHAN):
            a, i = divmod(seq_at, NEAR)
            b, p = divmod(chan_at, CHAN // FAR)
            pairs.append(
                (device(seq_at, chan_at), device(b * NEAR + i, a * (CHAN // FAR) + p))
            )
    return pairs


def swapped(array):
    return lax.ppermute(array, ("seq", "chan"), swap_pairs())


def near_pairs(step):
    return [(i, i ^ step) for i in range(SEQ)]


def chan_pairs(step):
    return [(i, i ^ step) for i in range(CHAN)]


def exchange(array, axis):
    return lax.all_to_all(array, axis, 0, 0, tiled=True)


def thrice(table):
    high = table.astype(ml_dtypes.bfloat16)
    low = (table - high.astype(np.float64)).astype(ml_dtypes.bfloat16)
    return np.concatenate([high, high, low], axis=-1)


def tables():
    n1 = np.arange(32)
    n2 = np.arange(64)
    k1 = np.arange(HALF)
    k2 = np.arange(64)
    time = 64 * n1[None, None, :] + n2[:, None, None]
    outer = 2.0 * np.pi / 4096.0 * ((time * k1[None, :, None]) % 4096)
    inner = 2.0 * np.pi / 64.0 * ((k2[:, None] * n2[None, :]) % 64)
    weight = np.where((k1 == 0) | (k1 == 32), 1.0, 2.0)[None, :, None] / 4096.0
    first = np.zeros((64, MID, 32))
    first[:, :HALF] = np.cos(outer)
    first[:, HALF : 2 * HALF] = -np.sin(outer)
    last = np.zeros((64, 32, BACK))
    last[:, :, 0 : 2 * HALF : 2] = (np.cos(outer) * weight).transpose(0, 2, 1)
    last[:, :, 1 : 2 * HALF : 2] = (-np.sin(outer) * weight).transpose(0, 2, 1)
    cos, sin = np.cos(inner), np.sin(inner)
    ahead = np.block([[cos, sin], [-sin, cos]])
    return thrice(first), thrice(ahead), thrice(ahead.T), thrice(last)


def pieces(array):
    high = array.astype(BF16)
    low = (array - high.astype(F32)).astype(BF16)
    return jnp.concatenate([high, low, high], axis=0)


def matmul(left, right):
    return jnp.dot(left, right, preferred_element_type=F32)


def every(count, width, step):
    def body(block, carry):
        for at in range(width):
            step(block * width + at)
        return carry

    lax.fori_loop(0, count // width, body, 0)


def column_rows(n2):
    return pl.ds(pl.multiple_of(n2 * 32, 32), 32)


def lanes_of(rows):
    return lax.broadcasted_iota(jnp.int32, (rows, 4 * LANE), 1)


def ahead_rows(mid_ref, first):
    return jnp.concatenate(
        [
            jnp.concatenate(
                [
                    mid_ref[pl.ds(first + at, 64, stride=MID), :],
                    mid_ref[pl.ds(HALF + first + at, 64, stride=MID), :],
                ],
                axis=0,
            )
            for at in range(GROUP)
        ],
        axis=1,
    )


def behind_rows(back_ref, first, behind_ref, products):
    found = matmul(behind_ref[...], pieces(jnp.concatenate(products, axis=1)))
    for at in range(GROUP):
        back_ref[pl.ds(pl.multiple_of((first + at) * 128, 128), 128), :] = found[
            :, at * 128 : (at + 1) * 128
        ]


def started(source, target, sem):
    copy = pltpu.make_async_copy(source, target, sem)
    copy.start()
    return copy


def forward_kernel(
    signal_ref, taps_ref, first_hbm, ahead_hbm, behind_hbm, last_hbm,
    gated_ref, kept_hbm, spec_hbm,
    wide_ref, mid_ref, back_ref, column_ref,
    first_ref, ahead_ref, behind_ref, last_ref, kept_ref, spec_ref, sems,
):
    first_copy = started(first_hbm, first_ref, sems.at[0])
    ahead_copy = started(ahead_hbm, ahead_ref, sems.at[1])
    behind_copy = started(behind_hbm, behind_ref, sems.at[2])
    last_copy = started(last_hbm, last_ref, sems.at[3])
    wide_ref[0:8, :] = jnp.zeros((8, 4 * LANE), F32)
    wide_ref[8:, :] = signal_ref[...].astype(F32)
    back_ref[2 * HALF * 64 :, :] = jnp.zeros(((BACK - 2 * HALF) * 64, 4 * LANE), F32)
    lane = lanes_of(32)
    tap0, tap1, tap2 = (jnp.broadcast_to(taps_ref[j : j + 1, :], (32, 4 * LANE)) for j in range(3))

    def outer(n2):
        now = wide_ref[pl.ds(n2 + 8, 32, stride=64), :]
        before = wide_ref[pl.ds(n2 + 7, 32, stride=64), :]
        earlier = wide_ref[pl.ds(n2 + 6, 32, stride=64), :]
        mixed = tap0 * now + tap1 * before + tap2 * earlier
        kept_ref[column_rows(n2), :] = mixed
        carried = mixed * pltpu.roll(mixed, LANE, 1)
        data = jnp.where((lane >= 2 * LANE) & (lane < 3 * LANE), carried, mixed)
        mid_ref[pl.ds(pl.multiple_of(n2 * MID, 8), MID), :] = matmul(first_ref[n2], pieces(data))

    first_copy.wait()
    every(64, WIDE, outer)

    def inner(group):
        spec = matmul(ahead_ref[...], pieces(ahead_rows(mid_ref, group * GROUP)))
        products = []
        for at in range(GROUP):
            one = spec[:, at * 128 : (at + 1) * 128]
            spec_ref[group * GROUP + at] = one
            other = pltpu.roll(one, 3 * LANE, 1)
            re, im, other_re, other_im = one[:64], one[64:], other[:64], other[64:]
            products.append(
                jnp.concatenate(
                    [re * other_re - im * other_im, re * other_im + im * other_re], axis=0
                )
            )
        behind_rows(back_ref, group * GROUP, behind_ref, products)

    ahead_copy.wait()
    behind_copy.wait()
    every(HALF // GROUP, 1, inner)
    spec_copy = started(spec_ref, spec_hbm, sems.at[4])

    def final(n2):
        conv = matmul(last_ref[n2], pieces(back_ref[pl.ds(n2, BACK, stride=64), :]))
        mixed = kept_ref[column_rows(n2), :]
        column_ref[pl.ds(n2, 32, stride=64), :] = mixed * pltpu.roll(conv, 2 * LANE, 1)
        kept_ref[column_rows(n2), :] = jnp.where(
            lane < 3 * LANE, mixed, pltpu.roll(conv, LANE, 1)
        )

    last_copy.wait()

    def block_of(block, carry):
        for at in range(WIDE):
            final(block * WIDE + at)
        rows = pl.ds(pl.multiple_of(block * WIDE * 32, 32), WIDE * 32)
        started(kept_ref.at[rows], kept_hbm.at[rows], sems.at[5])
        return carry

    lax.fori_loop(0, 64 // WIDE, block_of, 0)
    kept_copy = pltpu.make_async_copy(kept_ref, kept_hbm, sems.at[5])

    for block in range(SEQ):
        a, i = divmod(block, NEAR)
        turned = column_ref[block * ROWS : (block + 1) * ROWS, :].T
        gated_ref[i, :, a * ROWS : (a + 1) * ROWS] = turned[:LANE].astype(BF16)
    spec_copy.wait()
    kept_copy.wait()


def backward_kernel(
    share_ref, kept_hbm, spec_hbm, taps_ref, first_hbm, ahead_hbm, behind_hbm, last_hbm,
    out_ref,
    grad_ref, mid_ref, back_ref, column_ref, turned_ref,
    first_ref, ahead_ref, behind_ref, last_ref, kept_ref, spec_ref, sems,
):
    first_copy = started(first_hbm, first_ref, sems.at[0])
    kept_copy = started(kept_hbm, kept_ref, sems.at[5])
    ahead_copy = started(ahead_hbm, ahead_ref, sems.at[1])
    behind_copy = started(behind_hbm, behind_ref, sems.at[2])
    spec_copy = started(spec_hbm, spec_ref, sems.at[4])
    last_copy = started(last_hbm, last_ref, sems.at[3])
    back_ref[2 * HALF * 64 :, :] = jnp.zeros(((BACK - 2 * HALF) * 64, 4 * LANE), F32)
    column_ref[TOKENS:, :] = jnp.zeros((8, 4 * LANE), F32)
    for i in range(NEAR):
        total = share_ref[i].astype(F32)
        for far in range(1, FAR):
            total = total + share_ref[far * NEAR + i].astype(F32)
        for a in range(FAR):
            block = a * NEAR + i
            part = total[:, a * ROWS : (a + 1) * ROWS]
            grad_ref[block * ROWS : (block + 1) * ROWS, :] = jnp.concatenate([part] * 4, axis=0).T
    lane = lanes_of(32)

    def outer(n2):
        kept = kept_ref[column_rows(n2), :]
        query = jnp.where(lane < 3 * LANE, pltpu.roll(kept, 2 * LANE, 1), pltpu.roll(kept, 3 * LANE, 1))
        grad = grad_ref[pl.ds(n2, 32, stride=64), :]
        turned_ref[column_rows(n2), :] = grad
        data = grad * query
        mid_ref[pl.ds(pl.multiple_of(n2 * MID, 8), MID), :] = matmul(first_ref[n2], pieces(data))

    first_copy.wait()
    kept_copy.wait()
    every(64, WIDE, outer)

    wide = lanes_of(128)

    def inner(group):
        grad = matmul(ahead_ref[...], pieces(ahead_rows(mid_ref, group * GROUP)))
        products = []
        for at in range(GROUP):
            one = grad[:, at * 128 : (at + 1) * 128]
            spec = spec_ref[group * GROUP + at]
            other = jnp.where(
                wide < 3 * LANE, pltpu.roll(spec, 3 * LANE, 1), pltpu.roll(spec, LANE, 1)
            )
            re, im, other_re, other_im = one[:64], one[64:], other[:64], other[64:]
            products.append(
                jnp.concatenate(
                    [other_re * re + other_im * im, other_re * im - other_im * re], axis=0
                )
            )
        behind_rows(back_ref, group * GROUP, behind_ref, products)

    ahead_copy.wait()
    behind_copy.wait()
    spec_copy.wait()
    every(HALF // GROUP, 1, inner)

    def final(n2):
        found = matmul(last_ref[n2], pieces(back_ref[pl.ds(n2, BACK, stride=64), :]))
        kept = kept_ref[column_rows(n2), :]
        grad = turned_ref[column_rows(n2), :]
        up, down = pltpu.roll(kept, LANE, 1), pltpu.roll(kept, 3 * LANE, 1)
        mixed = jnp.where(
            lane < LANE,
            grad * up,
            jnp.where(
                lane < 2 * LANE,
                pltpu.roll(found, 3 * LANE, 1) * down,
                jnp.where(lane < 3 * LANE, found * up, found),
            ),
        )
        column_ref[pl.ds(n2, 32, stride=64), :] = mixed

    last_copy.wait()
    every(64, WIDE, final)

    tap0, tap1, tap2 = (
        jnp.broadcast_to(taps_ref[j : j + 1, :], (ROWS, 4 * LANE)) for j in range(3)
    )
    for block in range(SEQ):
        low = block * ROWS
        out_ref[block] = (
            tap0 * column_ref[low : low + ROWS, :]
            + tap1 * column_ref[low + 1 : low + 1 + ROWS, :]
            + tap2 * column_ref[low + 2 : low + 2 + ROWS, :]
        ).astype(BF16)


SHORT = pl.CostEstimate(flops=2_000_000_000, transcendentals=0, bytes_accessed=100_000)
LONG = pl.CostEstimate(flops=8_000_000_000, transcendentals=0, bytes_accessed=6_000_000)


def whole(shape):
    return pl.BlockSpec(shape, lambda _: (0,) * len(shape))


HELD = (
    pltpu.VMEM((64, MID, 96), BF16),
    pltpu.VMEM((128, 384), BF16),
    pltpu.VMEM((128, 384), BF16),
    pltpu.VMEM((64, 32, 3 * BACK), BF16),
    pltpu.VMEM((TOKENS, 4 * LANE), F32),
    pltpu.VMEM((HALF, 128, 4 * LANE), F32),
    pltpu.SemaphoreType.DMA((6,)),
)
FAR_OFF = pl.BlockSpec(memory_space=pltpu.HBM)


def resident(array):
    return pltpu.with_memory_space_constraint(array, pltpu.HBM)


def convolve(signals, taps, consts, interpret=False):
    return pl.pallas_call(
        forward_kernel,
        out_shape=(
            jax.ShapeDtypeStruct((NEAR, LANE, FAR * ROWS), BF16),
            pltpu.HBM((TOKENS, 4 * LANE), F32),
            pltpu.HBM((HALF, 128, 4 * LANE), F32),
        ),
        grid=(1,),
        in_specs=[whole(signals.shape), whole(taps.shape)] + [FAR_OFF] * 4,
        out_specs=(whole((NEAR, LANE, FAR * ROWS)), FAR_OFF, FAR_OFF),
        scratch_shapes=[
            pltpu.VMEM((TOKENS + 8, 4 * LANE), F32),
            pltpu.VMEM((64 * MID, 4 * LANE), F32),
            pltpu.VMEM((64 * BACK, 4 * LANE), F32),
            pltpu.VMEM((TOKENS, 4 * LANE), F32),
            *HELD,
        ],
        compiler_params=pltpu.CompilerParams(vmem_limit_bytes=VMEM_LIMIT),
        cost_estimate=SHORT,
        interpret=interpret,
        name="convolve",
    )(signals, taps, *(resident(x) for x in consts))


def correlate(shares, kept, spec, taps, consts, interpret=False):
    half = pl.BlockSpec((SEQ, LANE, FAR * ROWS), lambda _: (0, 1, 0))
    return pl.pallas_call(
        backward_kernel,
        out_shape=jax.ShapeDtypeStruct((SEQ, ROWS, 4 * LANE), BF16),
        grid=(1,),
        in_specs=[half, FAR_OFF, FAR_OFF, whole(taps.shape)] + [FAR_OFF] * 4,
        out_specs=whole((SEQ, ROWS, 4 * LANE)),
        scratch_shapes=[
            pltpu.VMEM((TOKENS, 4 * LANE), F32),
            pltpu.VMEM((64 * MID, 4 * LANE), F32),
            pltpu.VMEM((64 * BACK, 4 * LANE), F32),
            pltpu.VMEM((TOKENS + 8, 4 * LANE), F32),
            pltpu.VMEM((TOKENS, 4 * LANE), F32),
            *HELD,
        ],
        compiler_params=pltpu.CompilerParams(vmem_limit_bytes=VMEM_LIMIT),
        cost_estimate=LONG,
        interpret=interpret,
        name="correlate",
    )(shares, resident(kept), resident(spec), taps, *(resident(x) for x in consts))


def pack_kernel(streams_hbm, filter_hbm, out_hbm, streams_ref, filter_ref, out_ref, sems):
    lane = lanes_of(ROWS)
    columns = range(COLS // 128)
    spans = [slice(column * 128, (column + 1) * 128) for column in columns]
    arrivals = [
        (
            started(streams_hbm.at[:, :, span], streams_ref.at[column], sems.at[column]),
            started(filter_hbm.at[:, span], filter_ref.at[column], sems.at[4 + column]),
        )
        for column, span in zip(columns, spans)
    ]
    departures = []
    for column in columns:
        for copy in arrivals[column]:
            copy.wait()
        blocks = [streams_ref[column, j].astype(F32) for j in range(3)] + [filter_ref[column]]
        for part in range(4):
            placed = [pltpu.roll(b, ((j - part) % 4) * LANE, 1) if j != part else b
                      for j, b in enumerate(blocks)]
            joined = placed[3]
            for j in range(2, -1, -1):
                joined = jnp.where(lane < (j + 1) * LANE, placed[j], joined)
            out_ref[column * 4 + part] = joined.astype(BF16)
        part = slice(column * 4, column * 4 + 4)
        departures.append(started(out_ref.at[part], out_hbm.at[part], sems.at[8 + column]))
    for copy in departures:
        copy.wait()


def unpack_kernel(got_ref, streams_ref, filter_ref):
    lane = lanes_of(ROWS)
    for column in range(COLS // 128):
        at = slice(column * 128, (column + 1) * 128)
        blocks = [got_ref[column * 4 + part].astype(F32) for part in range(4)]
        for j in range(4):
            placed = [pltpu.roll(b, ((part - j) % 4) * LANE, 1) if j != part else b
                      for part, b in enumerate(blocks)]
            joined = placed[3]
            for part in range(2, -1, -1):
                joined = jnp.where(lane < (part + 1) * LANE, placed[part], joined)
            if j < 3:
                streams_ref[j, :, at] = joined.astype(BF16)
            else:
                filter_ref[:, at] = joined


def contract(left, right, left_dim, right_dim):
    return lax.dot_general(
        left, right, (((left_dim,), (right_dim,)), ((), ())), preferred_element_type=F32
    )


def fetch_weights(place_ref, refs, weights, sems):
    copies = []
    for step in range(NEAR):
        low = pl.multiple_of((place_ref[0] ^ step) * 256, 256)
        copies.append(started(refs[step], weights.at[:, pl.ds(low, 256)], sems.at[step]))
    return copies


def fetch_cots(place_ref, refs, cots, sems):
    copies = []
    for far in range(FAR):
        row = pl.multiple_of((place_ref[1] ^ far) * ROWS, ROWS)
        for side in range(2):
            low = pl.multiple_of((place_ref[2] ^ side) * COLS, COLS)
            copies.append(
                started(
                    refs[far].at[side],
                    cots.at[pl.ds(row, ROWS), pl.ds(low, COLS)],
                    sems.at[NEAR + 2 * far + side],
                )
            )
    return copies


def send_kernel(place_ref, gated_ref, *refs):
    sent_ref, weights, cots, sems = refs[NEAR + FAR :]
    copies = fetch_weights(place_ref, refs[:NEAR], weights, sems)
    copies += fetch_cots(place_ref, refs[NEAR : NEAR + FAR], cots, sems)
    for s in range(SEQ):
        sent_ref[s, :LANE, :] = gated_ref[s % NEAR]
    for copy in copies:
        copy.wait()
    total = contract(weights[...], cots[...], 1, 1).astype(BF16)
    for s in range(SEQ):
        sent_ref[s, LANE:, :] = total[s * LANE : (s + 1) * LANE]


def output_kernel(place_ref, got_ref, *refs):
    out_hbm, weights, out_ref, sems = refs[NEAR:]
    copies = fetch_weights(place_ref, refs[:NEAR], weights, sems)
    gated = got_ref[...].reshape(COLS, FAR * ROWS)
    for copy in copies:
        copy.wait()
    departures = []
    for a in range(FAR):
        part = contract(gated[:, a * ROWS : (a + 1) * ROWS], weights[...], 0, 0).astype(BF16)
        out_ref[2 * a] = part[:, :COLS]
        out_ref[2 * a + 1] = part[:, COLS:]
        span = slice(2 * a, 2 * a + 2)
        departures.append(started(out_ref.at[span], out_hbm.at[span], sems.at[NEAR + a]))
    for copy in departures:
        copy.wait()


def weight_kernel(place_ref, got_ref, *refs):
    grad_hbms = refs[FAR : FAR + NEAR]
    cots, own_ref, other_ref, sems = refs[FAR + NEAR :]
    copies = fetch_cots(place_ref, refs[:FAR], cots, sems)
    gated = got_ref[...].reshape(COLS, FAR * ROWS)
    for copy in copies:
        copy.wait()
    departures = []
    for step in reversed(range(NEAR)):
        low = pl.multiple_of((place_ref[0] ^ step) * 256, 256)
        grad = contract(gated, cots[:, pl.ds(low, 256)], 1, 0)
        if step:
            other_ref[step - 1] = grad.astype(BF16)
            source = other_ref.at[step - 1]
        else:
            own_ref[...] = grad
            source = own_ref
        departures.append(started(source, grad_hbms[step], sems.at[step]))
    for copy in departures:
        copy.wait()


def call(kernel, name, out_shape, interpret, *inputs, specs=None, scratch=(), far_out=False):
    many = isinstance(out_shape, tuple)
    outs = out_shape if many else (out_shape,)
    in_specs = [whole(x.shape) for x in inputs]
    for at, spec in (specs or {}).items():
        in_specs[at] = spec
    out_specs = tuple(FAR_OFF if far_out else whole(x.shape) for x in outs)
    return pl.pallas_call(
        kernel,
        out_shape=out_shape,
        grid=(1,),
        in_specs=in_specs,
        out_specs=out_specs if many else out_specs[0],
        scratch_shapes=list(scratch),
        compiler_params=pltpu.CompilerParams(vmem_limit_bytes=VMEM_LIMIT),
        cost_estimate=pl.CostEstimate(flops=1_000_000_000, transcendentals=0, bytes_accessed=2_000_000),
        interpret=interpret,
        name=name,
    )(*inputs)


SCALAR = pl.BlockSpec(memory_space=pltpu.SMEM)


def pack(streams, long_filter, interpret=False):
    return pl.pallas_call(
        pack_kernel,
        out_shape=pltpu.HBM((SEQ, ROWS, 4 * LANE), BF16),
        in_specs=[FAR_OFF, FAR_OFF],
        out_specs=FAR_OFF,
        scratch_shapes=[
            pltpu.VMEM((4, 3, ROWS, 128), BF16),
            pltpu.VMEM((4, ROWS, 128), F32),
            pltpu.VMEM((SEQ, ROWS, 4 * LANE), BF16),
            pltpu.SemaphoreType.DMA((12,)),
        ],
        compiler_params=pltpu.CompilerParams(vmem_limit_bytes=VMEM_LIMIT),
        interpret=interpret,
        name="pack",
    )(resident(streams), resident(long_filter))


def unpack(got, interpret=False):
    shapes = (
        jax.ShapeDtypeStruct((3, ROWS, COLS), BF16),
        jax.ShapeDtypeStruct((ROWS, COLS), F32),
    )
    return call(unpack_kernel, "unpack", shapes, interpret, got)


def far_off(low, high):
    return {at: FAR_OFF for at in range(low, high)}


GATHERED = (
    pltpu.VMEM((COLS, 2 * COLS), BF16),
    pltpu.VMEM((FAR * ROWS, 2 * COLS), BF16),
    pltpu.SemaphoreType.DMA((NEAR + 2 * FAR,)),
)


def to_send(place, gated, weights, cots, interpret=False):
    shape = jax.ShapeDtypeStruct((SEQ, 2 * LANE, FAR * ROWS), BF16)
    return call(
        send_kernel, "send", shape, interpret, place, gated, *weights, *cots,
        specs={0: SCALAR, **far_off(2, 2 + NEAR + FAR)}, scratch=GATHERED,
    )


GATED = pl.BlockSpec((SEQ, LANE, FAR * ROWS), lambda _: (0, 0, 0))


def output_shares(place, got, weights, interpret=False):
    return call(
        output_kernel, "outputs", pltpu.HBM((CHAN, ROWS, COLS), BF16), interpret,
        place, got, *weights, specs={0: SCALAR, 1: GATED, **far_off(2, 2 + NEAR)},
        scratch=(GATHERED[0], pltpu.VMEM((CHAN, ROWS, COLS), BF16), GATHERED[2]), far_out=True,
    )


def weight_shares(place, got, cots, width, interpret=False):
    shapes = tuple(pltpu.HBM((COLS, width), BF16 if step else F32) for step in range(NEAR))
    return call(
        weight_kernel, "weights", shapes, interpret, place, got, *cots,
        specs={0: SCALAR, 1: GATED, **far_off(2, 2 + FAR)}, far_out=True,
        scratch=(
            GATHERED[1],
            pltpu.VMEM((COLS, width), F32),
            pltpu.VMEM((NEAR - 1, COLS, width), BF16),
            GATHERED[2],
        ),
    )


def shards(projected, short_filter, long_filter, w_out, d_out):
    seq_at = lax.axis_index("seq")
    chan_at = lax.axis_index("chan")
    place = jnp.stack([seq_at % NEAR, chan_at // 2, chan_at % 2]).astype(jnp.int32)
    consts = [jnp.asarray(table) for table in tables()]

    moved = swapped(d_out)
    signals = exchange(pack(projected.transpose(1, 0, 2), long_filter), "seq")
    pair = jnp.stack([moved, lax.ppermute(moved, "chan", chan_pairs(1))])
    cots = [pair] + [lax.ppermute(pair, "chan", chan_pairs(2 * far)) for far in range(1, FAR)]
    weights = [w_out] + [lax.ppermute(w_out, "seq", near_pairs(step)) for step in range(1, NEAR)]

    own = lax.dynamic_slice_in_dim(short_filter, seq_at * LANE, LANE, axis=2).reshape(3, 3 * LANE)
    plain = jnp.zeros((3, LANE), F32).at[0].set(1.0)
    taps = jnp.concatenate([own, plain], axis=1)

    gated, kept, spec = convolve(signals.reshape(TOKENS, 4 * LANE), taps, consts)
    got = exchange(to_send(place, gated, weights, cots), "seq")

    shares = exchange(output_shares(place, got, weights), "chan")
    d_wout, *others = weight_shares(place, got, cots, w_out.shape[1])
    output = swapped(jnp.sum(shares.astype(F32), axis=0).astype(BF16))
    for step, piece in enumerate(others, 1):
        d_wout = d_wout + lax.ppermute(piece, "seq", near_pairs(step)).astype(F32)

    returned = exchange(correlate(got, kept, spec, taps, consts), "seq")
    d_projected, d_filter = unpack(returned)
    return (output, d_projected.transpose(1, 0, 2), d_wout, d_filter)


def solution(mesh):
    in_specs = (
        P("seq", None, "chan"),
        P(None, None, "chan"),
        P("seq", "chan"),
        P("chan", "seq"),
        P("seq", "chan"),
    )
    out_specs = (P("seq", "chan"), P("seq", None, "chan"), P("chan", "seq"), P("seq", "chan"))
    return jax.shard_map(shards, mesh=mesh, in_specs=in_specs, out_specs=out_specs, check_vma=False)
```

```python
import numpy as np
import ml_dtypes

import jax
import jax.numpy as jnp
from jax import lax
from jax.experimental import pallas as pl
from jax.experimental.pallas import tpu as pltpu
from jax.sharding import PartitionSpec as P

BF16 = jnp.bfloat16
F32 = jnp.float32

SEQ = 16
CHAN = 8
TOKENS = 2048
ROWS = 128
COLS = 512
LANE = 32
NEAR = 4
FAR = SEQ // NEAR
HALF = 33
MID = 72
BACK = 80
VMEM_LIMIT = 48 * 1024 * 1024
WIDE = 16
GROUP = 33


def device(seq_at, chan_at):
    return seq_at * CHAN + chan_at


def swap_pairs():
    pairs = []
    for seq_at in range(SEQ):
        for chan_at in range(CHAN):
            a, i = divmod(seq_at, NEAR)
            b, p = divmod(chan_at, CHAN // FAR)
            pairs.append(
                (device(seq_at, chan_at), device(b * NEAR + i, a * (CHAN // FAR) + p))
            )
    return pairs


def swapped(array):
    return lax.ppermute(array, ("seq", "chan"), swap_pairs())


def near_pairs(step):
    return [(i, i ^ step) for i in range(SEQ)]


def chan_pairs(step):
    return [(i, i ^ step) for i in range(CHAN)]


def exchange(array, axis):
    return lax.all_to_all(array, axis, 0, 0, tiled=True)


def thrice(table):
    high = table.astype(ml_dtypes.bfloat16)
    low = (table - high.astype(np.float64)).astype(ml_dtypes.bfloat16)
    return np.concatenate([high, high, low], axis=-1)


def tables():
    n1 = np.arange(32)
    n2 = np.arange(64)
    k1 = np.arange(HALF)
    k2 = np.arange(64)
    time = 64 * n1[None, None, :] + n2[:, None, None]
    outer = 2.0 * np.pi / 4096.0 * ((time * k1[None, :, None]) % 4096)
    inner = 2.0 * np.pi / 64.0 * ((k2[:, None] * n2[None, :]) % 64)
    weight = np.where((k1 == 0) | (k1 == 32), 1.0, 2.0)[None, :, None] / 4096.0
    first = np.zeros((64, MID, 32))
    first[:, :HALF] = np.cos(outer)
    first[:, HALF : 2 * HALF] = -np.sin(outer)
    last = np.zeros((64, 32, BACK))
    last[:, :, 0 : 2 * HALF : 2] = (np.cos(outer) * weight).transpose(0, 2, 1)
    last[:, :, 1 : 2 * HALF : 2] = (-np.sin(outer) * weight).transpose(0, 2, 1)
    cos, sin = np.cos(inner), np.sin(inner)
    ahead = np.block([[cos, sin], [-sin, cos]])
    return thrice(first), thrice(ahead), thrice(ahead.T), thrice(last)


def pieces(array):
    high = array.astype(BF16)
    low = (array - high.astype(F32)).astype(BF16)
    return jnp.concatenate([high, low, high], axis=0)


def matmul(left, right):
    return jnp.dot(left, right, preferred_element_type=F32)


def every(count, width, step):
    def body(block, carry):
        for at in range(width):
            step(block * width + at)
        return carry

    lax.fori_loop(0, count // width, body, 0)


def column_rows(n2):
    return pl.ds(pl.multiple_of(n2 * 32, 32), 32)


def lanes_of(rows):
    return lax.broadcasted_iota(jnp.int32, (rows, 4 * LANE), 1)


def ahead_rows(mid_ref, first):
    return jnp.concatenate(
        [
            jnp.concatenate(
                [
                    mid_ref[pl.ds(first + at, 64, stride=MID), :],
                    mid_ref[pl.ds(HALF + first + at, 64, stride=MID), :],
                ],
                axis=0,
            )
            for at in range(GROUP)
        ],
        axis=1,
    )


def behind_rows(back_ref, first, behind_ref, products):
    found = matmul(behind_ref[...], pieces(jnp.concatenate(products, axis=1)))
    for at in range(GROUP):
        back_ref[pl.ds(pl.multiple_of((first + at) * 128, 128), 128), :] = found[
            :, at * 128 : (at + 1) * 128
        ]


def started(source, target, sem):
    copy = pltpu.make_async_copy(source, target, sem)
    copy.start()
    return copy


def forward_kernel(
    signal_ref, taps_ref, first_hbm, ahead_hbm, behind_hbm, last_hbm,
    gated_ref, kept_hbm, spec_hbm,
    wide_ref, mid_ref, back_ref, column_ref,
    first_ref, ahead_ref, behind_ref, last_ref, kept_ref, spec_ref, sems,
):
    first_copy = started(first_hbm, first_ref, sems.at[0])
    ahead_copy = started(ahead_hbm, ahead_ref, sems.at[1])
    behind_copy = started(behind_hbm, behind_ref, sems.at[2])
    last_copy = started(last_hbm, last_ref, sems.at[3])
    wide_ref[0:8, :] = jnp.zeros((8, 4 * LANE), F32)
    wide_ref[8:, :] = signal_ref[...].astype(F32)
    back_ref[2 * HALF * 64 :, :] = jnp.zeros(((BACK - 2 * HALF) * 64, 4 * LANE), F32)
    lane = lanes_of(32)
    tap0, tap1, tap2 = (jnp.broadcast_to(taps_ref[j : j + 1, :], (32, 4 * LANE)) for j in range(3))

    def outer(n2):
        now = wide_ref[pl.ds(n2 + 8, 32, stride=64), :]
        before = wide_ref[pl.ds(n2 + 7, 32, stride=64), :]
        earlier = wide_ref[pl.ds(n2 + 6, 32, stride=64), :]
        mixed = tap0 * now + tap1 * before + tap2 * earlier
        kept_ref[column_rows(n2), :] = mixed
        carried = mixed * pltpu.roll(mixed, LANE, 1)
        data = jnp.where((lane >= 2 * LANE) & (lane < 3 * LANE), carried, mixed)
        mid_ref[pl.ds(pl.multiple_of(n2 * MID, 8), MID), :] = matmul(first_ref[n2], pieces(data))

    first_copy.wait()
    every(64, WIDE, outer)

    def inner(group):
        spec = matmul(ahead_ref[...], pieces(ahead_rows(mid_ref, group * GROUP)))
        products = []
        for at in range(GROUP):
            one = spec[:, at * 128 : (at + 1) * 128]
            spec_ref[group * GROUP + at] = one
            other = pltpu.roll(one, 3 * LANE, 1)
            re, im, other_re, other_im = one[:64], one[64:], other[:64], other[64:]
            products.append(
                jnp.concatenate(
                    [re * other_re - im * other_im, re * other_im + im * other_re], axis=0
                )
            )
        behind_rows(back_ref, group * GROUP, behind_ref, products)

    ahead_copy.wait()
    behind_copy.wait()
    every(HALF // GROUP, 1, inner)
    spec_copy = started(spec_ref, spec_hbm, sems.at[4])

    def final(n2):
        conv = matmul(last_ref[n2], pieces(back_ref[pl.ds(n2, BACK, stride=64), :]))
        mixed = kept_ref[column_rows(n2), :]
        column_ref[pl.ds(n2, 32, stride=64), :] = mixed * pltpu.roll(conv, 2 * LANE, 1)
        kept_ref[column_rows(n2), :] = jnp.where(
            lane < 3 * LANE, mixed, pltpu.roll(conv, LANE, 1)
        )

    last_copy.wait()

    def block_of(block, carry):
        for at in range(WIDE):
            final(block * WIDE + at)
        rows = pl.ds(pl.multiple_of(block * WIDE * 32, 32), WIDE * 32)
        started(kept_ref.at[rows], kept_hbm.at[rows], sems.at[5])
        return carry

    lax.fori_loop(0, 64 // WIDE, block_of, 0)
    kept_copy = pltpu.make_async_copy(kept_ref, kept_hbm, sems.at[5])

    for block in range(SEQ):
        a, i = divmod(block, NEAR)
        turned = column_ref[block * ROWS : (block + 1) * ROWS, :].T
        gated_ref[i, :, a * ROWS : (a + 1) * ROWS] = turned[:LANE].astype(BF16)
    spec_copy.wait()
    kept_copy.wait()


def backward_kernel(
    share_ref, kept_hbm, spec_hbm, taps_ref, first_hbm, ahead_hbm, behind_hbm, last_hbm,
    out_ref,
    grad_ref, mid_ref, back_ref, column_ref, turned_ref,
    first_ref, ahead_ref, behind_ref, last_ref, kept_ref, spec_ref, sems,
):
    first_copy = started(first_hbm, first_ref, sems.at[0])
    kept_copy = started(kept_hbm, kept_ref, sems.at[5])
    ahead_copy = started(ahead_hbm, ahead_ref, sems.at[1])
    behind_copy = started(behind_hbm, behind_ref, sems.at[2])
    spec_copy = started(spec_hbm, spec_ref, sems.at[4])
    last_copy = started(last_hbm, last_ref, sems.at[3])
    back_ref[2 * HALF * 64 :, :] = jnp.zeros(((BACK - 2 * HALF) * 64, 4 * LANE), F32)
    column_ref[TOKENS:, :] = jnp.zeros((8, 4 * LANE), F32)
    for i in range(NEAR):
        total = share_ref[i].astype(F32)
        for far in range(1, FAR):
            total = total + share_ref[far * NEAR + i].astype(F32)
        for a in range(FAR):
            block = a * NEAR + i
            part = total[:, a * ROWS : (a + 1) * ROWS]
            grad_ref[block * ROWS : (block + 1) * ROWS, :] = jnp.concatenate([part] * 4, axis=0).T
    lane = lanes_of(32)

    def outer(n2):
        kept = kept_ref[column_rows(n2), :]
        query = jnp.where(lane < 3 * LANE, pltpu.roll(kept, 2 * LANE, 1), pltpu.roll(kept, 3 * LANE, 1))
        grad = grad_ref[pl.ds(n2, 32, stride=64), :]
        turned_ref[column_rows(n2), :] = grad
        data = grad * query
        mid_ref[pl.ds(pl.multiple_of(n2 * MID, 8), MID), :] = matmul(first_ref[n2], pieces(data))

    first_copy.wait()
    kept_copy.wait()
    every(64, WIDE, outer)

    wide = lanes_of(128)

    def inner(group):
        grad = matmul(ahead_ref[...], pieces(ahead_rows(mid_ref, group * GROUP)))
        products = []
        for at in range(GROUP):
            one = grad[:, at * 128 : (at + 1) * 128]
            spec = spec_ref[group * GROUP + at]
            other = jnp.where(
                wide < 3 * LANE, pltpu.roll(spec, 3 * LANE, 1), pltpu.roll(spec, LANE, 1)
            )
            re, im, other_re, other_im = one[:64], one[64:], other[:64], other[64:]
            products.append(
                jnp.concatenate(
                    [other_re * re + other_im * im, other_re * im - other_im * re], axis=0
                )
            )
        behind_rows(back_ref, group * GROUP, behind_ref, products)

    ahead_copy.wait()
    behind_copy.wait()
    spec_copy.wait()
    every(HALF // GROUP, 1, inner)

    def final(n2):
        found = matmul(last_ref[n2], pieces(back_ref[pl.ds(n2, BACK, stride=64), :]))
        kept = kept_ref[column_rows(n2), :]
        grad = turned_ref[column_rows(n2), :]
        up, down = pltpu.roll(kept, LANE, 1), pltpu.roll(kept, 3 * LANE, 1)
        mixed = jnp.where(
            lane < LANE,
            grad * up,
            jnp.where(
                lane < 2 * LANE,
                pltpu.roll(found, 3 * LANE, 1) * down,
                jnp.where(lane < 3 * LANE, found * up, found),
            ),
        )
        column_ref[pl.ds(n2, 32, stride=64), :] = mixed

    last_copy.wait()
    every(64, WIDE, final)

    tap0, tap1, tap2 = (
        jnp.broadcast_to(taps_ref[j : j + 1, :], (ROWS, 4 * LANE)) for j in range(3)
    )
    for block in range(SEQ):
        low = block * ROWS
        out_ref[block] = (
            tap0 * column_ref[low : low + ROWS, :]
            + tap1 * column_ref[low + 1 : low + 1 + ROWS, :]
            + tap2 * column_ref[low + 2 : low + 2 + ROWS, :]
        ).astype(BF16)


SHORT = pl.CostEstimate(flops=2_000_000_000, transcendentals=0, bytes_accessed=100_000)
LONG = pl.CostEstimate(flops=8_000_000_000, transcendentals=0, bytes_accessed=6_000_000)


def whole(shape):
    return pl.BlockSpec(shape, lambda _: (0,) * len(shape))


HELD = (
    pltpu.VMEM((64, MID, 96), BF16),
    pltpu.VMEM((128, 384), BF16),
    pltpu.VMEM((128, 384), BF16),
    pltpu.VMEM((64, 32, 3 * BACK), BF16),
    pltpu.VMEM((TOKENS, 4 * LANE), F32),
    pltpu.VMEM((HALF, 128, 4 * LANE), F32),
    pltpu.SemaphoreType.DMA((6,)),
)
FAR_OFF = pl.BlockSpec(memory_space=pltpu.HBM)


def resident(array):
    return pltpu.with_memory_space_constraint(array, pltpu.HBM)


def convolve(signals, taps, consts, interpret=False):
    return pl.pallas_call(
        forward_kernel,
        out_shape=(
            jax.ShapeDtypeStruct((NEAR, LANE, FAR * ROWS), BF16),
            pltpu.HBM((TOKENS, 4 * LANE), F32),
            pltpu.HBM((HALF, 128, 4 * LANE), F32),
        ),
        grid=(1,),
        in_specs=[whole(signals.shape), whole(taps.shape)] + [FAR_OFF] * 4,
        out_specs=(whole((NEAR, LANE, FAR * ROWS)), FAR_OFF, FAR_OFF),
        scratch_shapes=[
            pltpu.VMEM((TOKENS + 8, 4 * LANE), F32),
            pltpu.VMEM((64 * MID, 4 * LANE), F32),
            pltpu.VMEM((64 * BACK, 4 * LANE), F32),
            pltpu.VMEM((TOKENS, 4 * LANE), F32),
            *HELD,
        ],
        compiler_params=pltpu.CompilerParams(vmem_limit_bytes=VMEM_LIMIT),
        cost_estimate=SHORT,
        interpret=interpret,
        name="convolve",
    )(signals, taps, *(resident(x) for x in consts))


def correlate(shares, kept, spec, taps, consts, interpret=False):
    half = pl.BlockSpec((SEQ, LANE, FAR * ROWS), lambda _: (0, 1, 0))
    return pl.pallas_call(
        backward_kernel,
        out_shape=jax.ShapeDtypeStruct((SEQ, ROWS, 4 * LANE), BF16),
        grid=(1,),
        in_specs=[half, FAR_OFF, FAR_OFF, whole(taps.shape)] + [FAR_OFF] * 4,
        out_specs=whole((SEQ, ROWS, 4 * LANE)),
        scratch_shapes=[
            pltpu.VMEM((TOKENS, 4 * LANE), F32),
            pltpu.VMEM((64 * MID, 4 * LANE), F32),
            pltpu.VMEM((64 * BACK, 4 * LANE), F32),
            pltpu.VMEM((TOKENS + 8, 4 * LANE), F32),
            pltpu.VMEM((TOKENS, 4 * LANE), F32),
            *HELD,
        ],
        compiler_params=pltpu.CompilerParams(vmem_limit_bytes=VMEM_LIMIT),
        cost_estimate=LONG,
        interpret=interpret,
        name="correlate",
    )(shares, resident(kept), resident(spec), taps, *(resident(x) for x in consts))


def pack_kernel(streams_hbm, filter_hbm, out_hbm, streams_ref, filter_ref, out_ref, sems):
    lane = lanes_of(ROWS)
    columns = range(COLS // 128)
    spans = [slice(column * 128, (column + 1) * 128) for column in columns]
    arrivals = [
        (
            started(streams_hbm.at[:, :, span], streams_ref.at[column], sems.at[column]),
            started(filter_hbm.at[:, span], filter_ref.at[column], sems.at[4 + column]),
        )
        for column, span in zip(columns, spans)
    ]
    departures = []
    for column in columns:
        for copy in arrivals[column]:
            copy.wait()
        blocks = [streams_ref[column, j].astype(F32) for j in range(3)] + [filter_ref[column]]
        for part in range(4):
            placed = [pltpu.roll(b, ((j - part) % 4) * LANE, 1) if j != part else b
                      for j, b in enumerate(blocks)]
            joined = placed[3]
            for j in range(2, -1, -1):
                joined = jnp.where(lane < (j + 1) * LANE, placed[j], joined)
            out_ref[column * 4 + part] = joined.astype(BF16)
        part = slice(column * 4, column * 4 + 4)
        departures.append(started(out_ref.at[part], out_hbm.at[part], sems.at[8 + column]))
    for copy in departures:
        copy.wait()


def unpack_kernel(got_ref, streams_ref, filter_ref):
    lane = lanes_of(ROWS)
    for column in range(COLS // 128):
        at = slice(column * 128, (column + 1) * 128)
        blocks = [got_ref[column * 4 + part].astype(F32) for part in range(4)]
        for j in range(4):
            placed = [pltpu.roll(b, ((part - j) % 4) * LANE, 1) if j != part else b
                      for part, b in enumerate(blocks)]
            joined = placed[3]
            for part in range(2, -1, -1):
                joined = jnp.where(lane < (part + 1) * LANE, placed[part], joined)
            if j < 3:
                streams_ref[j, :, at] = joined.astype(BF16)
            else:
                filter_ref[:, at] = joined


def contract(left, right, left_dim, right_dim):
    return lax.dot_general(
        left, right, (((left_dim,), (right_dim,)), ((), ())), preferred_element_type=F32
    )


def fetch_weights(place_ref, refs, weights, sems):
    copies = []
    for step in range(NEAR):
        low = pl.multiple_of((place_ref[0] ^ step) * 256, 256)
        copies.append(started(refs[step], weights.at[:, pl.ds(low, 256)], sems.at[step]))
    return copies


def fetch_cots(place_ref, refs, cots, sems):
    copies = []
    for far in range(FAR):
        low = pl.multiple_of((place_ref[2] ^ (far % 2)) * COLS, COLS)
        for side in range(2):
            row = pl.multiple_of((place_ref[1] ^ (far // 2 + 2 * side)) * ROWS, ROWS)
            copies.append(
                started(
                    refs[far].at[side],
                    cots.at[pl.ds(row, ROWS), pl.ds(low, COLS)],
                    sems.at[NEAR + 2 * far + side],
                )
            )
    return copies


def send_kernel(place_ref, gated_ref, *refs):
    sent_ref, weights, cots, sems = refs[NEAR + FAR :]
    copies = fetch_weights(place_ref, refs[:NEAR], weights, sems)
    copies += fetch_cots(place_ref, refs[NEAR : NEAR + FAR], cots, sems)
    for s in range(SEQ):
        sent_ref[s, :LANE, :] = gated_ref[s % NEAR]
    for copy in copies:
        copy.wait()
    total = contract(weights[...], cots[...], 1, 1).astype(BF16)
    for s in range(SEQ):
        sent_ref[s, LANE:, :] = total[s * LANE : (s + 1) * LANE]


def output_kernel(place_ref, got_ref, *refs):
    out_hbm, weights, out_ref, sems = refs[NEAR:]
    copies = fetch_weights(place_ref, refs[:NEAR], weights, sems)
    gated = got_ref[...].reshape(COLS, FAR * ROWS)
    for copy in copies:
        copy.wait()
    departures = []
    for a in range(FAR):
        part = contract(gated[:, a * ROWS : (a + 1) * ROWS], weights[...], 0, 0).astype(BF16)
        out_ref[2 * a] = part[:, :COLS]
        out_ref[2 * a + 1] = part[:, COLS:]
        span = slice(2 * a, 2 * a + 2)
        departures.append(started(out_ref.at[span], out_hbm.at[span], sems.at[NEAR + a]))
    for copy in departures:
        copy.wait()


def weight_kernel(place_ref, got_ref, *refs):
    grad_hbms = refs[FAR : FAR + NEAR]
    cots, own_ref, other_ref, sems = refs[FAR + NEAR :]
    copies = fetch_cots(place_ref, refs[:FAR], cots, sems)
    gated = got_ref[...].reshape(COLS, FAR * ROWS)
    for copy in copies:
        copy.wait()
    departures = []
    for step in reversed(range(NEAR)):
        low = pl.multiple_of((place_ref[0] ^ step) * 256, 256)
        grad = contract(gated, cots[:, pl.ds(low, 256)], 1, 0)
        if step:
            other_ref[step - 1] = grad.astype(BF16)
            source = other_ref.at[step - 1]
        else:
            own_ref[...] = grad
            source = own_ref
        departures.append(started(source, grad_hbms[step], sems.at[step]))
    for copy in departures:
        copy.wait()


def call(kernel, name, out_shape, interpret, *inputs, specs=None, scratch=(), far_out=False):
    many = isinstance(out_shape, tuple)
    outs = out_shape if many else (out_shape,)
    in_specs = [whole(x.shape) for x in inputs]
    for at, spec in (specs or {}).items():
        in_specs[at] = spec
    out_specs = tuple(FAR_OFF if far_out else whole(x.shape) for x in outs)
    return pl.pallas_call(
        kernel,
        out_shape=out_shape,
        grid=(1,),
        in_specs=in_specs,
        out_specs=out_specs if many else out_specs[0],
        scratch_shapes=list(scratch),
        compiler_params=pltpu.CompilerParams(vmem_limit_bytes=VMEM_LIMIT),
        cost_estimate=pl.CostEstimate(flops=1_000_000_000, transcendentals=0, bytes_accessed=2_000_000),
        interpret=interpret,
        name=name,
    )(*inputs)


SCALAR = pl.BlockSpec(memory_space=pltpu.SMEM)


def pack(streams, long_filter, interpret=False):
    return pl.pallas_call(
        pack_kernel,
        out_shape=pltpu.HBM((SEQ, ROWS, 4 * LANE), BF16),
        in_specs=[FAR_OFF, FAR_OFF],
        out_specs=FAR_OFF,
        scratch_shapes=[
            pltpu.VMEM((4, 3, ROWS, 128), BF16),
            pltpu.VMEM((4, ROWS, 128), F32),
            pltpu.VMEM((SEQ, ROWS, 4 * LANE), BF16),
            pltpu.SemaphoreType.DMA((12,)),
        ],
        compiler_params=pltpu.CompilerParams(vmem_limit_bytes=VMEM_LIMIT),
        interpret=interpret,
        name="pack",
    )(resident(streams), resident(long_filter))


def unpack(got, interpret=False):
    shapes = (
        jax.ShapeDtypeStruct((3, ROWS, COLS), BF16),
        jax.ShapeDtypeStruct((ROWS, COLS), F32),
    )
    return call(unpack_kernel, "unpack", shapes, interpret, got)


def far_off(low, high):
    return {at: FAR_OFF for at in range(low, high)}


GATHERED = (
    pltpu.VMEM((COLS, 2 * COLS), BF16),
    pltpu.VMEM((FAR * ROWS, 2 * COLS), BF16),
    pltpu.SemaphoreType.DMA((NEAR + 2 * FAR,)),
)


def to_send(place, gated, weights, cots, interpret=False):
    shape = jax.ShapeDtypeStruct((SEQ, 2 * LANE, FAR * ROWS), BF16)
    return call(
        send_kernel, "send", shape, interpret, place, gated, *weights, *cots,
        specs={0: SCALAR, **far_off(2, 2 + NEAR + FAR)}, scratch=GATHERED,
    )


GATED = pl.BlockSpec((SEQ, LANE, FAR * ROWS), lambda _: (0, 0, 0))


def output_shares(place, got, weights, interpret=False):
    return call(
        output_kernel, "outputs", pltpu.HBM((CHAN, ROWS, COLS), BF16), interpret,
        place, got, *weights, specs={0: SCALAR, 1: GATED, **far_off(2, 2 + NEAR)},
        scratch=(GATHERED[0], pltpu.VMEM((CHAN, ROWS, COLS), BF16), GATHERED[2]), far_out=True,
    )


def weight_shares(place, got, cots, width, interpret=False):
    shapes = tuple(pltpu.HBM((COLS, width), BF16 if step else F32) for step in range(NEAR))
    return call(
        weight_kernel, "weights", shapes, interpret, place, got, *cots,
        specs={0: SCALAR, 1: GATED, **far_off(2, 2 + FAR)}, far_out=True,
        scratch=(
            GATHERED[1],
            pltpu.VMEM((COLS, width), F32),
            pltpu.VMEM((NEAR - 1, COLS, width), BF16),
            GATHERED[2],
        ),
    )


def shards(projected, short_filter, long_filter, w_out, d_out):
    seq_at = lax.axis_index("seq")
    chan_at = lax.axis_index("chan")
    place = jnp.stack([seq_at % NEAR, chan_at // 2, chan_at % 2]).astype(jnp.int32)
    consts = [jnp.asarray(table) for table in tables()]

    moved = swapped(d_out)
    signals = exchange(pack(projected.transpose(1, 0, 2), long_filter), "seq")
    pair = jnp.stack([moved, lax.ppermute(moved, "chan", chan_pairs(4))])
    cots = [pair] + [lax.ppermute(pair, "chan", chan_pairs(far)) for far in range(1, FAR)]
    weights = [w_out] + [lax.ppermute(w_out, "seq", near_pairs(step)) for step in range(1, NEAR)]

    own = lax.dynamic_slice_in_dim(short_filter, seq_at * LANE, LANE, axis=2).reshape(3, 3 * LANE)
    plain = jnp.zeros((3, LANE), F32).at[0].set(1.0)
    taps = jnp.concatenate([own, plain], axis=1)

    gated, kept, spec = convolve(signals.reshape(TOKENS, 4 * LANE), taps, consts)
    got = exchange(to_send(place, gated, weights, cots), "seq")

    shares = exchange(output_shares(place, got, weights), "chan")
    d_wout, *others = weight_shares(place, got, cots, w_out.shape[1])
    output = swapped(jnp.sum(shares.astype(F32), axis=0).astype(BF16))
    for step, piece in enumerate(others, 1):
        d_wout = d_wout + lax.ppermute(piece, "seq", near_pairs(step)).astype(F32)

    returned = exchange(correlate(got, kept, spec, taps, consts), "seq")
    d_projected, d_filter = unpack(returned)
    return (output, d_projected.transpose(1, 0, 2), d_wout, d_filter)


def solution(mesh):
    in_specs = (
        P("seq", None, "chan"),
        P(None, None, "chan"),
        P("seq", "chan"),
        P("chan", "seq"),
        P("seq", "chan"),
    )
    out_specs = (P("seq", "chan"), P("seq", None, "chan"), P("chan", "seq"), P("seq", "chan"))
    return jax.shard_map(shards, mesh=mesh, in_specs=in_specs, out_specs=out_specs, check_vma=False)
```

```python
import numpy as np
import ml_dtypes

import jax
import jax.numpy as jnp
from jax import lax
from jax.experimental import pallas as pl
from jax.experimental.pallas import tpu as pltpu
from jax.sharding import PartitionSpec as P

BF16 = jnp.bfloat16
F32 = jnp.float32

SEQ = 16
CHAN = 8
TOKENS = 2048
ROWS = 128
COLS = 512
LANE = 32
NEAR = 4
FAR = SEQ // NEAR
HALF = 33
MID = 72
BACK = 80
VMEM_LIMIT = 48 * 1024 * 1024
WIDE = 16
GROUP = 33


def device(seq_at, chan_at):
    return seq_at * CHAN + chan_at


def swap_pairs():
    pairs = []
    for seq_at in range(SEQ):
        for chan_at in range(CHAN):
            a, i = divmod(seq_at, NEAR)
            b, p = divmod(chan_at, CHAN // FAR)
            pairs.append(
                (device(seq_at, chan_at), device(b * NEAR + i, a * (CHAN // FAR) + p))
            )
    return pairs


def swapped(array):
    return lax.ppermute(array, ("seq", "chan"), swap_pairs())


def near_pairs(step):
    return [(i, i ^ step) for i in range(SEQ)]


def chan_pairs(step):
    return [(i, i ^ step) for i in range(CHAN)]


def exchange(array, axis):
    return lax.all_to_all(array, axis, 0, 0, tiled=True)


def thrice(table):
    high = table.astype(ml_dtypes.bfloat16)
    low = (table - high.astype(np.float64)).astype(ml_dtypes.bfloat16)
    return np.concatenate([high, high, low], axis=-1)


def tables():
    n1 = np.arange(32)
    n2 = np.arange(64)
    k1 = np.arange(HALF)
    k2 = np.arange(64)
    time = 64 * n1[None, None, :] + n2[:, None, None]
    outer = 2.0 * np.pi / 4096.0 * ((time * k1[None, :, None]) % 4096)
    inner = 2.0 * np.pi / 64.0 * ((k2[:, None] * n2[None, :]) % 64)
    weight = np.where((k1 == 0) | (k1 == 32), 1.0, 2.0)[None, :, None] / 4096.0
    first = np.zeros((64, MID, 32))
    first[:, :HALF] = np.cos(outer)
    first[:, HALF : 2 * HALF] = -np.sin(outer)
    last = np.zeros((64, 32, BACK))
    last[:, :, 0 : 2 * HALF : 2] = (np.cos(outer) * weight).transpose(0, 2, 1)
    last[:, :, 1 : 2 * HALF : 2] = (-np.sin(outer) * weight).transpose(0, 2, 1)
    cos, sin = np.cos(inner), np.sin(inner)
    ahead = np.block([[cos, sin], [-sin, cos]])
    return thrice(first), thrice(ahead), thrice(ahead.T), thrice(last)


def pieces(array):
    high = array.astype(BF16)
    low = (array - high.astype(F32)).astype(BF16)
    return jnp.concatenate([high, low, high], axis=0)


def matmul(left, right):
    return jnp.dot(left, right, preferred_element_type=F32)


def every(count, width, step):
    def body(block, carry):
        for at in range(width):
            step(block * width + at)
        return carry

    lax.fori_loop(0, count // width, body, 0)


def column_rows(n2):
    return pl.ds(pl.multiple_of(n2 * 32, 32), 32)


def lanes_of(rows):
    return lax.broadcasted_iota(jnp.int32, (rows, 4 * LANE), 1)


def ahead_rows(mid_ref, first):
    return jnp.concatenate(
        [
            jnp.concatenate(
                [
                    mid_ref[pl.ds(first + at, 64, stride=MID), :],
                    mid_ref[pl.ds(HALF + first + at, 64, stride=MID), :],
                ],
                axis=0,
            )
            for at in range(GROUP)
        ],
        axis=1,
    )


def behind_rows(back_ref, first, behind_ref, products):
    found = matmul(behind_ref[...], pieces(jnp.concatenate(products, axis=1)))
    for at in range(GROUP):
        back_ref[pl.ds(pl.multiple_of((first + at) * 128, 128), 128), :] = found[
            :, at * 128 : (at + 1) * 128
        ]


def started(source, target, sem):
    copy = pltpu.make_async_copy(source, target, sem)
    copy.start()
    return copy


def forward_kernel(
    signal_ref, taps_ref, first_hbm, ahead_hbm, behind_hbm, last_hbm,
    gated_ref, kept_hbm, spec_hbm,
    wide_ref, mid_ref, back_ref, column_ref,
    first_ref, ahead_ref, behind_ref, last_ref, kept_ref, spec_ref, sems,
):
    first_copy = started(first_hbm, first_ref, sems.at[0])
    ahead_copy = started(ahead_hbm, ahead_ref, sems.at[1])
    behind_copy = started(behind_hbm, behind_ref, sems.at[2])
    last_copy = started(last_hbm, last_ref, sems.at[3])
    wide_ref[0:8, :] = jnp.zeros((8, 4 * LANE), F32)
    wide_ref[8:, :] = signal_ref[...].astype(F32)
    back_ref[2 * HALF * 64 :, :] = jnp.zeros(((BACK - 2 * HALF) * 64, 4 * LANE), F32)
    lane = lanes_of(32)
    tap0, tap1, tap2 = (jnp.broadcast_to(taps_ref[j : j + 1, :], (32, 4 * LANE)) for j in range(3))

    def outer(n2):
        now = wide_ref[pl.ds(n2 + 8, 32, stride=64), :]
        before = wide_ref[pl.ds(n2 + 7, 32, stride=64), :]
        earlier = wide_ref[pl.ds(n2 + 6, 32, stride=64), :]
        mixed = tap0 * now + tap1 * before + tap2 * earlier
        kept_ref[column_rows(n2), :] = mixed
        carried = mixed * pltpu.roll(mixed, LANE, 1)
        data = jnp.where((lane >= 2 * LANE) & (lane < 3 * LANE), carried, mixed)
        mid_ref[pl.ds(pl.multiple_of(n2 * MID, 8), MID), :] = matmul(first_ref[n2], pieces(data))

    first_copy.wait()
    every(64, WIDE, outer)

    def inner(group):
        spec = matmul(ahead_ref[...], pieces(ahead_rows(mid_ref, group * GROUP)))
        products = []
        for at in range(GROUP):
            one = spec[:, at * 128 : (at + 1) * 128]
            spec_ref[group * GROUP + at] = one
            other = pltpu.roll(one, 3 * LANE, 1)
            re, im, other_re, other_im = one[:64], one[64:], other[:64], other[64:]
            products.append(
                jnp.concatenate(
                    [re * other_re - im * other_im, re * other_im + im * other_re], axis=0
                )
            )
        behind_rows(back_ref, group * GROUP, behind_ref, products)

    ahead_copy.wait()
    behind_copy.wait()
    every(HALF // GROUP, 1, inner)
    spec_copy = started(spec_ref, spec_hbm, sems.at[4])

    def final(n2):
        conv = matmul(last_ref[n2], pieces(back_ref[pl.ds(n2, BACK, stride=64), :]))
        mixed = kept_ref[column_rows(n2), :]
        column_ref[pl.ds(n2, 32, stride=64), :] = mixed * pltpu.roll(conv, 2 * LANE, 1)
        kept_ref[column_rows(n2), :] = jnp.where(
            lane < 3 * LANE, mixed, pltpu.roll(conv, LANE, 1)
        )

    last_copy.wait()

    def block_of(block, carry):
        for at in range(WIDE):
            final(block * WIDE + at)
        rows = pl.ds(pl.multiple_of(block * WIDE * 32, 32), WIDE * 32)
        started(kept_ref.at[rows], kept_hbm.at[rows], sems.at[5])
        return carry

    lax.fori_loop(0, 64 // WIDE, block_of, 0)
    kept_copy = pltpu.make_async_copy(kept_ref, kept_hbm, sems.at[5])

    for block in range(SEQ):
        a, i = divmod(block, NEAR)
        turned = column_ref[block * ROWS : (block + 1) * ROWS, :].T
        gated_ref[i, :, a * ROWS : (a + 1) * ROWS] = turned[:LANE].astype(BF16)
    spec_copy.wait()
    kept_copy.wait()


def backward_kernel(
    share_ref, kept_hbm, spec_hbm, taps_ref, first_hbm, ahead_hbm, behind_hbm, last_hbm,
    out_ref,
    grad_ref, mid_ref, back_ref, column_ref, turned_ref,
    first_ref, ahead_ref, behind_ref, last_ref, kept_ref, spec_ref, sems,
):
    first_copy = started(first_hbm, first_ref, sems.at[0])
    kept_copy = started(kept_hbm, kept_ref, sems.at[5])
    ahead_copy = started(ahead_hbm, ahead_ref, sems.at[1])
    behind_copy = started(behind_hbm, behind_ref, sems.at[2])
    spec_copy = started(spec_hbm, spec_ref, sems.at[4])
    last_copy = started(last_hbm, last_ref, sems.at[3])
    back_ref[2 * HALF * 64 :, :] = jnp.zeros(((BACK - 2 * HALF) * 64, 4 * LANE), F32)
    column_ref[TOKENS:, :] = jnp.zeros((8, 4 * LANE), F32)
    for i in range(NEAR):
        total = share_ref[i].astype(F32)
        for far in range(1, FAR):
            total = total + share_ref[far * NEAR + i].astype(F32)
        for a in range(FAR):
            block = a * NEAR + i
            part = total[:, a * ROWS : (a + 1) * ROWS]
            grad_ref[block * ROWS : (block + 1) * ROWS, :] = jnp.concatenate([part] * 4, axis=0).T
    lane = lanes_of(32)

    def outer(n2):
        kept = kept_ref[column_rows(n2), :]
        query = jnp.where(lane < 3 * LANE, pltpu.roll(kept, 2 * LANE, 1), pltpu.roll(kept, 3 * LANE, 1))
        grad = grad_ref[pl.ds(n2, 32, stride=64), :]
        turned_ref[column_rows(n2), :] = grad
        data = grad * query
        mid_ref[pl.ds(pl.multiple_of(n2 * MID, 8), MID), :] = matmul(first_ref[n2], pieces(data))

    first_copy.wait()
    kept_copy.wait()
    every(64, WIDE, outer)

    wide = lanes_of(128)

    def inner(group):
        grad = matmul(ahead_ref[...], pieces(ahead_rows(mid_ref, group * GROUP)))
        products = []
        for at in range(GROUP):
            one = grad[:, at * 128 : (at + 1) * 128]
            spec = spec_ref[group * GROUP + at]
            other = jnp.where(
                wide < 3 * LANE, pltpu.roll(spec, 3 * LANE, 1), pltpu.roll(spec, LANE, 1)
            )
            re, im, other_re, other_im = one[:64], one[64:], other[:64], other[64:]
            products.append(
                jnp.concatenate(
                    [other_re * re + other_im * im, other_re * im - other_im * re], axis=0
                )
            )
        behind_rows(back_ref, group * GROUP, behind_ref, products)

    ahead_copy.wait()
    behind_copy.wait()
    spec_copy.wait()
    every(HALF // GROUP, 1, inner)

    def final(n2):
        found = matmul(last_ref[n2], pieces(back_ref[pl.ds(n2, BACK, stride=64), :]))
        kept = kept_ref[column_rows(n2), :]
        grad = turned_ref[column_rows(n2), :]
        up, down = pltpu.roll(kept, LANE, 1), pltpu.roll(kept, 3 * LANE, 1)
        mixed = jnp.where(
            lane < LANE,
            grad * up,
            jnp.where(
                lane < 2 * LANE,
                pltpu.roll(found, 3 * LANE, 1) * down,
                jnp.where(lane < 3 * LANE, found * up, found),
            ),
        )
        column_ref[pl.ds(n2, 32, stride=64), :] = mixed

    last_copy.wait()
    every(64, WIDE, final)

    tap0, tap1, tap2 = (
        jnp.broadcast_to(taps_ref[j : j + 1, :], (ROWS, 4 * LANE)) for j in range(3)
    )
    for block in range(SEQ):
        low = block * ROWS
        out_ref[block] = (
            tap0 * column_ref[low : low + ROWS, :]
            + tap1 * column_ref[low + 1 : low + 1 + ROWS, :]
            + tap2 * column_ref[low + 2 : low + 2 + ROWS, :]
        ).astype(BF16)


SHORT = pl.CostEstimate(flops=2_000_000_000, transcendentals=0, bytes_accessed=100_000)
LONG = pl.CostEstimate(flops=8_000_000_000, transcendentals=0, bytes_accessed=6_000_000)


def whole(shape):
    return pl.BlockSpec(shape, lambda _: (0,) * len(shape))


HELD = (
    pltpu.VMEM((64, MID, 96), BF16),
    pltpu.VMEM((128, 384), BF16),
    pltpu.VMEM((128, 384), BF16),
    pltpu.VMEM((64, 32, 3 * BACK), BF16),
    pltpu.VMEM((TOKENS, 4 * LANE), F32),
    pltpu.VMEM((HALF, 128, 4 * LANE), F32),
    pltpu.SemaphoreType.DMA((6,)),
)
FAR_OFF = pl.BlockSpec(memory_space=pltpu.HBM)


def resident(array):
    return pltpu.with_memory_space_constraint(array, pltpu.HBM)


def convolve(signals, taps, consts, interpret=False):
    return pl.pallas_call(
        forward_kernel,
        out_shape=(
            jax.ShapeDtypeStruct((NEAR, LANE, FAR * ROWS), BF16),
            pltpu.HBM((TOKENS, 4 * LANE), F32),
            pltpu.HBM((HALF, 128, 4 * LANE), F32),
        ),
        grid=(1,),
        in_specs=[whole(signals.shape), whole(taps.shape)] + [FAR_OFF] * 4,
        out_specs=(whole((NEAR, LANE, FAR * ROWS)), FAR_OFF, FAR_OFF),
        scratch_shapes=[
            pltpu.VMEM((TOKENS + 8, 4 * LANE), F32),
            pltpu.VMEM((64 * MID, 4 * LANE), F32),
            pltpu.VMEM((64 * BACK, 4 * LANE), F32),
            pltpu.VMEM((TOKENS, 4 * LANE), F32),
            *HELD,
        ],
        compiler_params=pltpu.CompilerParams(vmem_limit_bytes=VMEM_LIMIT),
        cost_estimate=SHORT,
        interpret=interpret,
        name="convolve",
    )(signals, taps, *(resident(x) for x in consts))


def correlate(shares, kept, spec, taps, consts, interpret=False):
    half = pl.BlockSpec((SEQ, LANE, FAR * ROWS), lambda _: (0, 1, 0))
    return pl.pallas_call(
        backward_kernel,
        out_shape=jax.ShapeDtypeStruct((SEQ, ROWS, 4 * LANE), BF16),
        grid=(1,),
        in_specs=[half, FAR_OFF, FAR_OFF, whole(taps.shape)] + [FAR_OFF] * 4,
        out_specs=whole((SEQ, ROWS, 4 * LANE)),
        scratch_shapes=[
            pltpu.VMEM((TOKENS, 4 * LANE), F32),
            pltpu.VMEM((64 * MID, 4 * LANE), F32),
            pltpu.VMEM((64 * BACK, 4 * LANE), F32),
            pltpu.VMEM((TOKENS + 8, 4 * LANE), F32),
            pltpu.VMEM((TOKENS, 4 * LANE), F32),
            *HELD,
        ],
        compiler_params=pltpu.CompilerParams(vmem_limit_bytes=VMEM_LIMIT),
        cost_estimate=LONG,
        interpret=interpret,
        name="correlate",
    )(shares, resident(kept), resident(spec), taps, *(resident(x) for x in consts))


def pack_kernel(streams_hbm, filter_hbm, out_hbm, streams_ref, filter_ref, out_ref, sems):
    lane = lanes_of(ROWS)
    columns = range(COLS // 128)
    spans = [slice(column * 128, (column + 1) * 128) for column in columns]
    arrivals = [
        (
            started(streams_hbm.at[:, :, span], streams_ref.at[column], sems.at[column]),
            started(filter_hbm.at[:, span], filter_ref.at[column], sems.at[4 + column]),
        )
        for column, span in zip(columns, spans)
    ]
    departures = []
    for column in columns:
        for copy in arrivals[column]:
            copy.wait()
        blocks = [streams_ref[column, j].astype(F32) for j in range(3)] + [filter_ref[column]]
        for part in range(4):
            placed = [pltpu.roll(b, ((j - part) % 4) * LANE, 1) if j != part else b
                      for j, b in enumerate(blocks)]
            joined = placed[3]
            for j in range(2, -1, -1):
                joined = jnp.where(lane < (j + 1) * LANE, placed[j], joined)
            out_ref[column * 4 + part] = joined.astype(BF16)
        part = slice(column * 4, column * 4 + 4)
        departures.append(started(out_ref.at[part], out_hbm.at[part], sems.at[8 + column]))
    for copy in departures:
        copy.wait()


def unpack_kernel(got_ref, streams_ref, filter_ref):
    lane = lanes_of(ROWS)
    for column in range(COLS // 128):
        at = slice(column * 128, (column + 1) * 128)
        blocks = [got_ref[column * 4 + part].astype(F32) for part in range(4)]
        for j in range(4):
            placed = [pltpu.roll(b, ((part - j) % 4) * LANE, 1) if j != part else b
                      for part, b in enumerate(blocks)]
            joined = placed[3]
            for part in range(2, -1, -1):
                joined = jnp.where(lane < (part + 1) * LANE, placed[part], joined)
            if j < 3:
                streams_ref[j, :, at] = joined.astype(BF16)
            else:
                filter_ref[:, at] = joined


def contract(left, right, left_dim, right_dim):
    return lax.dot_general(
        left, right, (((left_dim,), (right_dim,)), ((), ())), preferred_element_type=F32
    )


def fetch_weights(place_ref, refs, weights, sems):
    copies = []
    for step in range(NEAR):
        low = pl.multiple_of((place_ref[0] ^ (-step % NEAR)) * 256, 256)
        copies.append(started(refs[step], weights.at[:, pl.ds(low, 256)], sems.at[step]))
    return copies


def fetch_cots(place_ref, refs, cots, sems):
    copies = []
    for far in range(FAR):
        low = pl.multiple_of((place_ref[2] ^ (far % 2)) * COLS, COLS)
        for side in range(2):
            row = pl.multiple_of((place_ref[1] ^ (far // 2 + 2 * side)) * ROWS, ROWS)
            copies.append(
                started(
                    refs[far].at[side],
                    cots.at[pl.ds(row, ROWS), pl.ds(low, COLS)],
                    sems.at[NEAR + 2 * far + side],
                )
            )
    return copies


def send_kernel(place_ref, gated_ref, *refs):
    sent_ref, weights, cots, sems = refs[NEAR + FAR :]
    copies = fetch_weights(place_ref, refs[:NEAR], weights, sems)
    copies += fetch_cots(place_ref, refs[NEAR : NEAR + FAR], cots, sems)
    for s in range(SEQ):
        sent_ref[s, :LANE, :] = gated_ref[s % NEAR]
    for copy in copies:
        copy.wait()
    total = contract(weights[...], cots[...], 1, 1).astype(BF16)
    for s in range(SEQ):
        sent_ref[s, LANE:, :] = total[s * LANE : (s + 1) * LANE]


def output_kernel(place_ref, got_ref, *refs):
    out_hbm, weights, out_ref, sems = refs[NEAR:]
    copies = fetch_weights(place_ref, refs[:NEAR], weights, sems)
    gated = got_ref[...].reshape(COLS, FAR * ROWS)
    for copy in copies:
        copy.wait()
    departures = []
    for a in range(FAR):
        part = contract(gated[:, a * ROWS : (a + 1) * ROWS], weights[...], 0, 0).astype(BF16)
        out_ref[2 * a] = part[:, :COLS]
        out_ref[2 * a + 1] = part[:, COLS:]
        span = slice(2 * a, 2 * a + 2)
        departures.append(started(out_ref.at[span], out_hbm.at[span], sems.at[NEAR + a]))
    for copy in departures:
        copy.wait()


def weight_kernel(place_ref, got_ref, *refs):
    grad_hbms = refs[FAR : FAR + NEAR]
    cots, own_ref, other_ref, sems = refs[FAR + NEAR :]
    copies = fetch_cots(place_ref, refs[:FAR], cots, sems)
    gated = got_ref[...].reshape(COLS, FAR * ROWS)
    for copy in copies:
        copy.wait()
    departures = []
    for step in reversed(range(NEAR)):
        low = pl.multiple_of((place_ref[0] ^ step) * 256, 256)
        grad = contract(gated, cots[:, pl.ds(low, 256)], 1, 0)
        if step:
            other_ref[step - 1] = grad.astype(BF16)
            source = other_ref.at[step - 1]
        else:
            own_ref[...] = grad
            source = own_ref
        departures.append(started(source, grad_hbms[step], sems.at[step]))
    for copy in departures:
        copy.wait()


def call(kernel, name, out_shape, interpret, *inputs, specs=None, scratch=(), far_out=False):
    many = isinstance(out_shape, tuple)
    outs = out_shape if many else (out_shape,)
    in_specs = [whole(x.shape) for x in inputs]
    for at, spec in (specs or {}).items():
        in_specs[at] = spec
    out_specs = tuple(FAR_OFF if far_out else whole(x.shape) for x in outs)
    return pl.pallas_call(
        kernel,
        out_shape=out_shape,
        grid=(1,),
        in_specs=in_specs,
        out_specs=out_specs if many else out_specs[0],
        scratch_shapes=list(scratch),
        compiler_params=pltpu.CompilerParams(vmem_limit_bytes=VMEM_LIMIT),
        cost_estimate=pl.CostEstimate(flops=1_000_000_000, transcendentals=0, bytes_accessed=2_000_000),
        interpret=interpret,
        name=name,
    )(*inputs)


SCALAR = pl.BlockSpec(memory_space=pltpu.SMEM)


def pack(streams, long_filter, interpret=False):
    return pl.pallas_call(
        pack_kernel,
        out_shape=pltpu.HBM((SEQ, ROWS, 4 * LANE), BF16),
        in_specs=[FAR_OFF, FAR_OFF],
        out_specs=FAR_OFF,
        scratch_shapes=[
            pltpu.VMEM((4, 3, ROWS, 128), BF16),
            pltpu.VMEM((4, ROWS, 128), F32),
            pltpu.VMEM((SEQ, ROWS, 4 * LANE), BF16),
            pltpu.SemaphoreType.DMA((12,)),
        ],
        compiler_params=pltpu.CompilerParams(vmem_limit_bytes=VMEM_LIMIT),
        interpret=interpret,
        name="pack",
    )(resident(streams), resident(long_filter))


def unpack(got, interpret=False):
    shapes = (
        jax.ShapeDtypeStruct((3, ROWS, COLS), BF16),
        jax.ShapeDtypeStruct((ROWS, COLS), F32),
    )
    return call(unpack_kernel, "unpack", shapes, interpret, got)


def far_off(low, high):
    return {at: FAR_OFF for at in range(low, high)}


GATHERED = (
    pltpu.VMEM((COLS, 2 * COLS), BF16),
    pltpu.VMEM((FAR * ROWS, 2 * COLS), BF16),
    pltpu.SemaphoreType.DMA((NEAR + 2 * FAR,)),
)


def to_send(place, gated, weights, cots, interpret=False):
    shape = jax.ShapeDtypeStruct((SEQ, 2 * LANE, FAR * ROWS), BF16)
    return call(
        send_kernel, "send", shape, interpret, place, gated, *weights, *cots,
        specs={0: SCALAR, **far_off(2, 2 + NEAR + FAR)}, scratch=GATHERED,
    )


GATED = pl.BlockSpec((SEQ, LANE, FAR * ROWS), lambda _: (0, 0, 0))


def output_shares(place, got, weights, interpret=False):
    return call(
        output_kernel, "outputs", pltpu.HBM((CHAN, ROWS, COLS), BF16), interpret,
        place, got, *weights, specs={0: SCALAR, 1: GATED, **far_off(2, 2 + NEAR)},
        scratch=(GATHERED[0], pltpu.VMEM((CHAN, ROWS, COLS), BF16), GATHERED[2]), far_out=True,
    )


def weight_shares(place, got, cots, width, interpret=False):
    shapes = tuple(pltpu.HBM((COLS, width), BF16 if step else F32) for step in range(NEAR))
    return call(
        weight_kernel, "weights", shapes, interpret, place, got, *cots,
        specs={0: SCALAR, 1: GATED, **far_off(2, 2 + FAR)}, far_out=True,
        scratch=(
            GATHERED[1],
            pltpu.VMEM((COLS, width), F32),
            pltpu.VMEM((NEAR - 1, COLS, width), BF16),
            GATHERED[2],
        ),
    )


def shards(projected, short_filter, long_filter, w_out, d_out):
    seq_at = lax.axis_index("seq")
    chan_at = lax.axis_index("chan")
    place = jnp.stack([seq_at % NEAR, chan_at // 2, chan_at % 2]).astype(jnp.int32)
    consts = [jnp.asarray(table) for table in tables()]

    moved = swapped(d_out)
    signals = exchange(pack(projected.transpose(1, 0, 2), long_filter), "seq")
    pair = jnp.stack([moved, lax.ppermute(moved, "chan", chan_pairs(4))])
    cots = [pair] + [lax.ppermute(pair, "chan", chan_pairs(far)) for far in range(1, FAR)]
    weights = [w_out] + [
        lax.ppermute(w_out, "seq", near_pairs(-step % NEAR)) for step in range(1, NEAR)
    ]

    own = lax.dynamic_slice_in_dim(short_filter, seq_at * LANE, LANE, axis=2).reshape(3, 3 * LANE)
    plain = jnp.zeros((3, LANE), F32).at[0].set(1.0)
    taps = jnp.concatenate([own, plain], axis=1)

    gated, kept, spec = convolve(signals.reshape(TOKENS, 4 * LANE), taps, consts)
    got = exchange(to_send(place, gated, weights, cots), "seq")

    shares = exchange(output_shares(place, got, weights), "chan")
    d_wout, *others = weight_shares(place, got, cots, w_out.shape[1])
    output = swapped(jnp.sum(shares.astype(F32), axis=0).astype(BF16))
    for step, piece in enumerate(others, 1):
        d_wout = d_wout + lax.ppermute(piece, "seq", near_pairs(step)).astype(F32)

    returned = exchange(correlate(got, kept, spec, taps, consts), "seq")
    d_projected, d_filter = unpack(returned)
    return (output, d_projected.transpose(1, 0, 2), d_wout, d_filter)


def solution(mesh):
    in_specs = (
        P("seq", None, "chan"),
        P(None, None, "chan"),
        P("seq", "chan"),
        P("chan", "seq"),
        P("seq", "chan"),
    )
    out_specs = (P("seq", "chan"), P("seq", None, "chan"), P("chan", "seq"), P("seq", "chan"))
    return jax.shard_map(shards, mesh=mesh, in_specs=in_specs, out_specs=out_specs, check_vma=False)
```
